32 devices in a mesh: side: 2 (over y), slab: 16 (over z, x, core).
Axes of the slice: x: 2, y: 2, z: 4, core: 2. Of those that a mesh axis runs over, the one named last changes fastest.
Arguments:
- velocity: float32 [2, 4096, 4096], P('side', 'slab'), may hold values from -6 to 6
- kernel: bfloat16 [2, 9, 4096, 4096], P('side', None, 'slab'), may hold values from -4 to 4
- history: bfloat16 [2, 8, 2, 4096, 4096], P('side', None, None, 'slab'), may hold values from -24576 to 24576
- impedance: float32 [2], replicated, may hold values from 0.5 to 1.5
- prestress: float32 [4096, 4096], P('slab'), may hold values from 1 to 3
- strength: float32 [4096, 4096], P('slab'), may hold values from 0.5 to 2
- fault_state: float32 [4096, 4096], P('slab'), may hold values from -1 to 1
Outputs:
- new_velocity: float32 [2, 4096, 4096], P('side', 'slab')
- slip_rate: float32 [4096, 4096], P('slab')
- new_state: float32 [4096, 4096], P('slab')
The draws below stay inside these ranges and needn't reach their ends.
All inputs are finite; a program needn't handle non-finite values.
Results may differ from the reference program's by a relative error of at most 0.00058.
Values sent between devices are 32-bit elements; how exact they have to be, the bound alone decides.
No kernel may reach another device: no remote copies, remote signals or barrier semaphores. Data moves between devices by JAX's collectives and lax.ppermute only.
A program may use at most 320 MiB of HBM per device.

```python
import math
import jax
import jax.numpy as jnp

NX = 4096
NZ = 4096
LAGS = 8
NEWTON = 4
STEPS = 2


def level_of(key, dims, split, least, high):
    loudness, own = 1.0, jax.random.fold_in(key, 6)
    for position, parts in split:
        heights = jnp.exp(jax.random.uniform(jax.random.fold_in(own, position), (parts,), jnp.float32, least / len(split), high / len(split)))
        loudness = loudness * jnp.repeat(heights, dims[position] // parts).reshape([-1 if axis == position else 1 for axis in range(len(dims))])
    return loudness


def normal_values(key, extent, width, bound, shards=(), held_as=jnp.bfloat16):
    entries = jax.random.normal(key, extent, jnp.float32) * width
    if len(shards) > 0:
        entries = level_of(key, extent, shards, -0.22, 0.18) * entries
    return jnp.clip(entries, min=-bound, max=bound).astype(held_as)


def setup_inputs(seed: int = 0) -> dict:
    splits = jax.random.split(jax.random.key(seed), 8)
    velocity = normal_values(splits[0], (2, NX, NZ), 1.0, 6.0, ((0, 2), (1, 16)), jnp.float32)
    kernel = normal_values(splits[1], (2, LAGS + 1, NZ, NX), 0.3, 4.0, ((0, 2), (2, 16)))
    history = normal_values(splits[2], (2, LAGS, 2, NZ, NX), NX, 24576.0, ((0, 2), (3, 16)))
    impedance = jnp.clip(jax.random.uniform(splits[3], (2,), jnp.float32, 0.5, 1.5), 0.5, 1.5)
    prestress = jnp.clip(1.0 + 2.0 * jax.random.uniform(splits[4], (NX, NZ), jnp.float32) ** level_of(splits[4], (NX, NZ), ((0, 16),), -0.2, 0.2), 1.0, 3.0)
    strength = jnp.clip(jnp.exp(math.log(2.0) - 1.3862944 * jax.random.uniform(splits[5], (NX, NZ), jnp.float32) ** level_of(splits[5], (NX, NZ), ((0, 16),), -0.2, 0.2)), 0.5, 2.0)
    fault_state = jnp.clip(jax.random.uniform(splits[6], (NX, NZ), jnp.float32, -1.0, 1.0) * level_of(splits[6], (NX, NZ), ((0, 16),), -0.4, 0.0), -1.0, 1.0)
    return dict(velocity=velocity, kernel=kernel, history=history, impedance=impedance, prestress=prestress, strength=strength, fault_state=fault_state)


def inverse_sinh(value):
    magnitude = jnp.abs(value)
    result = jnp.log1p(magnitude + magnitude * magnitude / (1.0 + jnp.sqrt(1.0 + magnitude * magnitude)))
    return jnp.where(value < 0.0, -result, result)

def forward_spectrum(field):
    spec = jnp.fft.fft2(field).T
    return jnp.stack([jnp.real(spec), jnp.imag(spec)]).astype(jnp.bfloat16)

def inverse_force(total):
    combined = total[0] + 1j * total[1]
    return jnp.real(jnp.fft.ifft2(combined.T))

def reference(velocity, kernel, history, impedance, prestress, strength, fault_state):
    eta_first = impedance[0]
    eta_second = impedance[1]
    eta_total = eta_first + eta_second
    weight_first = eta_second / eta_total
    weight_second = eta_first / eta_total
    eta_joint = eta_first * eta_second / eta_total
    speeds = [velocity[0], velocity[1]]
    lag_lists = [[history[0, lag] for lag in range(LAGS)], [history[1, lag] for lag in range(LAGS)]]
    state_now = fault_state
    rate = jnp.zeros_like(prestress)
    for step_index in range(STEPS):
        forces = []
        for side_index in range(2):
            spec = forward_spectrum(speeds[side_index])
            total = kernel[side_index, 0].astype(jnp.float32) * spec.astype(jnp.float32)
            for lag in range(LAGS):
                total = total + kernel[side_index, lag + 1].astype(jnp.float32) * lag_lists[side_index][lag].astype(jnp.float32)
            forces.append(inverse_force(total))
            lag_lists[side_index] = [spec] + lag_lists[side_index][:-1]
        coupled = weight_first * forces[0] + weight_second * forces[1]
        locked = prestress + coupled
        rate = locked / (eta_joint + strength)
        factor = 0.5 * jnp.exp(state_now)
        for iteration in range(NEWTON):
            scaled = factor * rate
            misfit = strength * inverse_sinh(scaled) + eta_joint * rate - locked
            slope = strength * factor / jnp.sqrt(1.0 + scaled * scaled) + eta_joint
            rate = rate - 0.5 * misfit / slope
        stress = locked - eta_joint * rate
        speeds = [(prestress + forces[0] - stress) / eta_first, -1.0 * (prestress + forces[1] - stress) / eta_second]
        state_now = state_now + 0.25 * (jnp.exp(-state_now) - jnp.abs(rate))
    return (jnp.stack(speeds), rate, state_now)
```

```python
import functools
import math

import jax
import jax.numpy as jnp
import numpy as np
from jax import lax
from jax.experimental import pallas as pl
from jax.experimental.pallas import tpu as pltpu
from jax.sharding import PartitionSpec as P

NX = 4096
NZ = 4096
NEWTON = 4
STEPS = 2


highest = lax.Precision.HIGHEST


def swapped(value, axis, distance):
    mask = 2**distance
    pairs = [(source, source ^ mask) for source in range(lax.axis_size(axis))]
    return lax.ppermute(value, axis, pairs)


def inverse_sinh(value):
    magnitude = jnp.abs(value)
    result = jnp.log1p(
        magnitude + magnitude * magnitude / (1.0 + jnp.sqrt(1.0 + magnitude * magnitude))
    )
    return jnp.where(value < 0.0, -result, result)


def angle_table(rows_count, cols_count, period, sign):
    first = lax.broadcasted_iota(jnp.int32, (rows_count, cols_count), 0)
    second = lax.broadcasted_iota(jnp.int32, (rows_count, cols_count), 1)
    phase = (first * second % period).astype(jnp.float32) * (2.0 * math.pi / period)
    return (jnp.cos(phase), sign * jnp.sin(phase))


def transform_last(real_part, imag_part, sign, real_only):
    length = real_part.shape[-1]
    inner = min(length, 256)
    outer = length // inner
    leading = real_part.shape[:-1]
    cos_outer, sin_outer = angle_table(outer, outer, outer, sign)
    cos_twist, sin_twist = angle_table(outer, inner, length, sign)
    cos_inner, sin_inner = angle_table(inner, inner, inner, sign)
    shaped_real = real_part.reshape(leading + (outer, inner))
    step_real = jnp.einsum("kn,...nq->...kq", cos_outer, shaped_real, precision=highest)
    step_imag = jnp.einsum("kn,...nq->...kq", sin_outer, shaped_real, precision=highest)
    if imag_part is not None:
        shaped_imag = imag_part.reshape(leading + (outer, inner))
        step_real = step_real - jnp.einsum(
            "kn,...nq->...kq", sin_outer, shaped_imag, precision=highest
        )
        step_imag = step_imag + jnp.einsum(
            "kn,...nq->...kq", cos_outer, shaped_imag, precision=highest
        )
    twist_real = step_real * cos_twist - step_imag * sin_twist
    twist_imag = step_real * sin_twist + step_imag * cos_twist
    out_real = jnp.matmul(twist_real, cos_inner, precision=highest) - jnp.matmul(
        twist_imag, sin_inner, precision=highest
    )
    result_real = jnp.swapaxes(out_real, -1, -2).reshape(leading + (length,))
    if real_only:
        return (result_real, None)
    out_imag = jnp.matmul(twist_real, sin_inner, precision=highest) + jnp.matmul(
        twist_imag, cos_inner, precision=highest
    )
    result_imag = jnp.swapaxes(out_imag, -1, -2).reshape(leading + (length,))
    return (result_real, result_imag)


def to_spectrum(rows_field):
    slab_count = lax.axis_size("slab")
    z_real, z_imag = transform_last(rows_field, None, -1.0, False)
    stacked = jnp.stack([z_real, z_imag])
    rows_dev = stacked.shape[1]
    length_z = stacked.shape[2]
    moved = jnp.transpose(stacked, (0, 2, 1)).reshape(
        2, slab_count, length_z // slab_count, rows_dev
    )
    block = lax.all_to_all(moved, "slab", split_axis=1, concat_axis=3, tiled=True)
    spec_real, spec_imag = transform_last(block[0, 0], block[1, 0], -1.0, False)
    return jnp.stack([spec_real, spec_imag]).astype(jnp.bfloat16)


def to_rows(spec_real, spec_imag):
    slab_count = lax.axis_size("slab")
    x_real, x_imag = transform_last(spec_real, spec_imag, 1.0, False)
    stacked = jnp.stack([x_real, x_imag], axis=1)
    batch = stacked.shape[0]
    kz_dev = stacked.shape[2]
    length_x = stacked.shape[3]
    moved = stacked.reshape(batch, 2, kz_dev, slab_count, length_x // slab_count)
    scale = 1.0 / (NX * NZ)
    turned = jnp.swapaxes(
        lax.all_to_all(moved, "slab", split_axis=3, concat_axis=2, tiled=True)[:, :, :, 0, :], 2, 3
    )
    field_real, unused = transform_last(turned[:, 0], turned[:, 1], 1.0, True)
    return field_real * scale


def local_general(velocity, kernel, history, impedance, prestress, strength, fault_state):
    side_index = lax.axis_index("side")
    is_first = side_index == 0
    eta_first = impedance[0]
    eta_second = impedance[1]
    eta_total = eta_first + eta_second
    weight_first = eta_second / eta_total
    weight_second = eta_first / eta_total
    eta_joint = eta_first * eta_second / eta_total
    own_eta = jnp.where(is_first, eta_first, eta_second)
    own_sign = jnp.where(is_first, 1.0, -1.0).astype(jnp.float32)
    lag_kernel = kernel[0]
    lag_history = history[0]
    kernel_now = lag_kernel[0].astype(jnp.float32)
    speed = velocity[0]
    state_now = fault_state
    rate = jnp.zeros_like(prestress)
    for step_index in range(STEPS):
        spec_now = to_spectrum(speed)
        total = kernel_now * spec_now.astype(jnp.float32) + jnp.einsum(
            "lzx,lczx->czx", lag_kernel[1:], lag_history, preferred_element_type=jnp.float32
        )
        force_now = to_rows(total[0][None], total[1][None])[0]
        force_other = swapped(force_now, "side", 0)
        force_first = jnp.where(is_first, force_now, force_other)
        force_second = jnp.where(is_first, force_other, force_now)
        coupled = weight_first * force_first + weight_second * force_second
        locked = prestress + coupled
        friction_rate = locked / (eta_joint + strength)
        factor = 0.5 * jnp.exp(state_now)
        for iteration in range(NEWTON):
            scaled = factor * friction_rate
            misfit = strength * inverse_sinh(scaled) + eta_joint * friction_rate - locked
            slope = strength * factor / jnp.sqrt(1.0 + scaled * scaled) + eta_joint
            friction_rate = friction_rate - 0.5 * misfit / slope
        stress = locked - eta_joint * friction_rate
        speed_new = own_sign * (prestress + force_now - stress) / own_eta
        state_new = state_now + 0.25 * (jnp.exp(-state_now) - jnp.abs(friction_rate))
        speed = speed_new
        rate = friction_rate
        state_now = state_new
        lag_history = jnp.concatenate([spec_now[None], lag_history[:-1]], axis=0)
    return (speed[None], rate, state_now)


RADIX = 16
CHUNKS = 2
f32 = jnp.float32
bf16 = jnp.bfloat16


def constant_tables():
    inner = NX // RADIX
    grid = np.outer(np.arange(inner), np.arange(inner)) % inner
    phase = grid * (2.0 * np.pi / inner)
    cos, sin = np.cos(phase), np.sin(phase)
    full = np.concatenate(
        [np.concatenate([cos, sin], 1), np.concatenate([-sin, cos], 1)], 0
    ).astype(np.float32)
    high = full.astype(jnp.bfloat16)
    low = (full - high.astype(np.float32)).astype(jnp.bfloat16)
    table = np.concatenate([high, high, low], 1)
    turn = np.outer(np.arange(RADIX), np.arange(inner)) * (2.0 * np.pi / NX)
    twist = np.stack([np.cos(turn), np.sin(turn)]).astype(np.float32)
    return table, twist


def plus(a, b):
    return tuple(
        (p if q is None else q if p is None else p + q) for p, q in zip(a, b)
    )


def minus(a, b):
    return tuple(
        (p if q is None else -q if p is None else p - q) for p, q in zip(a, b)
    )


def times_i(a, sign):
    real, imag = a
    if sign > 0:
        return (None if imag is None else -imag, real)
    return (imag, None if real is None else -real)


def turned_by(a, cos, sin):
    real, imag = a
    if imag is None:
        return (real * cos, real * sin)
    if real is None:
        return (-(imag * sin), imag * cos)
    return (real * cos - imag * sin, real * sin + imag * cos)


def four(x, sign):
    a, b = plus(x[0], x[2]), minus(x[0], x[2])
    c, d = plus(x[1], x[3]), times_i(minus(x[1], x[3]), sign)
    return [plus(a, c), plus(b, d), minus(a, c), minus(b, d)]


def sixteen(x, sign):
    rows = [four([x[4 * m + n] for m in range(4)], sign) for n in range(4)]
    out = [None] * 16
    for k in range(4):
        terms = []
        for n in range(4):
            power = n * k
            term = rows[n][k]
            if power == 4:
                term = times_i(term, sign)
            elif power:
                angle = 2.0 * math.pi * power / 16
                term = turned_by(term, math.cos(angle), sign * math.sin(angle))
            terms.append(term)
        for m, value in enumerate(four(terms, sign)):
            out[k + 4 * m] = value
    return out


def store_split(held, k, group, lane, first, second):
    inner = NX // RADIX
    rows = pl.ds(pl.multiple_of(group * 16 + (k % 2) * 128, 16), 16)
    for place, value in ((0, first), (1, second)):
        high = value.astype(bf16)
        low = (value - high.astype(f32)).astype(bf16)
        held[k // 2, rows, pl.ds(place * inner + lane, 128)] = high
        held[k // 2, rows, pl.ds((2 + place) * inner + lane, 128)] = low


def twisted(value, twist, k, lane, sign):
    if k == 0:
        real, imag = value
        return (real, jnp.zeros_like(real) if imag is None else imag)
    cos = twist[0, k : k + 1, pl.ds(lane, 128)]
    sin = twist[1, k : k + 1, pl.ds(lane, 128)]
    return turned_by(value, cos, sin if sign > 0 else -sin)


def product(table, held, k, start):
    wide = table.shape[1] // 3
    rows = pl.ds(start, table.shape[0] - start)
    dims = (((1,), (1,)), ((), ()))
    return lax.dot_general(
        table[rows, : 2 * wide], held[k], dims, preferred_element_type=f32
    ) + lax.dot_general(
        table[rows, 2 * wide :], held[k, :, :wide], dims, preferred_element_type=f32
    )


def picked(refs, half):
    return (refs[0], half) if len(refs) == 1 else (refs[half], 0)


def forward_rows(rows_ref, table, twist, outs, held):
    rows, length = rows_ref.shape
    inner = length // RADIX

    def group(g, carry):
        at = pl.ds(pl.multiple_of(g * 16, 16), 16)
        for lane in range(0, inner, 128):
            values = [(rows_ref[at, pl.ds(n * inner + lane, 128)], None) for n in range(RADIX)]
            for k, value in enumerate(sixteen(values, -1)):
                store_split(held, k, g, lane, *twisted(value, twist, k, lane, -1))
        return carry

    lax.fori_loop(0, rows // 16, group, 0)

    def wave(pair, carry):
        both = product(table, held, pair, 0)
        slabs, halves = outs[0].shape[0], 2
        per = inner // slabs // halves
        for slab in range(slabs):
            for half in range(halves):
                out, place = picked(outs, half)
                for part in range(2):
                    first = part * inner + (slab * halves + half) * per
                    for odd in range(2):
                        out[slab, place, part, pl.ds(2 * pair + odd, per, RADIX), :] = both[
                            first : first + per, odd * 128 : odd * 128 + 128
                        ]
        return carry

    lax.fori_loop(0, RADIX // 2, wave, 0)


def start_kernel(velocity, table, twist, *refs):
    forward_rows(velocity.at[0], table, twist, refs[:-1], refs[-1])


def friction(scalars, own, other, prestress, strength, state):
    weight_own, weight_other, joint, eta, sign = [scalars[n] for n in range(5)]
    locked = prestress + (weight_own * own + weight_other * other)
    rate = locked / (joint + strength)
    factor = 0.5 * jnp.exp(state)
    for iteration in range(NEWTON):
        scaled = factor * rate
        misfit = strength * inverse_sinh(scaled) + joint * rate - locked
        slope = strength * factor / jnp.sqrt(1.0 + scaled * scaled) + joint
        rate = rate - 0.5 * misfit / slope
    stress = locked - joint * rate
    speed = sign * (prestress + own - stress) / eta
    state_new = state + 0.25 * (jnp.exp(-state) - jnp.abs(rate))
    return speed, rate, state_new


def middle_kernel(scalars, own, other, prestress, strength, state, table, twist, *refs):
    outs = refs[:-3]
    state_out, held, speed_held = refs[-3:]

    def group(g, carry):
        at = pl.ds(pl.multiple_of(g * 8, 8), 8)
        for lane in range(0, own.shape[1], 1024):
            cols = pl.ds(lane, 1024)
            speed, rate, state_new = friction(
                scalars,
                own[at, cols],
                other[at, cols],
                prestress[at, cols],
                strength[at, cols],
                state[at, cols],
            )
            speed_held[at, cols] = speed
            state_out[at, cols] = state_new
        return carry

    lax.fori_loop(0, own.shape[0] // 8, group, 0)
    forward_rows(speed_held, table, twist, outs, held)


def end_kernel(scalars, own, other, prestress, strength, state, *refs):
    speed_out, rate_out, state_out = refs[-3:]

    def group(g, carry):
        at = pl.ds(pl.multiple_of(g * 8, 8), 8)
        for lane in range(0, own.shape[1], 1024):
            cols = pl.ds(lane, 1024)
            speed, rate, state_new = friction(
                scalars,
                own[at, cols],
                other[at, cols],
                prestress[at, cols],
                strength[at, cols],
                state[at, cols],
            )
            speed_out[0, at, cols] = speed
            rate_out[at, cols] = rate
            state_out[at, cols] = state_new
        return carry

    lax.fori_loop(0, own.shape[0] // 8, group, 0)


def history_kernel(kernel, history, now, later):
    def group(g, carry):
        cols = pl.ds(pl.multiple_of(g * 256, 256), 256)
        lags = [kernel[0, n, :, cols].astype(f32) for n in range(kernel.shape[1])]
        for part in range(2):
            total_now = total_later = 0.0
            for n in range(history.shape[1]):
                past = history[0, n, part, :, cols].astype(f32)
                total_now = total_now + lags[n + 1] * past
                if n + 2 < len(lags):
                    total_later = total_later + lags[n + 2] * past
            now[part, :, cols] = total_now
            later[part, :, cols] = total_later
        return carry

    lax.fori_loop(0, now.shape[2] // 256, group, 0)


def spectral_kernel(has_past, half, *refs):
    blocks = refs[:CHUNKS]
    kernel_now, past_sum, table, twist = refs[CHUNKS : CHUNKS + 4]
    rest = list(refs[CHUNKS + 4 :])
    if has_past:
        kernel_past, spec_past = rest.pop(0), rest.pop(0)
        spec_out = None
    if half > 0:
        rest.pop(0)
    outs, rest = rest[:CHUNKS], rest[CHUNKS:]
    if not has_past:
        spec_out = rest.pop(0)
    held, turned, total = rest
    rows = blocks[0].shape[3]
    inner = RADIX * 16
    length = total.shape[2]

    def group(g, carry):
        at = pl.ds(pl.multiple_of(g * 16, 16), 16)
        for chunk in range(CHUNKS):
            values = [
                (blocks[chunk][n, 0, 0, at, :], blocks[chunk][n, 0, 1, at, :])
                for n in range(RADIX)
            ]
            lane = chunk * 128
            for k, value in enumerate(sixteen(values, -1)):
                store_split(held, k, g, lane, *twisted(value, twist, k, lane, -1))
        return carry

    lax.fori_loop(0, rows // 16, group, 0)

    def wave(pair, carry):
        both = product(table, held, pair, 0)
        for odd in range(2):
            for part in range(2):
                turned[part, pl.ds(2 * pair + odd, inner, RADIX), :] = both[
                    part * inner : part * inner + inner, odd * 128 : odd * 128 + 128
                ]
        return carry

    lax.fori_loop(0, RADIX // 2, wave, 0)

    def convolve(b, carry):
        cols = pl.ds(pl.multiple_of(b * 256, 256), 256)
        weight = kernel_now[0, 0, :, cols].astype(f32)
        for part in range(2):
            spec = turned[part, cols, :].T.astype(bf16)
            value = weight * spec.astype(f32) + past_sum[part, :, cols]
            if has_past:
                value = value + kernel_past[0, 0, :, cols].astype(f32) * spec_past[
                    part, :, cols
                ].astype(f32)
            else:
                spec_out[part, :, cols] = spec
            total[part, :, cols] = value
        return carry

    lax.fori_loop(0, length // 256, convolve, 0)

    def group_back(g, carry):
        at = pl.ds(pl.multiple_of(g * 16, 16), 16)
        for lane in range(0, inner, 128):
            values = [
                (total[0, at, pl.ds(n * inner + lane, 128)], total[1, at, pl.ds(n * inner + lane, 128)])
                for n in range(RADIX)
            ]
            for k, value in enumerate(sixteen(values, 1)):
                real, imag = twisted(value, twist, k, lane, 1)
                store_split(held, k, g, lane, imag, real)
        return carry

    lax.fori_loop(0, rows // 16, group_back, 0)

    def wave_back(pair, carry):
        both = product(table, held, pair, 0)
        slabs = outs[0].shape[0]
        per = inner // slabs // CHUNKS
        for slab in range(slabs):
            for chunk in range(CHUNKS):
                for part in range(2):
                    first = (1 - part) * inner + (slab * CHUNKS + chunk) * per
                    for odd in range(2):
                        outs[chunk][slab, 0, part, pl.ds(2 * pair + odd, per, RADIX), :] = both[
                            first : first + per, odd * 128 : odd * 128 + 128
                        ]
        return carry

    lax.fori_loop(0, RADIX // 2, wave_back, 0)


def inverse_kernel(count, *refs):
    blocks = refs[:count]
    table, twist, out, held, turned = refs[count:]
    rows, length = out.shape
    inner = length // RADIX

    def group(g, carry):
        at = pl.ds(pl.multiple_of(g * 16, 16), 16)
        for half in range(inner // 128):
            block, place = picked(blocks, half)
            values = [(block[n, place, 0, at, :], block[n, place, 1, at, :]) for n in range(RADIX)]
            for k, value in enumerate(sixteen(values, 1)):
                real, imag = twisted(value, twist, k, half * 128, 1)
                store_split(held, k, g, half * 128, imag, real)
        return carry

    lax.fori_loop(0, rows // 16, group, 0)

    def wave(pair, carry):
        both = product(table, held, pair, inner)
        for odd in range(2):
            turned[pl.ds(2 * pair + odd, inner, RADIX), :] = both[:, odd * 128 : odd * 128 + 128]
        return carry

    lax.fori_loop(0, RADIX // 2, wave, 0)
    scale = 1.0 / (NX * NZ)

    def turn(b, carry):
        cols = pl.ds(pl.multiple_of(b * 256, 256), 256)
        out[:, cols] = turned[cols, :].T * scale
        return carry

    lax.fori_loop(0, length // 256, turn, 0)


def whole_spec(array):
    zeros = (0,) * array.ndim
    return pl.BlockSpec(array.shape, lambda *_: zeros)


PARAMS = pltpu.CompilerParams(vmem_limit_bytes=62 * 1024 * 1024)
SCALARS = pl.BlockSpec(memory_space=pltpu.SMEM)


def exchanged(value):
    return lax.all_to_all(value, "slab", split_axis=0, concat_axis=0, tiled=True)


def local(velocity, kernel, history, impedance, prestress, strength, fault_state):
    slabs = lax.axis_size("slab")
    rows_dev, length = prestress.shape
    inner = length // RADIX
    chunk_rows = rows_dev // CHUNKS
    halves = rows_dev // 128
    if slabs != RADIX or rows_dev != inner or chunk_rows != 128:
        return local_general(
            velocity, kernel, history, impedance, prestress, strength, fault_state
        )
    lags = history.shape[1]
    table_np, twist_np = constant_tables()
    table, twist = jnp.asarray(table_np), jnp.asarray(twist_np)
    is_first = lax.axis_index("side") == 0
    eta_first, eta_second = impedance[0], impedance[1]
    eta_total = eta_first + eta_second
    weight_first, weight_second = eta_second / eta_total, eta_first / eta_total
    scalars = jnp.stack(
        [
            jnp.where(is_first, weight_first, weight_second),
            jnp.where(is_first, weight_second, weight_first),
            eta_first * eta_second / eta_total,
            jnp.where(is_first, eta_first, eta_second),
            jnp.where(is_first, 1.0, -1.0).astype(f32),
        ]
    )
    def tiles(counts):
        return [jax.ShapeDtypeStruct((slabs, count, 2, 128, 128), f32) for count in counts]

    def tile_specs(counts):
        return [pl.BlockSpec((slabs, count, 2, 128, 128), lambda *_: (0,) * 5) for count in counts]

    forward_cut = [[2], [1, 1]]
    held = pltpu.VMEM((RADIX // 2, 256, 4 * inner), bf16)
    rows_shape = jax.ShapeDtypeStruct((chunk_rows, length), f32)
    rows_spec = pl.BlockSpec((chunk_rows, length), lambda *_: (0, 0))

    def chunk_spec(chunk):
        return pl.BlockSpec((chunk_rows, length), lambda *_: (chunk, 0))

    def start(chunk):
        return pl.pallas_call(
            start_kernel,
            out_shape=tiles(forward_cut[chunk]),
            grid=(1,),
            in_specs=[
                pl.BlockSpec((1, chunk_rows, length), lambda *_: (0, chunk, 0)),
                whole_spec(table),
                whole_spec(twist),
            ],
            out_specs=tile_specs(forward_cut[chunk]),
            scratch_shapes=[held],
            compiler_params=PARAMS,
        )(velocity, table, twist)

    def middle(chunk, own, other, state):
        *sent, state_new = pl.pallas_call(
            middle_kernel,
            out_shape=tiles(forward_cut[chunk]) + [rows_shape],
            grid=(1,),
            in_specs=[
                SCALARS,
                rows_spec,
                rows_spec,
                chunk_spec(chunk),
                chunk_spec(chunk),
                chunk_spec(chunk),
                whole_spec(table),
                whole_spec(twist),
            ],
            out_specs=tile_specs(forward_cut[chunk]) + [rows_spec],
            scratch_shapes=[held, pltpu.VMEM((chunk_rows, length), f32)],
            compiler_params=PARAMS,
        )(scalars, own, other, prestress, strength, state, table, twist)
        return sent, state_new

    def end(chunk, own, other, state, before):
        full = jax.ShapeDtypeStruct((rows_dev, length), f32)
        step = 32
        parts = chunk_rows // step
        base = chunk * parts
        moving = pl.BlockSpec((step, length), lambda g: (base + g, 0))
        near = pl.BlockSpec((step, length), lambda g: (g, 0))
        moving_speed = pl.BlockSpec((1, step, length), lambda g: (0, base + g, 0))
        kept = [pl.BlockSpec(memory_space=pl.ANY)] * len(before)
        return pl.pallas_call(
            end_kernel,
            out_shape=(jax.ShapeDtypeStruct((1, rows_dev, length), f32), full, full),
            grid=(parts,),
            in_specs=[SCALARS, near, near, moving, moving, near] + kept,
            out_specs=(moving_speed, moving, moving),
            input_output_aliases={6 + n: n for n in range(len(before))},
            compiler_params=PARAMS,
        )(scalars, own, other, prestress, strength, state, *before)

    def past_sums():
        step = 32
        total = jax.ShapeDtypeStruct((2, rows_dev, length), f32)
        spec = pl.BlockSpec((2, step, length), lambda g: (0, g, 0))
        return pl.pallas_call(
            history_kernel,
            out_shape=(total, total),
            grid=(rows_dev // step,),
            in_specs=[
                pl.BlockSpec((1, lags + 1, step, length), lambda g: (0, 0, g, 0)),
                pl.BlockSpec((1, lags, 2, step, length), lambda g: (0, 0, 0, g, 0)),
            ],
            out_specs=(spec, spec),
            compiler_params=PARAMS,
        )(kernel, history)

    def spectral(half, blocks, past_sum, past, before):
        def block(array):
            place = half if array.shape[1] == halves else 0
            return pl.BlockSpec((slabs, 1, 2, 128, 128), lambda *_: (0, place, 0, 0, 0))

        lag_spec = [
            pl.BlockSpec((1, 1, 128, length), functools.partial(lambda lag, *_: (0, lag, half, 0), lag))
            for lag in range(2)
        ]
        sum_spec = pl.BlockSpec((2, 128, length), lambda *_: (0, half, 0))
        spec_spec = pl.BlockSpec((2, 128, length), lambda *_: (0, 0, 0))
        operands = list(blocks) + [kernel, past_sum, table, twist]
        in_specs = [block(b) for b in blocks]
        in_specs += [lag_spec[0], sum_spec, whole_spec(table), whole_spec(twist)]
        out_shape = tiles([1, halves])
        out_specs = [block(shape) for shape in out_shape]
        if past is not None:
            operands += [kernel, past]
            in_specs += [lag_spec[1], spec_spec]
        else:
            out_shape.append(jax.ShapeDtypeStruct((2, 128, length), bf16))
            out_specs.append(spec_spec)
        aliases = {}
        if before is not None:
            aliases = {len(operands): 1}
            operands.append(before)
            in_specs.append(pl.BlockSpec(memory_space=pl.ANY))
        return pl.pallas_call(
            functools.partial(spectral_kernel, past is not None, half),
            input_output_aliases=aliases,
            out_shape=out_shape,
            grid=(1,),
            in_specs=in_specs,
            out_specs=out_specs,
            scratch_shapes=[
                held,
                pltpu.VMEM((2, length, 128), f32),
                pltpu.VMEM((2, 128, length), f32),
            ],
            compiler_params=PARAMS,
        )(*operands)

    def inverse(*blocks):
        return pl.pallas_call(
            functools.partial(inverse_kernel, len(blocks)),
            out_shape=rows_shape,
            grid=(1,),
            in_specs=tile_specs([b.shape[1] for b in blocks]) + [whole_spec(table), whole_spec(twist)],
            out_specs=rows_spec,
            scratch_shapes=[held, pltpu.VMEM((length, 128), f32)],
            compiler_params=PARAMS,
        )(*blocks, table, twist)
    hold = lax.optimization_barrier
    sent = [start(0), None]
    states = [fault_state] * CHUNKS
    past = [None] * halves
    sums, results, waiting = None, (), None
    for step_index in range(STEPS):
        last = step_index == STEPS - 1
        first = exchanged(sent[0][0])
        if step_index == 0:
            sent[1] = start(1)
        else:
            own = inverse(waiting)
            sent[1], states[1] = middle(1, own, swapped(own, "side", 0), states[1])
        first, sent[1], states[1] = hold((first, sent[1], states[1]))
        near = exchanged(sent[1][0])
        if step_index == 0:
            sums = past_sums()
        near, far, sums = hold((near, sent[1][1], sums))
        far = exchanged(far)
        outs = spectral(0, (first, near), sums[step_index], past[0], None)
        if step_index == 0:
            past[0] = outs[2]
        back, late = outs[0], outs[1]
        far, back, late = hold((far, back, late))
        back = exchanged(back)
        outs = spectral(1, (first, far), sums[step_index], past[1], late)
        if step_index == 0:
            past[1] = outs[2]
        back, more, late = hold((back, outs[0], outs[1]))
        more = exchanged(more)
        more, late = hold((more, late))
        waiting = exchanged(late)
        own = inverse(back, more)
        other = swapped(own, "side", 0)
        if last:
            results = end(0, own, other, states[0], results)
            waiting, results = hold((waiting, tuple(results)))
            own = inverse(waiting)
            results = end(1, own, swapped(own, "side", 0), states[1], results)
        else:
            sent[0], states[0] = middle(0, own, other, states[0])
            waiting, sent[0], states[0] = hold((waiting, sent[0], states[0]))
    return tuple(results)


def solution(mesh):
    placed = (
        P("side", "slab", None),
        P("side", None, "slab", None),
        P("side", None, None, "slab", None),
        P(),
        P("slab", None),
        P("slab", None),
        P("slab", None),
    )
    return jax.shard_map(
        local,
        mesh=mesh,
        in_specs=placed,
        out_specs=(P("side", "slab", None), P("slab", None), P("slab", None)),
        check_vma=False,
    )
```

```python
import functools
import math

import jax
import jax.numpy as jnp
import numpy as np
from jax import lax
from jax.experimental import pallas as pl
from jax.experimental.pallas import tpu as pltpu
from jax.sharding import PartitionSpec as P

NX = 4096
NZ = 4096
NEWTON = 4
STEPS = 2


highest = lax.Precision.HIGHEST


def swapped(value, axis, distance):
    mask = 2**distance
    pairs = [(source, source ^ mask) for source in range(lax.axis_size(axis))]
    return lax.ppermute(value, axis, pairs)


def inverse_sinh(value):
    magnitude = jnp.abs(value)
    result = jnp.log1p(
        magnitude + magnitude * magnitude / (1.0 + jnp.sqrt(1.0 + magnitude * magnitude))
    )
    return jnp.where(value < 0.0, -result, result)


def angle_table(rows_count, cols_count, period, sign):
    first = lax.broadcasted_iota(jnp.int32, (rows_count, cols_count), 0)
    second = lax.broadcasted_iota(jnp.int32, (rows_count, cols_count), 1)
    phase = (first * second % period).astype(jnp.float32) * (2.0 * math.pi / period)
    return (jnp.cos(phase), sign * jnp.sin(phase))


def transform_last(real_part, imag_part, sign, real_only):
    length = real_part.shape[-1]
    inner = min(length, 256)
    outer = length // inner
    leading = real_part.shape[:-1]
    cos_outer, sin_outer = angle_table(outer, outer, outer, sign)
    cos_twist, sin_twist = angle_table(outer, inner, length, sign)
    cos_inner, sin_inner = angle_table(inner, inner, inner, sign)
    shaped_real = real_part.reshape(leading + (outer, inner))
    step_real = jnp.einsum("kn,...nq->...kq", cos_outer, shaped_real, precision=highest)
    step_imag = jnp.einsum("kn,...nq->...kq", sin_outer, shaped_real, precision=highest)
    if imag_part is not None:
        shaped_imag = imag_part.reshape(leading + (outer, inner))
        step_real = step_real - jnp.einsum(
            "kn,...nq->...kq", sin_outer, shaped_imag, precision=highest
        )
        step_imag = step_imag + jnp.einsum(
            "kn,...nq->...kq", cos_outer, shaped_imag, precision=highest
        )
    twist_real = step_real * cos_twist - step_imag * sin_twist
    twist_imag = step_real * sin_twist + step_imag * cos_twist
    out_real = jnp.matmul(twist_real, cos_inner, precision=highest) - jnp.matmul(
        twist_imag, sin_inner, precision=highest
    )
    result_real = jnp.swapaxes(out_real, -1, -2).reshape(leading + (length,))
    if real_only:
        return (result_real, None)
    out_imag = jnp.matmul(twist_real, sin_inner, precision=highest) + jnp.matmul(
        twist_imag, cos_inner, precision=highest
    )
    result_imag = jnp.swapaxes(out_imag, -1, -2).reshape(leading + (length,))
    return (result_real, result_imag)


def to_spectrum(rows_field):
    slab_count = lax.axis_size("slab")
    z_real, z_imag = transform_last(rows_field, None, -1.0, False)
    stacked = jnp.stack([z_real, z_imag])
    rows_dev = stacked.shape[1]
    length_z = stacked.shape[2]
    moved = jnp.transpose(stacked, (0, 2, 1)).reshape(
        2, slab_count, length_z // slab_count, rows_dev
    )
    block = lax.all_to_all(moved, "slab", split_axis=1, concat_axis=3, tiled=True)
    spec_real, spec_imag = transform_last(block[0, 0], block[1, 0], -1.0, False)
    return jnp.stack([spec_real, spec_imag]).astype(jnp.bfloat16)


def to_rows(spec_real, spec_imag):
    slab_count = lax.axis_size("slab")
    x_real, x_imag = transform_last(spec_real, spec_imag, 1.0, False)
    stacked = jnp.stack([x_real, x_imag], axis=1)
    batch = stacked.shape[0]
    kz_dev = stacked.shape[2]
    length_x = stacked.shape[3]
    moved = stacked.reshape(batch, 2, kz_dev, slab_count, length_x // slab_count)
    scale = 1.0 / (NX * NZ)
    turned = jnp.swapaxes(
        lax.all_to_all(moved, "slab", split_axis=3, concat_axis=2, tiled=True)[:, :, :, 0, :], 2, 3
    )
    field_real, unused = transform_last(turned[:, 0], turned[:, 1], 1.0, True)
    return field_real * scale


def local_general(velocity, kernel, history, impedance, prestress, strength, fault_state):
    side_index = lax.axis_index("side")
    is_first = side_index == 0
    eta_first = impedance[0]
    eta_second = impedance[1]
    eta_total = eta_first + eta_second
    weight_first = eta_second / eta_total
    weight_second = eta_first / eta_total
    eta_joint = eta_first * eta_second / eta_total
    own_eta = jnp.where(is_first, eta_first, eta_second)
    own_sign = jnp.where(is_first, 1.0, -1.0).astype(jnp.float32)
    lag_kernel = kernel[0]
    lag_history = history[0]
    kernel_now = lag_kernel[0].astype(jnp.float32)
    speed = velocity[0]
    state_now = fault_state
    rate = jnp.zeros_like(prestress)
    for step_index in range(STEPS):
        spec_now = to_spectrum(speed)
        total = kernel_now * spec_now.astype(jnp.float32) + jnp.einsum(
            "lzx,lczx->czx", lag_kernel[1:], lag_history, preferred_element_type=jnp.float32
        )
        force_now = to_rows(total[0][None], total[1][None])[0]
        force_other = swapped(force_now, "side", 0)
        force_first = jnp.where(is_first, force_now, force_other)
        force_second = jnp.where(is_first, force_other, force_now)
        coupled = weight_first * force_first + weight_second * force_second
        locked = prestress + coupled
        friction_rate = locked / (eta_joint + strength)
        factor = 0.5 * jnp.exp(state_now)
        for iteration in range(NEWTON):
            scaled = factor * friction_rate
            misfit = strength * inverse_sinh(scaled) + eta_joint * friction_rate - locked
            slope = strength * factor / jnp.sqrt(1.0 + scaled * scaled) + eta_joint
            friction_rate = friction_rate - 0.5 * misfit / slope
        stress = locked - eta_joint * friction_rate
        speed_new = own_sign * (prestress + force_now - stress) / own_eta
        state_new = state_now + 0.25 * (jnp.exp(-state_now) - jnp.abs(friction_rate))
        speed = speed_new
        rate = friction_rate
        state_now = state_new
        lag_history = jnp.concatenate([spec_now[None], lag_history[:-1]], axis=0)
    return (speed[None], rate, state_now)


RADIX = 16
CHUNKS = 2
LAST_CUT = 80
f32 = jnp.float32
bf16 = jnp.bfloat16


def constant_tables():
    inner = NX // RADIX
    grid = np.outer(np.arange(inner), np.arange(inner)) % inner
    phase = grid * (2.0 * np.pi / inner)
    cos, sin = np.cos(phase), np.sin(phase)
    full = np.concatenate(
        [np.concatenate([cos, sin], 1), np.concatenate([-sin, cos], 1)], 0
    ).astype(np.float32)
    high = full.astype(jnp.bfloat16)
    low = (full - high.astype(np.float32)).astype(jnp.bfloat16)
    table = np.concatenate([high, high, low], 1)
    turn = np.outer(np.arange(RADIX), np.arange(inner)) * (2.0 * np.pi / NX)
    twist = np.stack([np.cos(turn), np.sin(turn)]).astype(np.float32)
    return table, twist


def plus(a, b):
    return tuple(
        (p if q is None else q if p is None else p + q) for p, q in zip(a, b)
    )


def minus(a, b):
    return tuple(
        (p if q is None else -q if p is None else p - q) for p, q in zip(a, b)
    )


def times_i(a, sign):
    real, imag = a
    if sign > 0:
        return (None if imag is None else -imag, real)
    return (imag, None if real is None else -real)


def turned_by(a, cos, sin):
    real, imag = a
    if imag is None:
        return (real * cos, real * sin)
    if real is None:
        return (-(imag * sin), imag * cos)
    return (real * cos - imag * sin, real * sin + imag * cos)


def four(x, sign):
    a, b = plus(x[0], x[2]), minus(x[0], x[2])
    c, d = plus(x[1], x[3]), times_i(minus(x[1], x[3]), sign)
    return [plus(a, c), plus(b, d), minus(a, c), minus(b, d)]


def sixteen(x, sign):
    rows = [four([x[4 * m + n] for m in range(4)], sign) for n in range(4)]
    out = [None] * 16
    for k in range(4):
        terms = []
        for n in range(4):
            power = n * k
            term = rows[n][k]
            if power == 4:
                term = times_i(term, sign)
            elif power:
                angle = 2.0 * math.pi * power / 16
                term = turned_by(term, math.cos(angle), sign * math.sin(angle))
            terms.append(term)
        for m, value in enumerate(four(terms, sign)):
            out[k + 4 * m] = value
    return out


def store_split(held, k, group, lane, first, second):
    inner = NX // RADIX
    rows = pl.ds(pl.multiple_of(group * 16 + (k % 2) * 128, 16), 16)
    for place, value in ((0, first), (1, second)):
        high = value.astype(bf16)
        low = (value - high.astype(f32)).astype(bf16)
        held[k // 2, rows, pl.ds(place * inner + lane, 128)] = high
        held[k // 2, rows, pl.ds((2 + place) * inner + lane, 128)] = low


def twisted(value, twist, k, lane, sign):
    if k == 0:
        real, imag = value
        return (real, jnp.zeros_like(real) if imag is None else imag)
    cos = twist[0, k : k + 1, pl.ds(lane, 128)]
    sin = twist[1, k : k + 1, pl.ds(lane, 128)]
    return turned_by(value, cos, sin if sign > 0 else -sin)


def product(table, held, k, start):
    wide = table.shape[1] // 3
    rows = pl.ds(start, table.shape[0] - start)
    dims = (((1,), (1,)), ((), ()))
    return lax.dot_general(
        table[rows, : 2 * wide], held[k], dims, preferred_element_type=f32
    ) + lax.dot_general(
        table[rows, 2 * wide :], held[k, :, :wide], dims, preferred_element_type=f32
    )


def picked(refs, half):
    return (refs[0], half) if len(refs) == 1 else (refs[half], 0)


def forward_rows(rows_ref, table, twist, outs, held):
    rows, length = rows_ref.shape
    inner = length // RADIX

    def group(g, carry):
        at = pl.ds(pl.multiple_of(g * 16, 16), 16)
        for lane in range(0, inner, 128):
            values = [(rows_ref[at, pl.ds(n * inner + lane, 128)], None) for n in range(RADIX)]
            for k, value in enumerate(sixteen(values, -1)):
                store_split(held, k, g, lane, *twisted(value, twist, k, lane, -1))
        return carry

    lax.fori_loop(0, rows // 16, group, 0)

    def wave(pair, carry):
        both = product(table, held, pair, 0)
        slabs, halves = outs[0].shape[0], 2
        per = inner // slabs // halves
        for slab in range(slabs):
            for half in range(halves):
                out, place = picked(outs, half)
                for part in range(2):
                    first = part * inner + (slab * halves + half) * per
                    for odd in range(2):
                        out[slab, place, part, pl.ds(2 * pair + odd, per, RADIX), :] = both[
                            first : first + per, odd * 128 : odd * 128 + 128
                        ]
        return carry

    lax.fori_loop(0, RADIX // 2, wave, 0)


def start_kernel(velocity, table, twist, *refs):
    forward_rows(velocity.at[0], table, twist, refs[:-1], refs[-1])


def friction(scalars, own, other, prestress, strength, state):
    weight_own, weight_other, joint, eta, sign = [scalars[n] for n in range(5)]
    locked = prestress + (weight_own * own + weight_other * other)
    rate = locked / (joint + strength)
    factor = 0.5 * jnp.exp(state)
    for iteration in range(NEWTON):
        scaled = factor * rate
        wide = 1.0 + scaled * scaled
        narrow = lax.rsqrt(wide)
        bent = jnp.log(jnp.abs(scaled) + wide * narrow)
        bent = jnp.where(scaled < 0.0, -bent, bent)
        misfit = strength * bent + joint * rate - locked
        slope = strength * factor * narrow + joint
        rate = rate - 0.5 * misfit / slope
    stress = locked - joint * rate
    speed = (sign / eta) * (prestress + own - stress)
    state_new = state + 0.25 * (jnp.exp(-state) - jnp.abs(rate))
    return speed, rate, state_new


def middle_kernel(scalars, own, other, prestress, strength, state, table, twist, *refs):
    outs = refs[:-3]
    state_out, held, speed_held = refs[-3:]

    def group(g, carry):
        at = pl.ds(pl.multiple_of(g * 8, 8), 8)
        for lane in range(0, own.shape[1], 1024):
            cols = pl.ds(lane, 1024)
            speed, rate, state_new = friction(
                scalars,
                own[at, cols],
                other[at, cols],
                prestress[at, cols],
                strength[at, cols],
                state[at, cols],
            )
            speed_held[at, cols] = speed
            state_out[at, cols] = state_new
        return carry

    lax.fori_loop(0, own.shape[0] // 8, group, 0)
    forward_rows(speed_held, table, twist, outs, held)


def end_kernel(scalars, own, other, prestress, strength, state, *refs):
    speed_out, rate_out, state_out = refs[-3:]

    def group(g, carry):
        at = pl.ds(pl.multiple_of(g * 8, 8), 8)
        for lane in range(0, own.shape[1], 1024):
            cols = pl.ds(lane, 1024)
            speed, rate, state_new = friction(
                scalars,
                own[at, cols],
                other[at, cols],
                prestress[at, cols],
                strength[at, cols],
                state[at, cols],
            )
            speed_out[0, at, cols] = speed
            rate_out[at, cols] = rate
            state_out[at, cols] = state_new
        return carry

    lax.fori_loop(0, own.shape[0] // 8, group, 0)


def history_kernel(kernel, history, now, later):
    def group(g, carry):
        cols = pl.ds(pl.multiple_of(g * 256, 256), 256)
        lags = [kernel[0, n, :, cols].astype(f32) for n in range(kernel.shape[1])]
        for part in range(2):
            total_now = total_later = 0.0
            for n in range(history.shape[1]):
                past = history[0, n, part, :, cols].astype(f32)
                total_now = total_now + lags[n + 1] * past
                if n + 2 < len(lags):
                    total_later = total_later + lags[n + 2] * past
            now[part, :, cols] = total_now
            later[part, :, cols] = total_later
        return carry

    lax.fori_loop(0, now.shape[2] // 256, group, 0)


def spectral_kernel(has_past, half, pieces, *refs):
    blocks = refs[:CHUNKS]
    kernel_now, past_sum, table, twist = refs[CHUNKS : CHUNKS + 4]
    rest = list(refs[CHUNKS + 4 :])
    if has_past:
        kernel_past, spec_past = rest.pop(0), rest.pop(0)
        spec_out = None
    if half > 0:
        rest = rest[len(pieces) - 1 :]
    outs, rest = rest[: len(pieces)], rest[len(pieces) :]
    if not has_past:
        spec_out = rest.pop(0)
    held, turned, total = rest
    rows = blocks[0].shape[3]
    inner = RADIX * 16
    length = total.shape[2]

    def group(g, carry):
        at = pl.ds(pl.multiple_of(g * 16, 16), 16)
        for chunk in range(CHUNKS):
            values = [
                (blocks[chunk][n, 0, 0, at, :], blocks[chunk][n, 0, 1, at, :])
                for n in range(RADIX)
            ]
            lane = chunk * 128
            for k, value in enumerate(sixteen(values, -1)):
                store_split(held, k, g, lane, *twisted(value, twist, k, lane, -1))
        return carry

    lax.fori_loop(0, rows // 16, group, 0)

    def wave(pair, carry):
        both = product(table, held, pair, 0)
        for odd in range(2):
            for part in range(2):
                turned[part, pl.ds(2 * pair + odd, inner, RADIX), :] = both[
                    part * inner : part * inner + inner, odd * 128 : odd * 128 + 128
                ]
        return carry

    lax.fori_loop(0, RADIX // 2, wave, 0)

    def convolve(b, carry):
        cols = pl.ds(pl.multiple_of(b * 256, 256), 256)
        weight = kernel_now[0, 0, :, cols].astype(f32)
        for part in range(2):
            spec = turned[part, cols, :].T.astype(bf16)
            value = weight * spec.astype(f32) + past_sum[part, :, cols]
            if has_past:
                value = value + kernel_past[0, 0, :, cols].astype(f32) * spec_past[
                    part, :, cols
                ].astype(f32)
            else:
                spec_out[part, :, cols] = spec
            total[part, :, cols] = value
        return carry

    lax.fori_loop(0, length // 256, convolve, 0)

    def group_back(g, carry):
        at = pl.ds(pl.multiple_of(g * 16, 16), 16)
        for lane in range(0, inner, 128):
            values = [
                (total[0, at, pl.ds(n * inner + lane, 128)], total[1, at, pl.ds(n * inner + lane, 128)])
                for n in range(RADIX)
            ]
            for k, value in enumerate(sixteen(values, 1)):
                real, imag = twisted(value, twist, k, lane, 1)
                store_split(held, k, g, lane, imag, real)
        return carry

    lax.fori_loop(0, rows // 16, group_back, 0)

    def wave_back(pair, carry):
        both = product(table, held, pair, 0)
        slabs = outs[0].shape[0]
        per = inner // slabs
        for slab in range(slabs):
            for out, (row, count) in zip(outs, pieces):
                count = count // RADIX
                for part in range(2):
                    first = (1 - part) * inner + slab * per + row // RADIX
                    for odd in range(2):
                        out[slab, 0, part, pl.ds(2 * pair + odd, count, RADIX), :] = both[
                            first : first + count, odd * 128 : odd * 128 + 128
                        ]
        return carry

    lax.fori_loop(0, RADIX // 2, wave_back, 0)


def inverse_kernel(count, *refs):
    blocks = refs[:count]
    table, twist, out, held, turned = refs[count:]
    rows, length = out.shape
    inner = length // RADIX

    def group(g, carry):
        at = pl.ds(pl.multiple_of(g * 16, 16), 16)
        for half in range(inner // 128):
            block, place = picked(blocks, half)
            values = [(block[n, place, 0, at, :], block[n, place, 1, at, :]) for n in range(RADIX)]
            for k, value in enumerate(sixteen(values, 1)):
                real, imag = twisted(value, twist, k, half * 128, 1)
                store_split(held, k, g, half * 128, imag, real)
        return carry

    lax.fori_loop(0, rows // 16, group, 0)

    def wave(pair, carry):
        both = product(table, held, pair, inner)
        for odd in range(2):
            turned[pl.ds(2 * pair + odd, inner, RADIX), :] = both[:, odd * 128 : odd * 128 + 128]
        return carry

    lax.fori_loop(0, RADIX // 2, wave, 0)
    scale = 1.0 / (NX * NZ)

    def turn(b, carry):
        cols = pl.ds(pl.multiple_of(b * 256, 256), 256)
        out[:, cols] = turned[cols, :].T[:rows] * scale
        return carry

    lax.fori_loop(0, length // 256, turn, 0)


def whole_spec(array):
    zeros = (0,) * array.ndim
    return pl.BlockSpec(array.shape, lambda *_: zeros)


PARAMS = pltpu.CompilerParams(vmem_limit_bytes=62 * 1024 * 1024)
SCALARS = pl.BlockSpec(memory_space=pltpu.SMEM)


def exchanged(value):
    return lax.all_to_all(value, "slab", split_axis=0, concat_axis=0, tiled=True)


def local(velocity, kernel, history, impedance, prestress, strength, fault_state):
    slabs = lax.axis_size("slab")
    rows_dev, length = prestress.shape
    inner = length // RADIX
    chunk_rows = rows_dev // CHUNKS
    halves = rows_dev // 128
    if slabs != RADIX or rows_dev != inner or chunk_rows != 128:
        return local_general(
            velocity, kernel, history, impedance, prestress, strength, fault_state
        )
    lags = history.shape[1]
    table_np, twist_np = constant_tables()
    table, twist = jnp.asarray(table_np), jnp.asarray(twist_np)
    is_first = lax.axis_index("side") == 0
    eta_first, eta_second = impedance[0], impedance[1]
    eta_total = eta_first + eta_second
    weight_first, weight_second = eta_second / eta_total, eta_first / eta_total
    scalars = jnp.stack(
        [
            jnp.where(is_first, weight_first, weight_second),
            jnp.where(is_first, weight_second, weight_first),
            eta_first * eta_second / eta_total,
            jnp.where(is_first, eta_first, eta_second),
            jnp.where(is_first, 1.0, -1.0).astype(f32),
        ]
    )
    def tiles(counts, rows=128):
        return [jax.ShapeDtypeStruct((slabs, count, 2, rows, 128), f32) for count in counts]

    def tile_specs(counts):
        return [pl.BlockSpec((slabs, count, 2, 128, 128), lambda *_: (0,) * 5) for count in counts]

    forward_cut = [[2], [1, 1]]
    held = pltpu.VMEM((RADIX // 2, 256, 4 * inner), bf16)
    rows_shape = jax.ShapeDtypeStruct((chunk_rows, length), f32)
    rows_spec = pl.BlockSpec((chunk_rows, length), lambda *_: (0, 0))

    def chunk_spec(chunk):
        return pl.BlockSpec((chunk_rows, length), lambda *_: (chunk, 0))

    def start(chunk):
        return pl.pallas_call(
            start_kernel,
            out_shape=tiles(forward_cut[chunk]),
            grid=(1,),
            in_specs=[
                pl.BlockSpec((1, chunk_rows, length), lambda *_: (0, chunk, 0)),
                whole_spec(table),
                whole_spec(twist),
            ],
            out_specs=tile_specs(forward_cut[chunk]),
            scratch_shapes=[held],
            compiler_params=PARAMS,
        )(velocity, table, twist)

    def middle(chunk, own, other, state):
        *sent, state_new = pl.pallas_call(
            middle_kernel,
            out_shape=tiles(forward_cut[chunk]) + [rows_shape],
            grid=(1,),
            in_specs=[
                SCALARS,
                rows_spec,
                rows_spec,
                chunk_spec(chunk),
                chunk_spec(chunk),
                chunk_spec(chunk),
                whole_spec(table),
                whole_spec(twist),
            ],
            out_specs=tile_specs(forward_cut[chunk]) + [rows_spec],
            scratch_shapes=[held, pltpu.VMEM((chunk_rows, length), f32)],
            compiler_params=PARAMS,
        )(scalars, own, other, prestress, strength, state, table, twist)
        return sent, state_new

    def end(row, own, other, state, before):
        full = jax.ShapeDtypeStruct((rows_dev, length), f32)
        step = 16
        parts = own.shape[0] // step
        base = row // step
        ahead = row % chunk_rows // step
        moving = pl.BlockSpec((step, length), lambda g: (base + g, 0))
        near = pl.BlockSpec((step, length), lambda g: (g, 0))
        held_state = pl.BlockSpec((step, length), lambda g: (ahead + g, 0))
        moving_speed = pl.BlockSpec((1, step, length), lambda g: (0, base + g, 0))
        kept = [pl.BlockSpec(memory_space=pl.ANY)] * len(before)
        return pl.pallas_call(
            end_kernel,
            out_shape=(jax.ShapeDtypeStruct((1, rows_dev, length), f32), full, full),
            grid=(parts,),
            in_specs=[SCALARS, near, near, moving, moving, held_state] + kept,
            out_specs=(moving_speed, moving, moving),
            input_output_aliases={6 + n: n for n in range(len(before))},
            compiler_params=PARAMS,
        )(scalars, own, other, prestress, strength, state, *before)

    def past_sums():
        step = 32
        total = jax.ShapeDtypeStruct((2, rows_dev, length), f32)
        spec = pl.BlockSpec((2, step, length), lambda g: (0, g, 0))
        return pl.pallas_call(
            history_kernel,
            out_shape=(total, total),
            grid=(rows_dev // step,),
            in_specs=[
                pl.BlockSpec((1, lags + 1, step, length), lambda g: (0, 0, g, 0)),
                pl.BlockSpec((1, lags, 2, step, length), lambda g: (0, 0, 0, g, 0)),
            ],
            out_specs=(spec, spec),
            compiler_params=PARAMS,
        )(kernel, history)

    def spectral(half, blocks, past_sum, past, pieces, before):
        def block(array):
            place = half if array.shape[1] == halves else 0
            shape = (slabs, 1, 2, array.shape[3], 128)
            return pl.BlockSpec(shape, lambda *_: (0, place, 0, 0, 0))

        lag_spec = [
            pl.BlockSpec((1, 1, 128, length), functools.partial(lambda lag, *_: (0, lag, half, 0), lag))
            for lag in range(2)
        ]
        sum_spec = pl.BlockSpec((2, 128, length), lambda *_: (0, half, 0))
        spec_spec = pl.BlockSpec((2, 128, length), lambda *_: (0, 0, 0))
        operands = list(blocks) + [kernel, past_sum, table, twist]
        in_specs = [block(b) for b in blocks]
        in_specs += [lag_spec[0], sum_spec, whole_spec(table), whole_spec(twist)]
        out_shape = tiles([1])
        for row, count in pieces[1:]:
            out_shape += tiles([halves], count)
        out_specs = [block(shape) for shape in out_shape]
        if past is not None:
            operands += [kernel, past]
            in_specs += [lag_spec[1], spec_spec]
        else:
            out_shape.append(jax.ShapeDtypeStruct((2, 128, length), bf16))
            out_specs.append(spec_spec)
        aliases = {}
        if before is not None:
            aliases = {len(operands) + n: 1 + n for n in range(len(before))}
            operands += before
            in_specs += [pl.BlockSpec(memory_space=pl.ANY)] * len(before)
        return pl.pallas_call(
            functools.partial(spectral_kernel, past is not None, half, pieces),
            input_output_aliases=aliases,
            out_shape=out_shape,
            grid=(1,),
            in_specs=in_specs,
            out_specs=out_specs,
            scratch_shapes=[
                held,
                pltpu.VMEM((2, length, 128), f32),
                pltpu.VMEM((2, 128, length), f32),
            ],
            compiler_params=PARAMS,
        )(*operands)

    def inverse(*blocks):
        rows = blocks[0].shape[3]
        return pl.pallas_call(
            functools.partial(inverse_kernel, len(blocks)),
            out_shape=jax.ShapeDtypeStruct((rows, length), f32),
            grid=(1,),
            in_specs=[whole_spec(b) for b in blocks] + [whole_spec(table), whole_spec(twist)],
            out_specs=pl.BlockSpec((rows, length), lambda *_: (0, 0)),
            scratch_shapes=[held, pltpu.VMEM((length, 128), f32)],
            compiler_params=PARAMS,
        )(*blocks, table, twist)
    hold = lax.optimization_barrier
    sent = [start(0), None]
    states = [fault_state] * CHUNKS
    past = [None] * halves
    sums, waiting = None, None
    whole, cut = chunk_rows, LAST_CUT
    for step_index in range(STEPS):
        last = step_index == STEPS - 1
        pieces = [(0, whole), (whole, cut), (whole + cut, whole - cut)]
        if not last:
            pieces = [(0, whole), (whole, whole)]
        first = exchanged(sent[0][0])
        if step_index == 0:
            sent[1] = start(1)
        else:
            own = inverse(waiting)
            sent[1], states[1] = middle(1, own, swapped(own, "side", 0), states[1])
        first, sent[1], states[1] = hold((first, sent[1], states[1]))
        near = exchanged(sent[1][0])
        if step_index == 0:
            sums = past_sums()
        near, far, sums = hold((near, sent[1][1], sums))
        far = exchanged(far)
        outs = spectral(0, (first, near), sums[step_index], past[0], pieces, None)
        if step_index == 0:
            past[0] = outs[-1]
        back, late = outs[0], outs[1 : len(pieces)]
        far, back, late = hold((far, back, late))
        back = exchanged(back)
        outs = spectral(1, (first, far), sums[step_index], past[1], pieces, late)
        if step_index == 0:
            past[1] = outs[-1]
        back, more, late = hold((back, outs[0], outs[1 : len(pieces)]))
        more = exchanged(more)
        more, late = hold((more, late))
        waiting = exchanged(late[0])
        own = inverse(back, more)
        other = swapped(own, "side", 0)
        if not last:
            sent[0], states[0] = middle(0, own, other, states[0])
            waiting, sent[0], states[0] = hold((waiting, sent[0], states[0]))
            continue
        waiting, own, other, final = hold((waiting, own, other, late[1]))
        final = exchanged(final)
        own_near = inverse(waiting)
        other_near = swapped(own_near, "side", 0)
        results = end(0, own, other, states[0], ())
        final, own_near, results = hold((final, own_near, tuple(results)))
        own = inverse(final)
        other = swapped(own, "side", 0)
        results = end(whole, own_near, other_near, states[1], results)
        results = end(whole + cut, own, other, states[1], results)
    return tuple(results)


def solution(mesh):
    placed = (
        P("side", "slab", None),
        P("side", None, "slab", None),
        P("side", None, None, "slab", None),
        P(),
        P("slab", None),
        P("slab", None),
        P("slab", None),
    )
    return jax.shard_map(
        local,
        mesh=mesh,
        in_specs=placed,
        out_specs=(P("side", "slab", None), P("slab", None), P("slab", None)),
        check_vma=False,
    )
```

```python
import functools
import math

import jax
import jax.numpy as jnp
import numpy as np
from jax import lax
from jax.experimental import pallas as pl
from jax.experimental.pallas import tpu as pltpu
from jax.sharding import PartitionSpec as P


NX = 4096
NZ = 4096
NEWTON = 4
STEPS = 2


highest = lax.Precision.HIGHEST


def swapped(value, axis, distance):
    mask = 2**distance
    pairs = [(source, source ^ mask) for source in range(lax.axis_size(axis))]
    return lax.ppermute(value, axis, pairs)


def inverse_sinh(value):
    magnitude = jnp.abs(value)
    result = jnp.log1p(
        magnitude + magnitude * magnitude / (1.0 + jnp.sqrt(1.0 + magnitude * magnitude))
    )
    return jnp.where(value < 0.0, -result, result)


def angle_table(rows_count, cols_count, period, sign):
    first = lax.broadcasted_iota(jnp.int32, (rows_count, cols_count), 0)
    second = lax.broadcasted_iota(jnp.int32, (rows_count, cols_count), 1)
    phase = (first * second % period).astype(jnp.float32) * (2.0 * math.pi / period)
    return (jnp.cos(phase), sign * jnp.sin(phase))


def transform_last(real_part, imag_part, sign, real_only):
    length = real_part.shape[-1]
    inner = min(length, 256)
    outer = length // inner
    leading = real_part.shape[:-1]
    cos_outer, sin_outer = angle_table(outer, outer, outer, sign)
    cos_twist, sin_twist = angle_table(outer, inner, length, sign)
    cos_inner, sin_inner = angle_table(inner, inner, inner, sign)
    shaped_real = real_part.reshape(leading + (outer, inner))
    step_real = jnp.einsum("kn,...nq->...kq", cos_outer, shaped_real, precision=highest)
    step_imag = jnp.einsum("kn,...nq->...kq", sin_outer, shaped_real, precision=highest)
    if imag_part is not None:
        shaped_imag = imag_part.reshape(leading + (outer, inner))
        step_real = step_real - jnp.einsum(
            "kn,...nq->...kq", sin_outer, shaped_imag, precision=highest
        )
        step_imag = step_imag + jnp.einsum(
            "kn,...nq->...kq", cos_outer, shaped_imag, precision=highest
        )
    twist_real = step_real * cos_twist - step_imag * sin_twist
    twist_imag = step_real * sin_twist + step_imag * cos_twist
    out_real = jnp.matmul(twist_real, cos_inner, precision=highest) - jnp.matmul(
        twist_imag, sin_inner, precision=highest
    )
    result_real = jnp.swapaxes(out_real, -1, -2).reshape(leading + (length,))
    if real_only:
        return (result_real, None)
    out_imag = jnp.matmul(twist_real, sin_inner, precision=highest) + jnp.matmul(
        twist_imag, cos_inner, precision=highest
    )
    result_imag = jnp.swapaxes(out_imag, -1, -2).reshape(leading + (length,))
    return (result_real, result_imag)


def to_spectrum(rows_field):
    slab_count = lax.axis_size("slab")
    z_real, z_imag = transform_last(rows_field, None, -1.0, False)
    stacked = jnp.stack([z_real, z_imag])
    rows_dev = stacked.shape[1]
    length_z = stacked.shape[2]
    moved = jnp.transpose(stacked, (0, 2, 1)).reshape(
        2, slab_count, length_z // slab_count, rows_dev
    )
    block = lax.all_to_all(moved, "slab", split_axis=1, concat_axis=3, tiled=True)
    spec_real, spec_imag = transform_last(block[0, 0], block[1, 0], -1.0, False)
    return jnp.stack([spec_real, spec_imag]).astype(jnp.bfloat16)


def to_rows(spec_real, spec_imag):
    slab_count = lax.axis_size("slab")
    x_real, x_imag = transform_last(spec_real, spec_imag, 1.0, False)
    stacked = jnp.stack([x_real, x_imag], axis=1)
    batch = stacked.shape[0]
    kz_dev = stacked.shape[2]
    length_x = stacked.shape[3]
    moved = stacked.reshape(batch, 2, kz_dev, slab_count, length_x // slab_count)
    scale = 1.0 / (NX * NZ)
    turned = jnp.swapaxes(
        lax.all_to_all(moved, "slab", split_axis=3, concat_axis=2, tiled=True)[:, :, :, 0, :], 2, 3
    )
    field_real, _ = transform_last(turned[:, 0], turned[:, 1], 1.0, True)
    return field_real * scale


def local_general(velocity, kernel, history, impedance, prestress, strength, fault_state):
    side_index = lax.axis_index("side")
    is_first = side_index == 0
    eta_first = impedance[0]
    eta_second = impedance[1]
    eta_total = eta_first + eta_second
    weight_first = eta_second / eta_total
    weight_second = eta_first / eta_total
    eta_joint = eta_first * eta_second / eta_total
    own_eta = jnp.where(is_first, eta_first, eta_second)
    own_sign = jnp.where(is_first, 1.0, -1.0).astype(jnp.float32)
    lag_kernel = kernel[0]
    lag_history = history[0]
    kernel_now = lag_kernel[0].astype(jnp.float32)
    speed = velocity[0]
    state_now = fault_state
    rate = jnp.zeros_like(prestress)
    for _ in range(STEPS):
        spec_now = to_spectrum(speed)
        total = kernel_now * spec_now.astype(jnp.float32) + jnp.einsum(
            "lzx,lczx->czx", lag_kernel[1:], lag_history, preferred_element_type=jnp.float32
        )
        force_now = to_rows(total[0][None], total[1][None])[0]
        force_other = swapped(force_now, "side", 0)
        force_first = jnp.where(is_first, force_now, force_other)
        force_second = jnp.where(is_first, force_other, force_now)
        coupled = weight_first * force_first + weight_second * force_second
        locked = prestress + coupled
        friction_rate = locked / (eta_joint + strength)
        factor = 0.5 * jnp.exp(state_now)
        for _ in range(NEWTON):
            scaled = factor * friction_rate
            misfit = strength * inverse_sinh(scaled) + eta_joint * friction_rate - locked
            slope = strength * factor / jnp.sqrt(1.0 + scaled * scaled) + eta_joint
            friction_rate = friction_rate - 0.5 * misfit / slope
        stress = locked - eta_joint * friction_rate
        speed_new = own_sign * (prestress + force_now - stress) / own_eta
        state_new = state_now + 0.25 * (jnp.exp(-state_now) - jnp.abs(friction_rate))
        speed = speed_new
        rate = friction_rate
        state_now = state_new
        lag_history = jnp.concatenate([spec_now[None], lag_history[:-1]], axis=0)
    return (speed[None], rate, state_now)


RADIX = 16
CHUNKS = 2
LAST_CUT = 80
f32 = jnp.float32
bf16 = jnp.bfloat16


def constant_tables():
    inner = NX // RADIX
    grid = np.outer(np.arange(inner), np.arange(inner)) % inner
    phase = grid * (2.0 * np.pi / inner)
    cos, sin = np.cos(phase), np.sin(phase)
    full = np.concatenate(
        [np.concatenate([cos, sin], 1), np.concatenate([-sin, cos], 1)], 0
    ).astype(np.float32)
    high = full.astype(jnp.bfloat16)
    low = (full - high.astype(np.float32)).astype(jnp.bfloat16)
    table = np.concatenate([high, high, low], 1)
    turn = np.outer(np.arange(RADIX), np.arange(inner)) * (2.0 * np.pi / NX)
    twist = np.stack([np.cos(turn), np.sin(turn)]).astype(np.float32)
    return table, twist


def plus(a, b):
    return tuple(
        (p if q is None else q if p is None else p + q) for p, q in zip(a, b)
    )


def minus(a, b):
    return tuple(
        (p if q is None else -q if p is None else p - q) for p, q in zip(a, b)
    )


def times_i(a, sign):
    real, imag = a
    if sign > 0:
        return (None if imag is None else -imag, real)
    return (imag, None if real is None else -real)


def turned_by(a, cos, sin):
    real, imag = a
    if imag is None:
        return (real * cos, real * sin)
    if real is None:
        return (-(imag * sin), imag * cos)
    return (real * cos - imag * sin, real * sin + imag * cos)


def four(x, sign):
    a, b = plus(x[0], x[2]), minus(x[0], x[2])
    c, d = plus(x[1], x[3]), times_i(minus(x[1], x[3]), sign)
    return [plus(a, c), plus(b, d), minus(a, c), minus(b, d)]


def sixteen(x, sign):
    rows = [four([x[4 * m + n] for m in range(4)], sign) for n in range(4)]
    out = [None] * 16
    for k in range(4):
        terms = []
        for n in range(4):
            power = n * k
            term = rows[n][k]
            if power == 4:
                term = times_i(term, sign)
            elif power:
                angle = 2.0 * math.pi * power / 16
                term = turned_by(term, math.cos(angle), sign * math.sin(angle))
            terms.append(term)
        for m, value in enumerate(four(terms, sign)):
            out[k + 4 * m] = value
    return out


def store_split(held, k, group, lane, first, second):
    inner = NX // RADIX
    rows = pl.ds(pl.multiple_of(group * 16 + (k % 2) * 128, 16), 16)
    for place, value in ((0, first), (1, second)):
        high = value.astype(bf16)
        low = (value - high.astype(f32)).astype(bf16)
        held[k // 2, rows, pl.ds(place * inner + lane, 128)] = high
        held[k // 2, rows, pl.ds((2 + place) * inner + lane, 128)] = low


def twisted(value, twist, k, lane, sign):
    if k == 0:
        real, imag = value
        return (real, jnp.zeros_like(real) if imag is None else imag)
    cos = twist[0, k : k + 1, pl.ds(lane, 128)]
    sin = twist[1, k : k + 1, pl.ds(lane, 128)]
    return turned_by(value, cos, sin if sign > 0 else -sin)


def product(table, held, k, start):
    wide = table.shape[1] // 3
    rows = pl.ds(start, table.shape[0] - start)
    dims = (((1,), (1,)), ((), ()))
    return lax.dot_general(
        table[rows, : 2 * wide], held[k], dims, preferred_element_type=f32
    ) + lax.dot_general(
        table[rows, 2 * wide :], held[k, :, :wide], dims, preferred_element_type=f32
    )


def picked(refs, half):
    return (refs[0], half) if len(refs) == 1 else (refs[half], 0)


def store_ring(place, spread, both, outs, pair, lead, first_part, row):
    inner = both.shape[0] // 2
    per = inner // RADIX
    spread[...] = both
    for n in range(RADIX):
        target = lax.rem(place[0] + n, RADIX)
        for part in range(2):
            base = (part if first_part == 0 else 1 - part) * inner
            rows = pl.ds(pl.multiple_of(base + target * per + row, 8), 8)
            for odd in range(2):
                outs[n][lead, part, pl.ds(2 * pair + odd, 8, RADIX), :] = spread[
                    rows, odd * 128 : odd * 128 + 128
                ]


def forward_rows(rows_ref, table, twist, place, outs, held, spread):
    rows, length = rows_ref.shape
    inner = length // RADIX

    def group(g, carry):
        at = pl.ds(pl.multiple_of(g * 16, 16), 16)
        for lane in range(0, inner, 128):
            values = [(rows_ref[at, pl.ds(n * inner + lane, 128)], None) for n in range(RADIX)]
            for k, value in enumerate(sixteen(values, -1)):
                store_split(held, k, g, lane, *twisted(value, twist, k, lane, -1))
        return carry

    lax.fori_loop(0, rows // 16, group, 0)

    def wave(pair, carry):
        both = product(table, held, pair, 0)
        if len(outs) == RADIX:
            for half in range(2):
                store_ring(place, spread, both, outs, pair, half, 0, half * 8)
            return carry
        slabs, halves = outs[0].shape[0], 2
        per = inner // slabs // halves
        for slab in range(slabs):
            for half in range(halves):
                out, spot = picked(outs, half)
                for part in range(2):
                    first = part * inner + (slab * halves + half) * per
                    for odd in range(2):
                        out[slab, spot, part, pl.ds(2 * pair + odd, per, RADIX), :] = both[
                            first : first + per, odd * 128 : odd * 128 + 128
                        ]
        return carry

    lax.fori_loop(0, RADIX // 2, wave, 0)


def start_kernel(place, velocity, table, twist, *refs):
    forward_rows(velocity.at[0], table, twist, place, refs[:-2], *refs[-2:])


def friction(scalars, own, other, prestress, strength, state):
    weight_own, weight_other, joint, eta, sign = [scalars[n] for n in range(5)]
    locked = prestress + (weight_own * own + weight_other * other)
    rate = locked / (joint + strength)
    factor = 0.5 * jnp.exp(state)
    for _ in range(NEWTON):
        scaled = factor * rate
        wide = 1.0 + scaled * scaled
        narrow = lax.rsqrt(wide)
        bent = jnp.log(jnp.abs(scaled) + wide * narrow)
        bent = jnp.where(scaled < 0.0, -bent, bent)
        misfit = strength * bent + joint * rate - locked
        slope = strength * factor * narrow + joint
        rate = rate - 0.5 * misfit / slope
    stress = locked - joint * rate
    speed = (sign / eta) * (prestress + own - stress)
    state_new = state + 0.25 * (jnp.exp(-state) - jnp.abs(rate))
    return speed, rate, state_new


def middle_kernel(place, scalars, own, other, prestress, strength, state, table, twist, *refs):
    outs = refs[:-4]
    state_out, held, spread, speed_held = refs[-4:]

    def group(g, carry):
        at = pl.ds(pl.multiple_of(g * 8, 8), 8)
        for lane in range(0, own.shape[1], 1024):
            cols = pl.ds(lane, 1024)
            speed, _, state_new = friction(
                scalars,
                own[at, cols],
                other[at, cols],
                prestress[at, cols],
                strength[at, cols],
                state[at, cols],
            )
            speed_held[at, cols] = speed
            state_out[at, cols] = state_new
        return carry

    lax.fori_loop(0, own.shape[0] // 8, group, 0)
    forward_rows(speed_held, table, twist, place, outs, held, spread)


def end_kernel(scalars, own, other, prestress, strength, state, *refs):
    speed_out, rate_out, state_out = refs[-3:]

    def group(g, carry):
        at = pl.ds(pl.multiple_of(g * 8, 8), 8)
        for lane in range(0, own.shape[1], 1024):
            cols = pl.ds(lane, 1024)
            speed, rate, state_new = friction(
                scalars,
                own[at, cols],
                other[at, cols],
                prestress[at, cols],
                strength[at, cols],
                state[at, cols],
            )
            speed_out[0, at, cols] = speed
            rate_out[at, cols] = rate
            state_out[at, cols] = state_new
        return carry

    lax.fori_loop(0, own.shape[0] // 8, group, 0)


def history_kernel(kernel, history, now, later):
    def group(g, carry):
        cols = pl.ds(pl.multiple_of(g * 256, 256), 256)
        lags = [kernel[0, n, :, cols].astype(f32) for n in range(kernel.shape[1])]
        for part in range(2):
            total_now = total_later = 0.0
            for n in range(history.shape[1]):
                past = history[0, n, part, :, cols].astype(f32)
                total_now = total_now + lags[n + 1] * past
                if n + 2 < len(lags):
                    total_later = total_later + lags[n + 2] * past
            now[part, :, cols] = total_now
            later[part, :, cols] = total_later
        return carry

    lax.fori_loop(0, now.shape[2] // 256, group, 0)


def spectral_kernel(has_past, half, pieces, *refs):
    place, ring, block = refs[0], refs[1 : RADIX + 1], refs[RADIX + 1]
    kernel_now, past_sum, table, twist, twist_ring = refs[RADIX + 2 : RADIX + 7]
    rest = list(refs[RADIX + 7 :])
    if has_past:
        kernel_past, spec_past = rest.pop(0), rest.pop(0)
        spec_out = None
    if half > 0:
        rest = rest[len(pieces) - 1 :]
    ring_out = []
    if half == 0:
        ring_out, rest = rest[:RADIX], rest[RADIX:]
        pieces = pieces[1:]
    outs, rest = rest[: len(pieces)], rest[len(pieces) :]
    if not has_past:
        spec_out = rest.pop(0)
    held, turned, total, spread = rest
    rows = block.shape[3]
    inner = RADIX * 16
    length = total.shape[2]

    def group(g, carry):
        at = pl.ds(pl.multiple_of(g * 16, 16), 16)
        values = [(ring[n][0, 0, at, :], ring[n][0, 1, at, :]) for n in range(RADIX)]
        for k, value in enumerate(sixteen(values, 1)):
            store_split(held, k, g, 0, *twisted(value, twist_ring, k, 0, -1))
        values = [(block[n, 0, 0, at, :], block[n, 0, 1, at, :]) for n in range(RADIX)]
        for k, value in enumerate(sixteen(values, -1)):
            store_split(held, k, g, 128, *twisted(value, twist, k, 128, -1))
        return carry

    lax.fori_loop(0, rows // 16, group, 0)

    def wave(pair, carry):
        both = product(table, held, pair, 0)
        for odd in range(2):
            for part in range(2):
                turned[part, pl.ds(2 * pair + odd, inner, RADIX), :] = both[
                    part * inner : part * inner + inner, odd * 128 : odd * 128 + 128
                ]
        return carry

    lax.fori_loop(0, RADIX // 2, wave, 0)

    def convolve(b, carry):
        cols = pl.ds(pl.multiple_of(b * 256, 256), 256)
        weight = kernel_now[0, 0, :, cols].astype(f32)
        for part in range(2):
            spec = turned[part, cols, :].T.astype(bf16)
            value = weight * spec.astype(f32) + past_sum[part, :, cols]
            if has_past:
                value = value + kernel_past[0, 0, :, cols].astype(f32) * spec_past[
                    part, :, cols
                ].astype(f32)
            else:
                spec_out[part, :, cols] = spec
            total[part, :, cols] = value
        return carry

    lax.fori_loop(0, length // 256, convolve, 0)

    def group_back(g, carry):
        at = pl.ds(pl.multiple_of(g * 16, 16), 16)
        for lane in range(0, inner, 128):
            values = [
                (total[0, at, pl.ds(n * inner + lane, 128)], total[1, at, pl.ds(n * inner + lane, 128)])
                for n in range(RADIX)
            ]
            for k, value in enumerate(sixteen(values, 1)):
                real, imag = twisted(value, twist, k, lane, 1)
                store_split(held, k, g, lane, imag, real)
        return carry

    lax.fori_loop(0, rows // 16, group_back, 0)

    def wave_back(pair, carry):
        both = product(table, held, pair, 0)
        if half == 0:
            store_ring(place, spread, both, ring_out, pair, 0, 1, 0)
        slabs = outs[0].shape[0]
        per = inner // slabs
        for slab in range(slabs):
            for out, (row, count) in zip(outs, pieces):
                count = count // RADIX
                for part in range(2):
                    first = (1 - part) * inner + slab * per + row // RADIX
                    for odd in range(2):
                        out[slab, 0, part, pl.ds(2 * pair + odd, count, RADIX), :] = both[
                            first : first + count, odd * 128 : odd * 128 + 128
                        ]
        return carry

    lax.fori_loop(0, RADIX // 2, wave_back, 0)


def inverse_kernel(count, *refs):
    blocks = refs[:count]
    ring = blocks[:RADIX] if count > RADIX else None
    table, twist, twist_ring, out, held, turned = refs[count:]
    rows, length = out.shape
    inner = length // RADIX

    def group(g, carry):
        at = pl.ds(pl.multiple_of(g * 16, 16), 16)
        for half in range(inner // 128):
            sign, turn = 1, twist
            if ring is not None and half == 0:
                values = [(ring[n][0, 0, at, :], ring[n][0, 1, at, :]) for n in range(RADIX)]
                sign, turn = -1, twist_ring
            else:
                block = blocks[-1]
                spot = 0 if ring is not None else half
                values = [(block[n, spot, 0, at, :], block[n, spot, 1, at, :]) for n in range(RADIX)]
            for k, value in enumerate(sixteen(values, sign)):
                real, imag = twisted(value, turn, k, half * 128, 1)
                store_split(held, k, g, half * 128, imag, real)
        return carry

    lax.fori_loop(0, rows // 16, group, 0)

    def wave(pair, carry):
        both = product(table, held, pair, inner)
        for odd in range(2):
            turned[pl.ds(2 * pair + odd, inner, RADIX), :] = both[:, odd * 128 : odd * 128 + 128]
        return carry

    lax.fori_loop(0, RADIX // 2, wave, 0)
    scale = 1.0 / (NX * NZ)

    def turn(b, carry):
        cols = pl.ds(pl.multiple_of(b * 256, 256), 256)
        out[:, cols] = turned[cols, :].T[:rows] * scale
        return carry

    lax.fori_loop(0, length // 256, turn, 0)


def whole_spec(array):
    zeros = (0,) * array.ndim
    return pl.BlockSpec(array.shape, lambda *_: zeros)


PARAMS = pltpu.CompilerParams(vmem_limit_bytes=67043328)
SCALARS = pl.BlockSpec(memory_space=pltpu.SMEM)


def ringed(blocks):
    count = lax.axis_size("slab")
    return [blocks[0]] + [
        lax.ppermute(blocks[n], "slab", [(source, (source + n) % count) for source in range(count)])
        for n in range(1, count)
    ]


def exchanged(value):
    return lax.all_to_all(value, "slab", split_axis=0, concat_axis=0, tiled=True)


def local(velocity, kernel, history, impedance, prestress, strength, fault_state):
    slabs = lax.axis_size("slab")
    rows_dev, length = prestress.shape
    inner = length // RADIX
    chunk_rows = rows_dev // CHUNKS
    halves = rows_dev // 128
    if slabs != RADIX or rows_dev != inner or chunk_rows != 128:
        return local_general(
            velocity, kernel, history, impedance, prestress, strength, fault_state
        )
    lags = history.shape[1]
    table_np, twist_np = constant_tables()
    table, twist = jnp.asarray(table_np), jnp.asarray(twist_np)
    is_first = lax.axis_index("side") == 0
    eta_first, eta_second = impedance[0], impedance[1]
    eta_total = eta_first + eta_second
    weight_first, weight_second = eta_second / eta_total, eta_first / eta_total
    scalars = jnp.stack(
        [
            jnp.where(is_first, weight_first, weight_second),
            jnp.where(is_first, weight_second, weight_first),
            eta_first * eta_second / eta_total,
            jnp.where(is_first, eta_first, eta_second),
            jnp.where(is_first, 1.0, -1.0).astype(f32),
        ]
    )

    def tiles(counts, rows=128):
        return [jax.ShapeDtypeStruct((slabs, count, 2, rows, 128), f32) for count in counts]

    def ring_tiles(count):
        return [jax.ShapeDtypeStruct((count, 2, 128, 128), f32)] * slabs

    def forward_shapes(chunk):
        shapes = ring_tiles(halves) if chunk == 0 else tiles([1, 1])
        return shapes, [whole_spec(shape) for shape in shapes]

    me = lax.axis_index("slab")
    place = jnp.reshape(me, (1,)).astype(jnp.int32)
    spread = pltpu.VMEM((2 * inner, 2 * 128), f32)
    held = pltpu.VMEM((RADIX // 2, 256, 4 * inner), bf16)
    rows_shape = jax.ShapeDtypeStruct((chunk_rows, length), f32)
    rows_spec = pl.BlockSpec((chunk_rows, length), lambda *_: (0, 0))

    def chunk_spec(chunk):
        return pl.BlockSpec((chunk_rows, length), lambda *_: (chunk, 0))

    def start(chunk):
        shapes, specs = forward_shapes(chunk)
        return pl.pallas_call(
            start_kernel,
            out_shape=shapes,
            grid=(1,),
            in_specs=[
                SCALARS,
                pl.BlockSpec((1, chunk_rows, length), lambda *_: (0, chunk, 0)),
                whole_spec(table),
                whole_spec(twist),
            ],
            out_specs=specs,
            scratch_shapes=[held, spread],
            compiler_params=PARAMS,
        )(place, velocity, table, twist)

    def middle(chunk, own, other, state):
        shapes, specs = forward_shapes(chunk)
        *sent, state_new = pl.pallas_call(
            middle_kernel,
            out_shape=shapes + [rows_shape],
            grid=(1,),
            in_specs=[
                SCALARS,
                SCALARS,
                rows_spec,
                rows_spec,
                chunk_spec(chunk),
                chunk_spec(chunk),
                chunk_spec(chunk),
                whole_spec(table),
                whole_spec(twist),
            ],
            out_specs=specs + [rows_spec],
            scratch_shapes=[held, spread, pltpu.VMEM((chunk_rows, length), f32)],
            compiler_params=PARAMS,
        )(place, scalars, own, other, prestress, strength, state, table, twist)
        return sent, state_new

    def end(row, own, other, state, before):
        full = jax.ShapeDtypeStruct((rows_dev, length), f32)
        step = 16
        parts = own.shape[0] // step
        base = row // step
        ahead = row % chunk_rows // step
        moving = pl.BlockSpec((step, length), lambda g: (base + g, 0))
        near = pl.BlockSpec((step, length), lambda g: (g, 0))
        held_state = pl.BlockSpec((step, length), lambda g: (ahead + g, 0))
        moving_speed = pl.BlockSpec((1, step, length), lambda g: (0, base + g, 0))
        kept = [pl.BlockSpec(memory_space=pl.ANY)] * len(before)
        return pl.pallas_call(
            end_kernel,
            out_shape=(jax.ShapeDtypeStruct((1, rows_dev, length), f32), full, full),
            grid=(parts,),
            in_specs=[SCALARS, near, near, moving, moving, held_state] + kept,
            out_specs=(moving_speed, moving, moving),
            input_output_aliases={6 + n: n for n in range(len(before))},
            compiler_params=PARAMS,
        )(scalars, own, other, prestress, strength, state, *before)

    def past_sums():
        step = 32
        total = jax.ShapeDtypeStruct((2, rows_dev, length), f32)
        spec = pl.BlockSpec((2, step, length), lambda g: (0, g, 0))
        return pl.pallas_call(
            history_kernel,
            out_shape=(total, total),
            grid=(rows_dev // step,),
            in_specs=[
                pl.BlockSpec((1, lags + 1, step, length), lambda g: (0, 0, g, 0)),
                pl.BlockSpec((1, lags, 2, step, length), lambda g: (0, 0, 0, g, 0)),
            ],
            out_specs=(spec, spec),
            compiler_params=PARAMS,
        )(kernel, history)

    def spectral(half, ring, near, past_sum, past, pieces, before):
        def block(array):
            place = half if array.shape[1] == halves else 0
            shape = (slabs, 1, 2, array.shape[3], 128)
            return pl.BlockSpec(shape, lambda *_: (0, place, 0, 0, 0))

        lag_spec = [
            pl.BlockSpec((1, 1, 128, length), functools.partial(lambda lag, *_: (0, lag, half, 0), lag))
            for lag in range(2)
        ]
        sum_spec = pl.BlockSpec((2, 128, length), lambda *_: (0, half, 0))
        spec_spec = pl.BlockSpec((2, 128, length), lambda *_: (0, 0, 0))
        ring_spec = pl.BlockSpec((1, 2, 128, 128), lambda *_: (half, 0, 0, 0))
        operands = [place, *ring, near, kernel, past_sum, table, twist, twist_ring]
        in_specs = [SCALARS] + [ring_spec] * slabs + [block(near), lag_spec[0], sum_spec]
        in_specs += [whole_spec(table), whole_spec(twist), whole_spec(twist_ring)]
        out_shape = tiles([1]) if half else []
        for row, count in pieces[1:]:
            out_shape += tiles([halves], count)
        out_specs = [block(shape) for shape in out_shape]
        if half == 0:
            shapes = ring_tiles(1)
            out_shape = shapes + out_shape
            out_specs = [whole_spec(shape) for shape in shapes] + out_specs
        if past is not None:
            operands += [kernel, past]
            in_specs += [lag_spec[1], spec_spec]
        else:
            out_shape.append(jax.ShapeDtypeStruct((2, 128, length), bf16))
            out_specs.append(spec_spec)
        aliases = {}
        if before is not None:
            aliases = {len(operands) + n: 1 + n for n in range(len(before))}
            operands += before
            in_specs += [pl.BlockSpec(memory_space=pl.ANY)] * len(before)
        return pl.pallas_call(
            functools.partial(spectral_kernel, past is not None, half, pieces),
            input_output_aliases=aliases,
            out_shape=out_shape,
            grid=(1,),
            in_specs=in_specs,
            out_specs=out_specs,
            scratch_shapes=[
                held,
                pltpu.VMEM((2, length, 128), f32),
                pltpu.VMEM((2, 128, length), f32),
                spread,
            ],
            compiler_params=PARAMS,
        )(*operands)

    def inverse(*blocks):
        rows = blocks[-1].shape[3]
        return pl.pallas_call(
            functools.partial(inverse_kernel, len(blocks)),
            out_shape=jax.ShapeDtypeStruct((rows, length), f32),
            grid=(1,),
            in_specs=[whole_spec(b) for b in (*blocks, table, twist, twist_ring)],
            out_specs=pl.BlockSpec((rows, length), lambda *_: (0, 0)),
            scratch_shapes=[held, pltpu.VMEM((length, 128), f32)],
            compiler_params=PARAMS,
        )(*blocks, table, twist, twist_ring)

    hold = lax.optimization_barrier
    states = [fault_state] * CHUNKS
    past = [None] * halves
    sums, waiting = None, None
    whole, cut = chunk_rows, LAST_CUT
    sent = [start(0), None]
    for step_index in range(STEPS):
        last = step_index == STEPS - 1
        pieces = [(0, whole), (whole, cut), (whole + cut, whole - cut)]
        if not last:
            pieces = [(0, whole), (whole, whole)]
        ring = ringed(sent[0])
        if step_index == 0:
            sent[1] = start(1)
            sent[1], shift = hold((tuple(sent[1]), me))
            turn = lax.broadcasted_iota(jnp.int32, (RADIX, inner), 0) * (
                lax.broadcasted_iota(jnp.int32, (RADIX, inner), 1) + inner * shift
            )
            turn = (turn % length).astype(f32) * (2.0 * math.pi / length)
            twist_ring = jnp.stack([jnp.cos(turn), jnp.sin(turn)])
        else:
            own = inverse(waiting)
            sent[1], states[1] = middle(1, own, swapped(own, "side", 0), states[1])
        near = exchanged(sent[1][0])
        if step_index == 0:
            sums = past_sums()
        near, far, sums = hold((near, sent[1][1], sums))
        far = exchanged(far)
        outs = spectral(0, ring, near, sums[step_index], past[0], pieces, None)
        if step_index == 0:
            past[0] = outs[-1]
        late = outs[slabs : slabs + len(pieces) - 1]
        back = ringed(outs[:slabs])
        far, late = hold((far, list(late)))
        outs = spectral(1, ring, far, sums[step_index], past[1], pieces, late)
        if step_index == 0:
            past[1] = outs[-1]
        more, late = outs[0], outs[1 : len(pieces)]
        more = exchanged(more)
        more, late = hold((more, list(late)))
        waiting = exchanged(late[0])
        own = inverse(*back, more)
        other = swapped(own, "side", 0)
        if not last:
            sent[0], states[0] = middle(0, own, other, states[0])
        if not last:
            continue
        waiting, own, other, final = hold((waiting, own, other, late[1]))
        final = exchanged(final)
        own_near = inverse(waiting)
        other_near = swapped(own_near, "side", 0)
        results = end(0, own, other, states[0], ())
        final, own_near, results = hold((final, own_near, tuple(results)))
        own = inverse(final)
        other = swapped(own, "side", 0)
        results = end(whole, own_near, other_near, states[1], results)
        results = end(whole + cut, own, other, states[1], results)
    return tuple(results)


def solution(mesh):
    placed = (
        P("side", "slab", None),
        P("side", None, "slab", None),
        P("side", None, None, "slab", None),
        P(),
        P("slab", None),
        P("slab", None),
        P("slab", None),
    )
    return jax.shard_map(
        local,
        mesh=mesh,
        in_specs=placed,
        out_specs=(P("side", "slab", None), P("slab", None), P("slab", None)),
        check_vma=False,
    )
```

```python
import functools
import math

import jax
import jax.numpy as jnp
import numpy as np
from jax import lax
from jax.experimental import pallas as pl
from jax.experimental.pallas import tpu as pltpu
from jax.sharding import PartitionSpec as P


NX = 4096
NZ = 4096
NEWTON = 4
STEPS = 2


highest = lax.Precision.HIGHEST


def swapped(value, axis, distance):
    mask = 2**distance
    pairs = [(source, source ^ mask) for source in range(lax.axis_size(axis))]
    return lax.ppermute(value, axis, pairs)


def inverse_sinh(value):
    magnitude = jnp.abs(value)
    result = jnp.log1p(
        magnitude + magnitude * magnitude / (1.0 + jnp.sqrt(1.0 + magnitude * magnitude))
    )
    return jnp.where(value < 0.0, -result, result)


def angle_table(rows_count, cols_count, period, sign):
    first = lax.broadcasted_iota(jnp.int32, (rows_count, cols_count), 0)
    second = lax.broadcasted_iota(jnp.int32, (rows_count, cols_count), 1)
    phase = (first * second % period).astype(jnp.float32) * (2.0 * math.pi / period)
    return (jnp.cos(phase), sign * jnp.sin(phase))


def transform_last(real_part, imag_part, sign, real_only):
    length = real_part.shape[-1]
    inner = min(length, 256)
    outer = length // inner
    leading = real_part.shape[:-1]
    cos_outer, sin_outer = angle_table(outer, outer, outer, sign)
    cos_twist, sin_twist = angle_table(outer, inner, length, sign)
    cos_inner, sin_inner = angle_table(inner, inner, inner, sign)
    shaped_real = real_part.reshape(leading + (outer, inner))
    step_real = jnp.einsum("kn,...nq->...kq", cos_outer, shaped_real, precision=highest)
    step_imag = jnp.einsum("kn,...nq->...kq", sin_outer, shaped_real, precision=highest)
    if imag_part is not None:
        shaped_imag = imag_part.reshape(leading + (outer, inner))
        step_real = step_real - jnp.einsum(
            "kn,...nq->...kq", sin_outer, shaped_imag, precision=highest
        )
        step_imag = step_imag + jnp.einsum(
            "kn,...nq->...kq", cos_outer, shaped_imag, precision=highest
        )
    twist_real = step_real * cos_twist - step_imag * sin_twist
    twist_imag = step_real * sin_twist + step_imag * cos_twist
    out_real = jnp.matmul(twist_real, cos_inner, precision=highest) - jnp.matmul(
        twist_imag, sin_inner, precision=highest
    )
    result_real = jnp.swapaxes(out_real, -1, -2).reshape(leading + (length,))
    if real_only:
        return (result_real, None)
    out_imag = jnp.matmul(twist_real, sin_inner, precision=highest) + jnp.matmul(
        twist_imag, cos_inner, precision=highest
    )
    result_imag = jnp.swapaxes(out_imag, -1, -2).reshape(leading + (length,))
    return (result_real, result_imag)


def to_spectrum(rows_field):
    slab_count = lax.axis_size("slab")
    z_real, z_imag = transform_last(rows_field, None, -1.0, False)
    stacked = jnp.stack([z_real, z_imag])
    rows_dev = stacked.shape[1]
    length_z = stacked.shape[2]
    moved = jnp.transpose(stacked, (0, 2, 1)).reshape(
        2, slab_count, length_z // slab_count, rows_dev
    )
    block = lax.all_to_all(moved, "slab", split_axis=1, concat_axis=3, tiled=True)
    spec_real, spec_imag = transform_last(block[0, 0], block[1, 0], -1.0, False)
    return jnp.stack([spec_real, spec_imag]).astype(jnp.bfloat16)


def to_rows(spec_real, spec_imag):
    slab_count = lax.axis_size("slab")
    x_real, x_imag = transform_last(spec_real, spec_imag, 1.0, False)
    stacked = jnp.stack([x_real, x_imag], axis=1)
    batch = stacked.shape[0]
    kz_dev = stacked.shape[2]
    length_x = stacked.shape[3]
    moved = stacked.reshape(batch, 2, kz_dev, slab_count, length_x // slab_count)
    scale = 1.0 / (NX * NZ)
    turned = jnp.swapaxes(
        lax.all_to_all(moved, "slab", split_axis=3, concat_axis=2, tiled=True)[:, :, :, 0, :], 2, 3
    )
    field_real, _ = transform_last(turned[:, 0], turned[:, 1], 1.0, True)
    return field_real * scale


def local_general(velocity, kernel, history, impedance, prestress, strength, fault_state):
    side_index = lax.axis_index("side")
    is_first = side_index == 0
    eta_first = impedance[0]
    eta_second = impedance[1]
    eta_total = eta_first + eta_second
    weight_first = eta_second / eta_total
    weight_second = eta_first / eta_total
    eta_joint = eta_first * eta_second / eta_total
    own_eta = jnp.where(is_first, eta_first, eta_second)
    own_sign = jnp.where(is_first, 1.0, -1.0).astype(jnp.float32)
    lag_kernel = kernel[0]
    lag_history = history[0]
    kernel_now = lag_kernel[0].astype(jnp.float32)
    speed = velocity[0]
    state_now = fault_state
    rate = jnp.zeros_like(prestress)
    for _ in range(STEPS):
        spec_now = to_spectrum(speed)
        total = kernel_now * spec_now.astype(jnp.float32) + jnp.einsum(
            "lzx,lczx->czx", lag_kernel[1:], lag_history, preferred_element_type=jnp.float32
        )
        force_now = to_rows(total[0][None], total[1][None])[0]
        force_other = swapped(force_now, "side", 0)
        force_first = jnp.where(is_first, force_now, force_other)
        force_second = jnp.where(is_first, force_other, force_now)
        coupled = weight_first * force_first + weight_second * force_second
        locked = prestress + coupled
        friction_rate = locked / (eta_joint + strength)
        factor = 0.5 * jnp.exp(state_now)
        for _ in range(NEWTON):
            scaled = factor * friction_rate
            misfit = strength * inverse_sinh(scaled) + eta_joint * friction_rate - locked
            slope = strength * factor / jnp.sqrt(1.0 + scaled * scaled) + eta_joint
            friction_rate = friction_rate - 0.5 * misfit / slope
        stress = locked - eta_joint * friction_rate
        speed_new = own_sign * (prestress + force_now - stress) / own_eta
        state_new = state_now + 0.25 * (jnp.exp(-state_now) - jnp.abs(friction_rate))
        speed = speed_new
        rate = friction_rate
        state_now = state_new
        lag_history = jnp.concatenate([spec_now[None], lag_history[:-1]], axis=0)
    return (speed[None], rate, state_now)


RADIX = 16
CHUNKS = 2
LAST_CUT = 80
f32 = jnp.float32
bf16 = jnp.bfloat16


def constant_tables():
    inner = NX // RADIX
    grid = np.outer(np.arange(inner), np.arange(inner)) % inner
    phase = grid * (2.0 * np.pi / inner)
    cos, sin = np.cos(phase), np.sin(phase)
    full = np.concatenate(
        [np.concatenate([cos, sin], 1), np.concatenate([-sin, cos], 1)], 0
    ).astype(np.float32)
    high = full.astype(jnp.bfloat16)
    low = (full - high.astype(np.float32)).astype(jnp.bfloat16)
    table = np.concatenate([high, high, low], 1)
    turn = np.outer(np.arange(RADIX), np.arange(inner)) * (2.0 * np.pi / NX)
    twist = np.stack([np.cos(turn), np.sin(turn)]).astype(np.float32)
    return table, twist


def plus(a, b):
    return tuple(
        (p if q is None else q if p is None else p + q) for p, q in zip(a, b)
    )


def minus(a, b):
    return tuple(
        (p if q is None else -q if p is None else p - q) for p, q in zip(a, b)
    )


def times_i(a, sign):
    real, imag = a
    if sign > 0:
        return (None if imag is None else -imag, real)
    return (imag, None if real is None else -real)


def turned_by(a, cos, sin):
    real, imag = a
    if imag is None:
        return (real * cos, real * sin)
    if real is None:
        return (-(imag * sin), imag * cos)
    return (real * cos - imag * sin, real * sin + imag * cos)


def four(x, sign):
    a, b = plus(x[0], x[2]), minus(x[0], x[2])
    c, d = plus(x[1], x[3]), times_i(minus(x[1], x[3]), sign)
    return [plus(a, c), plus(b, d), minus(a, c), minus(b, d)]


def sixteen(x, sign):
    rows = [four([x[4 * m + n] for m in range(4)], sign) for n in range(4)]
    out = [None] * 16
    for k in range(4):
        terms = []
        for n in range(4):
            power = n * k
            term = rows[n][k]
            if power == 4:
                term = times_i(term, sign)
            elif power:
                angle = 2.0 * math.pi * power / 16
                term = turned_by(term, math.cos(angle), sign * math.sin(angle))
            terms.append(term)
        for m, value in enumerate(four(terms, sign)):
            out[k + 4 * m] = value
    return out


def store_split(held, k, group, lane, first, second):
    inner = NX // RADIX
    rows = pl.ds(pl.multiple_of(group * 16 + (k % 2) * 128, 16), 16)
    for place, value in ((0, first), (1, second)):
        high = value.astype(bf16)
        low = (value - high.astype(f32)).astype(bf16)
        held[k // 2, rows, pl.ds(place * inner + lane, 128)] = high
        held[k // 2, rows, pl.ds((2 + place) * inner + lane, 128)] = low


def twisted(value, twist, k, lane, sign):
    if k == 0:
        real, imag = value
        return (real, jnp.zeros_like(real) if imag is None else imag)
    cos = twist[0, k : k + 1, pl.ds(lane, 128)]
    sin = twist[1, k : k + 1, pl.ds(lane, 128)]
    return turned_by(value, cos, sin if sign > 0 else -sin)


def product(table, held, k, start):
    wide = table.shape[1] // 3
    rows = pl.ds(start, table.shape[0] - start)
    dims = (((1,), (1,)), ((), ()))
    return lax.dot_general(
        table[rows, : 2 * wide], held[k], dims, preferred_element_type=f32
    ) + lax.dot_general(
        table[rows, 2 * wide :], held[k, :, :wide], dims, preferred_element_type=f32
    )


def picked(refs, half):
    return (refs[0], half) if len(refs) == 1 else (refs[half], 0)


def store_ring(place, spread, both, outs, pair, lead, first_part, row):
    inner = both.shape[0] // 2
    per = inner // RADIX
    spread[...] = both
    for n in range(RADIX):
        target = lax.rem(place[0] + n, RADIX)
        for part in range(2):
            base = (part if first_part == 0 else 1 - part) * inner
            rows = pl.ds(pl.multiple_of(base + target * per + row, 8), 8)
            for odd in range(2):
                outs[n][lead, part, pl.ds(2 * pair + odd, 8, RADIX), :] = spread[
                    rows, odd * 128 : odd * 128 + 128
                ]


def forward_rows(rows_ref, table, twist, place, outs, held, spread):
    rows, length = rows_ref.shape
    inner = length // RADIX

    def group(g, carry):
        at = pl.ds(pl.multiple_of(g * 16, 16), 16)
        for lane in range(0, inner, 128):
            values = [(rows_ref[at, pl.ds(n * inner + lane, 128)], None) for n in range(RADIX)]
            for k, value in enumerate(sixteen(values, -1)):
                store_split(held, k, g, lane, *twisted(value, twist, k, lane, -1))
        return carry

    lax.fori_loop(0, rows // 16, group, 0)

    def wave(pair, carry):
        both = product(table, held, pair, 0)
        if len(outs) == RADIX:
            for half in range(2):
                store_ring(place, spread, both, outs, pair, half, 0, half * 8)
            return carry
        slabs, halves = outs[0].shape[0], 2
        per = inner // slabs // halves
        for slab in range(slabs):
            for half in range(halves):
                out, spot = picked(outs, half)
                for part in range(2):
                    first = part * inner + (slab * halves + half) * per
                    for odd in range(2):
                        out[slab, spot, part, pl.ds(2 * pair + odd, per, RADIX), :] = both[
                            first : first + per, odd * 128 : odd * 128 + 128
                        ]
        return carry

    lax.fori_loop(0, RADIX // 2, wave, 0)


def start_kernel(place, velocity, table, twist, *refs):
    forward_rows(velocity.at[0], table, twist, place, refs[:-2], *refs[-2:])


def friction(scalars, own, other, prestress, strength, state):
    weight_own, weight_other, joint, eta, sign = [scalars[n] for n in range(5)]
    locked = prestress + (weight_own * own + weight_other * other)
    rate = locked / (joint + strength)
    factor = 0.5 * jnp.exp(state)
    for _ in range(NEWTON):
        scaled = factor * rate
        wide = 1.0 + scaled * scaled
        narrow = lax.rsqrt(wide)
        bent = jnp.log(jnp.abs(scaled) + wide * narrow)
        bent = jnp.where(scaled < 0.0, -bent, bent)
        misfit = strength * bent + joint * rate - locked
        slope = strength * factor * narrow + joint
        rate = rate - 0.5 * misfit / slope
    stress = locked - joint * rate
    speed = (sign / eta) * (prestress + own - stress)
    state_new = state + 0.25 * (jnp.exp(-state) - jnp.abs(rate))
    return speed, rate, state_new


def middle_kernel(place, scalars, own, other, prestress, strength, state, table, twist, *refs):
    outs = refs[:-4]
    state_out, held, spread, speed_held = refs[-4:]

    def group(g, carry):
        at = pl.ds(pl.multiple_of(g * 8, 8), 8)
        for lane in range(0, own.shape[1], 1024):
            cols = pl.ds(lane, 1024)
            speed, _, state_new = friction(
                scalars,
                own[at, cols],
                other[at, cols],
                prestress[at, cols],
                strength[at, cols],
                state[at, cols],
            )
            speed_held[at, cols] = speed
            state_out[at, cols] = state_new
        return carry

    lax.fori_loop(0, own.shape[0] // 8, group, 0)
    forward_rows(speed_held, table, twist, place, outs, held, spread)


def end_kernel(scalars, own, other, prestress, strength, state, *refs):
    speed_out, rate_out, state_out = refs[-3:]

    def group(g, carry):
        at = pl.ds(pl.multiple_of(g * 8, 8), 8)
        for lane in range(0, own.shape[1], 1024):
            cols = pl.ds(lane, 1024)
            speed, rate, state_new = friction(
                scalars,
                own[at, cols],
                other[at, cols],
                prestress[at, cols],
                strength[at, cols],
                state[at, cols],
            )
            speed_out[0, at, cols] = speed
            rate_out[at, cols] = rate
            state_out[at, cols] = state_new
        return carry

    lax.fori_loop(0, own.shape[0] // 8, group, 0)


def history_kernel(kernel, history, now, later):
    def group(g, carry):
        cols = pl.ds(pl.multiple_of(g * 256, 256), 256)
        lags = [kernel[0, n, :, cols].astype(f32) for n in range(kernel.shape[1])]
        for part in range(2):
            total_now = total_later = 0.0
            for n in range(history.shape[1]):
                past = history[0, n, part, :, cols].astype(f32)
                total_now = total_now + lags[n + 1] * past
                if n + 2 < len(lags):
                    total_later = total_later + lags[n + 2] * past
            now[part, :, cols] = total_now
            later[part, :, cols] = total_later
        return carry

    lax.fori_loop(0, now.shape[2] // 256, group, 0)


def spectral_kernel(count, has_past, half, pieces, *refs):
    place, ring, block = refs[0], refs[1 : count + 1], refs[count + 1]
    kernel_now, past_sum, table, twist, twist_ring = refs[count + 2 : count + 7]
    rest = list(refs[count + 7 :])
    if has_past:
        kernel_past, spec_past = rest.pop(0), rest.pop(0)
        spec_out = None
    if half > 0:
        rest = rest[len(pieces) - 1 :]
    ring_out = []
    if half == 0:
        ring_out, rest = rest[:RADIX], rest[RADIX:]
        pieces = pieces[1:]
    outs, rest = rest[: len(pieces)], rest[len(pieces) :]
    if not has_past:
        spec_out = rest.pop(0)
    held, turned, total, spread = rest
    rows = block.shape[3]
    inner = RADIX * 16
    length = total.shape[2]

    def group(g, carry):
        at = pl.ds(pl.multiple_of(g * 16, 16), 16)
        if count == 1:
            values = [(ring[0][n, 0, 0, at, :], ring[0][n, 0, 1, at, :]) for n in range(RADIX)]
            sign, turn = -1, twist
        else:
            values = [(ring[n][0, 0, at, :], ring[n][0, 1, at, :]) for n in range(RADIX)]
            sign, turn = 1, twist_ring
        for k, value in enumerate(sixteen(values, sign)):
            store_split(held, k, g, 0, *twisted(value, turn, k, 0, -1))
        values = [(block[n, 0, 0, at, :], block[n, 0, 1, at, :]) for n in range(RADIX)]
        for k, value in enumerate(sixteen(values, -1)):
            store_split(held, k, g, 128, *twisted(value, twist, k, 128, -1))
        return carry

    lax.fori_loop(0, rows // 16, group, 0)

    def wave(pair, carry):
        both = product(table, held, pair, 0)
        for odd in range(2):
            for part in range(2):
                turned[part, pl.ds(2 * pair + odd, inner, RADIX), :] = both[
                    part * inner : part * inner + inner, odd * 128 : odd * 128 + 128
                ]
        return carry

    lax.fori_loop(0, RADIX // 2, wave, 0)

    def convolve(b, carry):
        cols = pl.ds(pl.multiple_of(b * 256, 256), 256)
        weight = kernel_now[0, 0, :, cols].astype(f32)
        for part in range(2):
            spec = turned[part, cols, :].T.astype(bf16)
            value = weight * spec.astype(f32) + past_sum[part, :, cols]
            if has_past:
                value = value + kernel_past[0, 0, :, cols].astype(f32) * spec_past[
                    part, :, cols
                ].astype(f32)
            else:
                spec_out[part, :, cols] = spec
            total[part, :, cols] = value
        return carry

    lax.fori_loop(0, length // 256, convolve, 0)

    def group_back(g, carry):
        at = pl.ds(pl.multiple_of(g * 16, 16), 16)
        for lane in range(0, inner, 128):
            values = [
                (total[0, at, pl.ds(n * inner + lane, 128)], total[1, at, pl.ds(n * inner + lane, 128)])
                for n in range(RADIX)
            ]
            for k, value in enumerate(sixteen(values, 1)):
                real, imag = twisted(value, twist, k, lane, 1)
                store_split(held, k, g, lane, imag, real)
        return carry

    lax.fori_loop(0, rows // 16, group_back, 0)

    def wave_back(pair, carry):
        both = product(table, held, pair, 0)
        if half == 0:
            store_ring(place, spread, both, ring_out, pair, 0, 1, 0)
        slabs = outs[0].shape[0]
        per = inner // slabs
        for slab in range(slabs):
            for out, (row, count) in zip(outs, pieces):
                count = count // RADIX
                for part in range(2):
                    first = (1 - part) * inner + slab * per + row // RADIX
                    for odd in range(2):
                        out[slab, 0, part, pl.ds(2 * pair + odd, count, RADIX), :] = both[
                            first : first + count, odd * 128 : odd * 128 + 128
                        ]
        return carry

    lax.fori_loop(0, RADIX // 2, wave_back, 0)


def inverse_kernel(count, *refs):
    blocks = refs[:count]
    ring = blocks[:RADIX] if count > RADIX else None
    table, twist, twist_ring, out, held, turned = refs[count:]
    rows, length = out.shape
    inner = length // RADIX

    def group(g, carry):
        at = pl.ds(pl.multiple_of(g * 16, 16), 16)
        for half in range(inner // 128):
            sign, turn = 1, twist
            if ring is not None and half == 0:
                values = [(ring[n][0, 0, at, :], ring[n][0, 1, at, :]) for n in range(RADIX)]
                sign, turn = -1, twist_ring
            else:
                block = blocks[-1]
                spot = 0 if ring is not None else half
                values = [(block[n, spot, 0, at, :], block[n, spot, 1, at, :]) for n in range(RADIX)]
            for k, value in enumerate(sixteen(values, sign)):
                real, imag = twisted(value, turn, k, half * 128, 1)
                store_split(held, k, g, half * 128, imag, real)
        return carry

    lax.fori_loop(0, rows // 16, group, 0)

    def wave(pair, carry):
        both = product(table, held, pair, inner)
        for odd in range(2):
            turned[pl.ds(2 * pair + odd, inner, RADIX), :] = both[:, odd * 128 : odd * 128 + 128]
        return carry

    lax.fori_loop(0, RADIX // 2, wave, 0)
    scale = 1.0 / (NX * NZ)

    def turn(b, carry):
        cols = pl.ds(pl.multiple_of(b * 256, 256), 256)
        out[:, cols] = turned[cols, :].T[:rows] * scale
        return carry

    lax.fori_loop(0, length // 256, turn, 0)


def whole_spec(array):
    zeros = (0,) * array.ndim
    return pl.BlockSpec(array.shape, lambda *_: zeros)


PARAMS = pltpu.CompilerParams(vmem_limit_bytes=67043328)
SCALARS = pl.BlockSpec(memory_space=pltpu.SMEM)


def ringed(blocks):
    count = lax.axis_size("slab")
    return [blocks[0]] + [
        lax.ppermute(blocks[n], "slab", [(source, (source + n) % count) for source in range(count)])
        for n in range(1, count)
    ]


def exchanged(value):
    return lax.all_to_all(value, "slab", split_axis=0, concat_axis=0, tiled=True)


def local(velocity, kernel, history, impedance, prestress, strength, fault_state):
    slabs = lax.axis_size("slab")
    rows_dev, length = prestress.shape
    inner = length // RADIX
    chunk_rows = rows_dev // CHUNKS
    halves = rows_dev // 128
    if slabs != RADIX or rows_dev != inner or chunk_rows != 128:
        return local_general(
            velocity, kernel, history, impedance, prestress, strength, fault_state
        )
    lags = history.shape[1]
    table_np, twist_np = constant_tables()
    table, twist = jnp.asarray(table_np), jnp.asarray(twist_np)
    is_first = lax.axis_index("side") == 0
    eta_first, eta_second = impedance[0], impedance[1]
    eta_total = eta_first + eta_second
    weight_first, weight_second = eta_second / eta_total, eta_first / eta_total
    scalars = jnp.stack(
        [
            jnp.where(is_first, weight_first, weight_second),
            jnp.where(is_first, weight_second, weight_first),
            eta_first * eta_second / eta_total,
            jnp.where(is_first, eta_first, eta_second),
            jnp.where(is_first, 1.0, -1.0).astype(f32),
        ]
    )

    def tiles(counts, rows=128):
        return [jax.ShapeDtypeStruct((slabs, count, 2, rows, 128), f32) for count in counts]

    def ring_tiles(count):
        return [jax.ShapeDtypeStruct((count, 2, 128, 128), f32)] * slabs

    def forward_shapes(chunk, ring):
        shapes = ring_tiles(halves) if ring else tiles([[halves], [1, 1]][chunk])
        return shapes, [whole_spec(shape) for shape in shapes]

    me = lax.axis_index("slab")
    place = jnp.reshape(me, (1,)).astype(jnp.int32)
    spread = pltpu.VMEM((2 * inner, 2 * 128), f32)
    held = pltpu.VMEM((RADIX // 2, 256, 4 * inner), bf16)
    rows_shape = jax.ShapeDtypeStruct((chunk_rows, length), f32)
    rows_spec = pl.BlockSpec((chunk_rows, length), lambda *_: (0, 0))

    def chunk_spec(chunk):
        return pl.BlockSpec((chunk_rows, length), lambda *_: (chunk, 0))

    def start(chunk):
        shapes, specs = forward_shapes(chunk, chunk == 0)
        return pl.pallas_call(
            start_kernel,
            out_shape=shapes,
            grid=(1,),
            in_specs=[
                SCALARS,
                pl.BlockSpec((1, chunk_rows, length), lambda *_: (0, chunk, 0)),
                whole_spec(table),
                whole_spec(twist),
            ],
            out_specs=specs,
            scratch_shapes=[held, spread],
            compiler_params=PARAMS,
        )(place, velocity, table, twist)

    def middle(chunk, own, other, state):
        shapes, specs = forward_shapes(chunk, False)
        *sent, state_new = pl.pallas_call(
            middle_kernel,
            out_shape=shapes + [rows_shape],
            grid=(1,),
            in_specs=[
                SCALARS,
                SCALARS,
                rows_spec,
                rows_spec,
                chunk_spec(chunk),
                chunk_spec(chunk),
                chunk_spec(chunk),
                whole_spec(table),
                whole_spec(twist),
            ],
            out_specs=specs + [rows_spec],
            scratch_shapes=[held, spread, pltpu.VMEM((chunk_rows, length), f32)],
            compiler_params=PARAMS,
        )(place, scalars, own, other, prestress, strength, state, table, twist)
        return sent, state_new

    def end(row, own, other, state, before):
        full = jax.ShapeDtypeStruct((rows_dev, length), f32)
        step = 16
        parts = own.shape[0] // step
        base = row // step
        ahead = row % chunk_rows // step
        moving = pl.BlockSpec((step, length), lambda g: (base + g, 0))
        near = pl.BlockSpec((step, length), lambda g: (g, 0))
        held_state = pl.BlockSpec((step, length), lambda g: (ahead + g, 0))
        moving_speed = pl.BlockSpec((1, step, length), lambda g: (0, base + g, 0))
        kept = [pl.BlockSpec(memory_space=pl.ANY)] * len(before)
        return pl.pallas_call(
            end_kernel,
            out_shape=(jax.ShapeDtypeStruct((1, rows_dev, length), f32), full, full),
            grid=(parts,),
            in_specs=[SCALARS, near, near, moving, moving, held_state] + kept,
            out_specs=(moving_speed, moving, moving),
            input_output_aliases={6 + n: n for n in range(len(before))},
            compiler_params=PARAMS,
        )(scalars, own, other, prestress, strength, state, *before)

    def past_sums():
        step = 32
        total = jax.ShapeDtypeStruct((2, rows_dev, length), f32)
        spec = pl.BlockSpec((2, step, length), lambda g: (0, g, 0))
        return pl.pallas_call(
            history_kernel,
            out_shape=(total, total),
            grid=(rows_dev // step,),
            in_specs=[
                pl.BlockSpec((1, lags + 1, step, length), lambda g: (0, 0, g, 0)),
                pl.BlockSpec((1, lags, 2, step, length), lambda g: (0, 0, 0, g, 0)),
            ],
            out_specs=(spec, spec),
            compiler_params=PARAMS,
        )(kernel, history)

    def spectral(half, ring, near, past_sum, past, pieces, before):
        def block(array):
            place = half if array.shape[1] == halves else 0
            shape = (slabs, 1, 2, array.shape[3], 128)
            return pl.BlockSpec(shape, lambda *_: (0, place, 0, 0, 0))

        lag_spec = [
            pl.BlockSpec((1, 1, 128, length), functools.partial(lambda lag, *_: (0, lag, half, 0), lag))
            for lag in range(2)
        ]
        sum_spec = pl.BlockSpec((2, 128, length), lambda *_: (0, half, 0))
        spec_spec = pl.BlockSpec((2, 128, length), lambda *_: (0, 0, 0))
        ring_spec = pl.BlockSpec((1, 2, 128, 128), lambda *_: (half, 0, 0, 0))
        operands = [place, *ring, near, kernel, past_sum, table, twist, twist_ring]
        in_specs = [SCALARS] + ([ring_spec] * slabs if len(ring) > 1 else [block(ring[0])])
        in_specs += [block(near), lag_spec[0], sum_spec]
        in_specs += [whole_spec(table), whole_spec(twist), whole_spec(twist_ring)]
        out_shape = tiles([1]) if half else []
        for row, count in pieces[1:]:
            out_shape += tiles([halves], count)
        out_specs = [block(shape) for shape in out_shape]
        if half == 0:
            shapes = ring_tiles(1)
            out_shape = shapes + out_shape
            out_specs = [whole_spec(shape) for shape in shapes] + out_specs
        if past is not None:
            operands += [kernel, past]
            in_specs += [lag_spec[1], spec_spec]
        else:
            out_shape.append(jax.ShapeDtypeStruct((2, 128, length), bf16))
            out_specs.append(spec_spec)
        aliases = {}
        if before is not None:
            aliases = {len(operands) + n: 1 + n for n in range(len(before))}
            operands += before
            in_specs += [pl.BlockSpec(memory_space=pl.ANY)] * len(before)
        return pl.pallas_call(
            functools.partial(spectral_kernel, len(ring), past is not None, half, pieces),
            input_output_aliases=aliases,
            out_shape=out_shape,
            grid=(1,),
            in_specs=in_specs,
            out_specs=out_specs,
            scratch_shapes=[
                held,
                pltpu.VMEM((2, length, 128), f32),
                pltpu.VMEM((2, 128, length), f32),
                spread,
            ],
            compiler_params=PARAMS,
        )(*operands)

    def inverse(*blocks):
        rows = blocks[-1].shape[3]
        return pl.pallas_call(
            functools.partial(inverse_kernel, len(blocks)),
            out_shape=jax.ShapeDtypeStruct((rows, length), f32),
            grid=(1,),
            in_specs=[whole_spec(b) for b in (*blocks, table, twist, twist_ring)],
            out_specs=pl.BlockSpec((rows, length), lambda *_: (0, 0)),
            scratch_shapes=[held, pltpu.VMEM((length, 128), f32)],
            compiler_params=PARAMS,
        )(*blocks, table, twist, twist_ring)

    hold = lax.optimization_barrier
    states = [fault_state] * CHUNKS
    past = [None] * halves
    sums, waiting = None, None
    whole, cut = chunk_rows, LAST_CUT
    sent = [start(0), None]
    for step_index in range(STEPS):
        last = step_index == STEPS - 1
        pieces = [(0, whole), (whole, cut), (whole + cut, whole - cut)]
        if not last:
            pieces = [(0, whole), (whole, whole)]
        ring = ringed(sent[0]) if step_index == 0 else [exchanged(sent[0][0])]
        if step_index == 0:
            sent[1] = start(1)
            sent[1], shift = hold((tuple(sent[1]), me))
            turn = lax.broadcasted_iota(jnp.int32, (RADIX, inner), 0) * (
                lax.broadcasted_iota(jnp.int32, (RADIX, inner), 1) + inner * shift
            )
            turn = (turn % length).astype(f32) * (2.0 * math.pi / length)
            twist_ring = jnp.stack([jnp.cos(turn), jnp.sin(turn)])
        else:
            own = inverse(waiting)
            sent[1], states[1] = middle(1, own, swapped(own, "side", 0), states[1])
            ring, sent[1], states[1] = hold((ring, sent[1], states[1]))
        near = exchanged(sent[1][0])
        if step_index == 0:
            sums = past_sums()
        near, far, sums = hold((near, sent[1][1], sums))
        far = exchanged(far)
        outs = spectral(0, ring, near, sums[step_index], past[0], pieces, None)
        if step_index == 0:
            past[0] = outs[-1]
        late = outs[slabs : slabs + len(pieces) - 1]
        back = ringed(outs[:slabs])
        far, late = hold((far, list(late)))
        outs = spectral(1, ring, far, sums[step_index], past[1], pieces, late)
        if step_index == 0:
            past[1] = outs[-1]
        more, late = outs[0], outs[1 : len(pieces)]
        more = exchanged(more)
        more, late = hold((more, list(late)))
        waiting = exchanged(late[0])
        own = inverse(*back, more)
        other = swapped(own, "side", 0)
        if not last:
            sent[0], states[0] = middle(0, own, other, states[0])
        if not last:
            waiting, sent[0], states[0] = hold((waiting, sent[0], states[0]))
            continue
        waiting, own, other, final = hold((waiting, own, other, late[1]))
        final = exchanged(final)
        own_near = inverse(waiting)
        other_near = swapped(own_near, "side", 0)
        results = end(0, own, other, states[0], ())
        final, own_near, results = hold((final, own_near, tuple(results)))
        own = inverse(final)
        other = swapped(own, "side", 0)
        results = end(whole, own_near, other_near, states[1], results)
        results = end(whole + cut, own, other, states[1], results)
    return tuple(results)


def solution(mesh):
    placed = (
        P("side", "slab", None),
        P("side", None, "slab", None),
        P("side", None, None, "slab", None),
        P(),
        P("slab", None),
        P("slab", None),
        P("slab", None),
    )
    return jax.shard_map(
        local,
        mesh=mesh,
        in_specs=placed,
        out_specs=(P("side", "slab", None), P("slab", None), P("slab", None)),
        check_vma=False,
    )
```

```python
import functools
import math

import jax
import jax.numpy as jnp
import numpy as np
from jax import lax
from jax.experimental import pallas as pl
from jax.experimental.pallas import tpu as pltpu
from jax.sharding import PartitionSpec as P


NX = 4096
NZ = 4096
NEWTON = 4
STEPS = 2


highest = lax.Precision.HIGHEST


def swapped(value, axis, distance):
    mask = 2**distance
    pairs = [(source, source ^ mask) for source in range(lax.axis_size(axis))]
    return lax.ppermute(value, axis, pairs)


def inverse_sinh(value):
    magnitude = jnp.abs(value)
    result = jnp.log1p(
        magnitude + magnitude * magnitude / (1.0 + jnp.sqrt(1.0 + magnitude * magnitude))
    )
    return jnp.where(value < 0.0, -result, result)


def angle_table(rows_count, cols_count, period, sign):
    first = lax.broadcasted_iota(jnp.int32, (rows_count, cols_count), 0)
    second = lax.broadcasted_iota(jnp.int32, (rows_count, cols_count), 1)
    phase = (first * second % period).astype(jnp.float32) * (2.0 * math.pi / period)
    return (jnp.cos(phase), sign * jnp.sin(phase))


def transform_last(real_part, imag_part, sign, real_only):
    length = real_part.shape[-1]
    inner = min(length, 256)
    outer = length // inner
    leading = real_part.shape[:-1]
    cos_outer, sin_outer = angle_table(outer, outer, outer, sign)
    cos_twist, sin_twist = angle_table(outer, inner, length, sign)
    cos_inner, sin_inner = angle_table(inner, inner, inner, sign)
    shaped_real = real_part.reshape(leading + (outer, inner))
    step_real = jnp.einsum("kn,...nq->...kq", cos_outer, shaped_real, precision=highest)
    step_imag = jnp.einsum("kn,...nq->...kq", sin_outer, shaped_real, precision=highest)
    if imag_part is not None:
        shaped_imag = imag_part.reshape(leading + (outer, inner))
        step_real = step_real - jnp.einsum(
            "kn,...nq->...kq", sin_outer, shaped_imag, precision=highest
        )
        step_imag = step_imag + jnp.einsum(
            "kn,...nq->...kq", cos_outer, shaped_imag, precision=highest
        )
    twist_real = step_real * cos_twist - step_imag * sin_twist
    twist_imag = step_real * sin_twist + step_imag * cos_twist
    out_real = jnp.matmul(twist_real, cos_inner, precision=highest) - jnp.matmul(
        twist_imag, sin_inner, precision=highest
    )
    result_real = jnp.swapaxes(out_real, -1, -2).reshape(leading + (length,))
    if real_only:
        return (result_real, None)
    out_imag = jnp.matmul(twist_real, sin_inner, precision=highest) + jnp.matmul(
        twist_imag, cos_inner, precision=highest
    )
    result_imag = jnp.swapaxes(out_imag, -1, -2).reshape(leading + (length,))
    return (result_real, result_imag)


def to_spectrum(rows_field):
    slab_count = lax.axis_size("slab")
    z_real, z_imag = transform_last(rows_field, None, -1.0, False)
    stacked = jnp.stack([z_real, z_imag])
    rows_dev = stacked.shape[1]
    length_z = stacked.shape[2]
    moved = jnp.transpose(stacked, (0, 2, 1)).reshape(
        2, slab_count, length_z // slab_count, rows_dev
    )
    block = lax.all_to_all(moved, "slab", split_axis=1, concat_axis=3, tiled=True)
    spec_real, spec_imag = transform_last(block[0, 0], block[1, 0], -1.0, False)
    return jnp.stack([spec_real, spec_imag]).astype(jnp.bfloat16)


def to_rows(spec_real, spec_imag):
    slab_count = lax.axis_size("slab")
    x_real, x_imag = transform_last(spec_real, spec_imag, 1.0, False)
    stacked = jnp.stack([x_real, x_imag], axis=1)
    batch = stacked.shape[0]
    kz_dev = stacked.shape[2]
    length_x = stacked.shape[3]
    moved = stacked.reshape(batch, 2, kz_dev, slab_count, length_x // slab_count)
    scale = 1.0 / (NX * NZ)
    turned = jnp.swapaxes(
        lax.all_to_all(moved, "slab", split_axis=3, concat_axis=2, tiled=True)[:, :, :, 0, :], 2, 3
    )
    field_real, _ = transform_last(turned[:, 0], turned[:, 1], 1.0, True)
    return field_real * scale


def local_general(velocity, kernel, history, impedance, prestress, strength, fault_state):
    side_index = lax.axis_index("side")
    is_first = side_index == 0
    eta_first = impedance[0]
    eta_second = impedance[1]
    eta_total = eta_first + eta_second
    weight_first = eta_second / eta_total
    weight_second = eta_first / eta_total
    eta_joint = eta_first * eta_second / eta_total
    own_eta = jnp.where(is_first, eta_first, eta_second)
    own_sign = jnp.where(is_first, 1.0, -1.0).astype(jnp.float32)
    lag_kernel = kernel[0]
    lag_history = history[0]
    kernel_now = lag_kernel[0].astype(jnp.float32)
    speed = velocity[0]
    state_now = fault_state
    rate = jnp.zeros_like(prestress)
    for _ in range(STEPS):
        spec_now = to_spectrum(speed)
        total = kernel_now * spec_now.astype(jnp.float32) + jnp.einsum(
            "lzx,lczx->czx", lag_kernel[1:], lag_history, preferred_element_type=jnp.float32
        )
        force_now = to_rows(total[0][None], total[1][None])[0]
        force_other = swapped(force_now, "side", 0)
        force_first = jnp.where(is_first, force_now, force_other)
        force_second = jnp.where(is_first, force_other, force_now)
        coupled = weight_first * force_first + weight_second * force_second
        locked = prestress + coupled
        friction_rate = locked / (eta_joint + strength)
        factor = 0.5 * jnp.exp(state_now)
        for _ in range(NEWTON):
            scaled = factor * friction_rate
            misfit = strength * inverse_sinh(scaled) + eta_joint * friction_rate - locked
            slope = strength * factor / jnp.sqrt(1.0 + scaled * scaled) + eta_joint
            friction_rate = friction_rate - 0.5 * misfit / slope
        stress = locked - eta_joint * friction_rate
        speed_new = own_sign * (prestress + force_now - stress) / own_eta
        state_new = state_now + 0.25 * (jnp.exp(-state_now) - jnp.abs(friction_rate))
        speed = speed_new
        rate = friction_rate
        state_now = state_new
        lag_history = jnp.concatenate([spec_now[None], lag_history[:-1]], axis=0)
    return (speed[None], rate, state_now)


RADIX = 16
CHUNKS = 2
LAST_CUT = 80
f32 = jnp.float32
bf16 = jnp.bfloat16


def constant_tables():
    inner = NX // RADIX
    grid = np.outer(np.arange(inner), np.arange(inner)) % inner
    phase = grid * (2.0 * np.pi / inner)
    cos, sin = np.cos(phase), np.sin(phase)
    full = np.concatenate(
        [np.concatenate([cos, sin], 1), np.concatenate([-sin, cos], 1)], 0
    ).astype(np.float32)
    high = full.astype(jnp.bfloat16)
    low = (full - high.astype(np.float32)).astype(jnp.bfloat16)
    table = np.concatenate([high, high, low], 1)
    turn = np.outer(np.arange(RADIX), np.arange(inner)) * (2.0 * np.pi / NX)
    twist = np.stack([np.cos(turn), np.sin(turn)]).astype(np.float32)
    return table, twist


def plus(a, b):
    return tuple(
        (p if q is None else q if p is None else p + q) for p, q in zip(a, b)
    )


def minus(a, b):
    return tuple(
        (p if q is None else -q if p is None else p - q) for p, q in zip(a, b)
    )


def times_i(a, sign):
    real, imag = a
    if sign > 0:
        return (None if imag is None else -imag, real)
    return (imag, None if real is None else -real)


def turned_by(a, cos, sin):
    real, imag = a
    if imag is None:
        return (real * cos, real * sin)
    if real is None:
        return (-(imag * sin), imag * cos)
    return (real * cos - imag * sin, real * sin + imag * cos)


def four(x, sign):
    a, b = plus(x[0], x[2]), minus(x[0], x[2])
    c, d = plus(x[1], x[3]), times_i(minus(x[1], x[3]), sign)
    return [plus(a, c), plus(b, d), minus(a, c), minus(b, d)]


def sixteen(x, sign):
    rows = [four([x[4 * m + n] for m in range(4)], sign) for n in range(4)]
    out = [None] * 16
    for k in range(4):
        terms = []
        for n in range(4):
            power = n * k
            term = rows[n][k]
            if power == 4:
                term = times_i(term, sign)
            elif power:
                angle = 2.0 * math.pi * power / 16
                term = turned_by(term, math.cos(angle), sign * math.sin(angle))
            terms.append(term)
        for m, value in enumerate(four(terms, sign)):
            out[k + 4 * m] = value
    return out


def store_split(held, k, group, lane, first, second):
    inner = NX // RADIX
    rows = pl.ds(pl.multiple_of(group * 16 + (k % 2) * 128, 16), 16)
    for place, value in ((0, first), (1, second)):
        high = value.astype(bf16)
        low = (value - high.astype(f32)).astype(bf16)
        held[k // 2, rows, pl.ds(place * inner + lane, 128)] = high
        held[k // 2, rows, pl.ds((2 + place) * inner + lane, 128)] = low


def twisted(value, twist, k, lane, sign):
    if k == 0:
        real, imag = value
        return (real, jnp.zeros_like(real) if imag is None else imag)
    cos = twist[0, k : k + 1, pl.ds(lane, 128)]
    sin = twist[1, k : k + 1, pl.ds(lane, 128)]
    return turned_by(value, cos, sin if sign > 0 else -sin)


def product(table, held, k, start):
    wide = table.shape[1] // 3
    rows = pl.ds(start, table.shape[0] - start)
    dims = (((1,), (1,)), ((), ()))
    return lax.dot_general(
        table[rows, : 2 * wide], held[k], dims, preferred_element_type=f32
    ) + lax.dot_general(
        table[rows, 2 * wide :], held[k, :, :wide], dims, preferred_element_type=f32
    )


def store_ring(place, spread, both, outs, pair, lead, first_part, row):
    inner = both.shape[0] // 2
    per = inner // RADIX
    spread[...] = both
    for n in range(RADIX):
        target = lax.rem(place[0] + n, RADIX)
        for part in range(2):
            base = (part if first_part == 0 else 1 - part) * inner
            rows = pl.ds(pl.multiple_of(base + target * per + row, 8), 8)
            for odd in range(2):
                outs[n][lead, part, pl.ds(2 * pair + odd, 8, RADIX), :] = spread[
                    rows, odd * 128 : odd * 128 + 128
                ]


def forward_rows(rows_ref, table, twist, place, outs, held, spread):
    rows, length = rows_ref.shape
    inner = length // RADIX

    def group(g, carry):
        at = pl.ds(pl.multiple_of(g * 16, 16), 16)
        for lane in range(0, inner, 128):
            values = [(rows_ref[at, pl.ds(n * inner + lane, 128)], None) for n in range(RADIX)]
            for k, value in enumerate(sixteen(values, -1)):
                store_split(held, k, g, lane, *twisted(value, twist, k, lane, -1))
        return carry

    lax.fori_loop(0, rows // 16, group, 0)

    def wave(pair, carry):
        both = product(table, held, pair, 0)
        if len(outs) >= RADIX:
            for half in range(outs[0].shape[0]):
                store_ring(place, spread, both, outs[:RADIX], pair, half, 0, half * 8)
            if len(outs) == RADIX:
                return carry
        slabs, halves = outs[-1].shape[0], 2
        per = inner // slabs // halves
        for slab in range(slabs):
            for half in range(halves - outs[-1].shape[1], halves):
                out, spot = outs[-1], half - halves + outs[-1].shape[1]
                for part in range(2):
                    first = part * inner + (slab * halves + half) * per
                    for odd in range(2):
                        out[slab, spot, part, pl.ds(2 * pair + odd, per, RADIX), :] = both[
                            first : first + per, odd * 128 : odd * 128 + 128
                        ]
        return carry

    lax.fori_loop(0, RADIX // 2, wave, 0)


def start_kernel(place, velocity, table, twist, *refs):
    forward_rows(velocity.at[0], table, twist, place, refs[:-2], *refs[-2:])


def friction(scalars, own, other, prestress, strength, state):
    weight_own, weight_other, joint, eta, sign = [scalars[n] for n in range(5)]
    locked = prestress + (weight_own * own + weight_other * other)
    rate = locked / (joint + strength)
    factor = 0.5 * jnp.exp(state)
    for _ in range(NEWTON):
        scaled = factor * rate
        wide = 1.0 + scaled * scaled
        narrow = lax.rsqrt(wide)
        bent = jnp.log(jnp.abs(scaled) + wide * narrow)
        bent = jnp.where(scaled < 0.0, -bent, bent)
        misfit = strength * bent + joint * rate - locked
        slope = strength * factor * narrow + joint
        rate = rate - 0.5 * misfit / slope
    stress = locked - joint * rate
    speed = (sign / eta) * (prestress + own - stress)
    state_new = state + 0.25 * (jnp.exp(-state) - jnp.abs(rate))
    return speed, rate, state_new


def middle_kernel(place, scalars, own, other, prestress, strength, state, table, twist, *refs):
    outs = refs[:-4]
    state_out, held, spread, speed_held = refs[-4:]

    def group(g, carry):
        at = pl.ds(pl.multiple_of(g * 8, 8), 8)
        for lane in range(0, own.shape[1], 1024):
            cols = pl.ds(lane, 1024)
            speed, _, state_new = friction(
                scalars,
                own[at, cols],
                other[at, cols],
                prestress[at, cols],
                strength[at, cols],
                state[at, cols],
            )
            speed_held[at, cols] = speed
            state_out[at, cols] = state_new
        return carry

    lax.fori_loop(0, own.shape[0] // 8, group, 0)
    forward_rows(speed_held, table, twist, place, outs, held, spread)


def end_kernel(scalars, own, other, prestress, strength, state, *refs):
    speed_out, rate_out, state_out = refs[-3:]

    def group(g, carry):
        at = pl.ds(pl.multiple_of(g * 8, 8), 8)
        for lane in range(0, own.shape[1], 1024):
            cols = pl.ds(lane, 1024)
            speed, rate, state_new = friction(
                scalars,
                own[at, cols],
                other[at, cols],
                prestress[at, cols],
                strength[at, cols],
                state[at, cols],
            )
            speed_out[0, at, cols] = speed
            rate_out[at, cols] = rate
            state_out[at, cols] = state_new
        return carry

    lax.fori_loop(0, own.shape[0] // 8, group, 0)


def history_kernel(kernel, history, now, later):
    def group(g, carry):
        cols = pl.ds(pl.multiple_of(g * 256, 256), 256)
        lags = [kernel[0, n, :, cols].astype(f32) for n in range(kernel.shape[1])]
        for part in range(2):
            total_now = total_later = 0.0
            for n in range(history.shape[1]):
                past = history[0, n, part, :, cols].astype(f32)
                total_now = total_now + lags[n + 1] * past
                if n + 2 < len(lags):
                    total_later = total_later + lags[n + 2] * past
            now[part, :, cols] = total_now
            later[part, :, cols] = total_later
        return carry

    lax.fori_loop(0, now.shape[2] // 256, group, 0)


def spectral_kernel(counts, has_past, half, pieces, *refs):
    count = 1 + sum(counts)
    place, arrived = refs[0], (refs[1 : 1 + counts[0]], refs[1 + counts[0] : count])
    kernel_now, past_sum, table, twist, twist_ring = refs[count : count + 5]
    rest = list(refs[count + 5 :])
    if has_past:
        kernel_past, spec_past = rest.pop(0), rest.pop(0)
        spec_out = None
    if half > 0:
        rest = rest[len(pieces) - 1 :]
    ring_out, rest = rest[:RADIX], rest[RADIX:]
    pieces = pieces[1:]
    outs, rest = rest[: len(pieces)], rest[len(pieces) :]
    if not has_past:
        spec_out = rest.pop(0)
    held, turned, total, spread = rest
    rows = 128
    inner = RADIX * 16
    length = total.shape[2]

    def group(g, carry):
        at = pl.ds(pl.multiple_of(g * 16, 16), 16)
        for chunk, tile in enumerate(arrived):
            if len(tile) == 1:
                values = [(tile[0][n, 0, 0, at, :], tile[0][n, 0, 1, at, :]) for n in range(RADIX)]
                sign, turn = -1, twist
            else:
                values = [(tile[n][0, 0, at, :], tile[n][0, 1, at, :]) for n in range(RADIX)]
                sign, turn = 1, twist_ring
            lane = chunk * 128
            for k, value in enumerate(sixteen(values, sign)):
                store_split(held, k, g, lane, *twisted(value, turn, k, lane, -1))
        return carry

    lax.fori_loop(0, rows // 16, group, 0)

    def wave(pair, carry):
        both = product(table, held, pair, 0)
        for odd in range(2):
            for part in range(2):
                turned[part, pl.ds(2 * pair + odd, inner, RADIX), :] = both[
                    part * inner : part * inner + inner, odd * 128 : odd * 128 + 128
                ]
        return carry

    lax.fori_loop(0, RADIX // 2, wave, 0)

    def convolve(b, carry):
        cols = pl.ds(pl.multiple_of(b * 256, 256), 256)
        weight = kernel_now[0, 0, :, cols].astype(f32)
        for part in range(2):
            spec = turned[part, cols, :].T.astype(bf16)
            value = weight * spec.astype(f32) + past_sum[part, :, cols]
            if has_past:
                value = value + kernel_past[0, 0, :, cols].astype(f32) * spec_past[
                    part, :, cols
                ].astype(f32)
            else:
                spec_out[part, :, cols] = spec
            total[part, :, cols] = value
        return carry

    lax.fori_loop(0, length // 256, convolve, 0)

    def group_back(g, carry):
        at = pl.ds(pl.multiple_of(g * 16, 16), 16)
        for lane in range(0, inner, 128):
            values = [
                (total[0, at, pl.ds(n * inner + lane, 128)], total[1, at, pl.ds(n * inner + lane, 128)])
                for n in range(RADIX)
            ]
            for k, value in enumerate(sixteen(values, 1)):
                real, imag = twisted(value, twist, k, lane, 1)
                store_split(held, k, g, lane, imag, real)
        return carry

    lax.fori_loop(0, rows // 16, group_back, 0)

    def wave_back(pair, carry):
        both = product(table, held, pair, 0)
        store_ring(place, spread, both, ring_out, pair, 0, 1, 0)
        slabs = outs[0].shape[0]
        per = inner // slabs
        for slab in range(slabs):
            for out, (row, count) in zip(outs, pieces):
                count = count // RADIX
                for part in range(2):
                    first = (1 - part) * inner + slab * per + row // RADIX
                    for odd in range(2):
                        out[slab, 0, part, pl.ds(2 * pair + odd, count, RADIX), :] = both[
                            first : first + count, odd * 128 : odd * 128 + 128
                        ]
        return carry

    lax.fori_loop(0, RADIX // 2, wave_back, 0)


def inverse_kernel(count, *refs):
    blocks = refs[:count]
    ring = blocks if count > 1 else None
    table, twist, twist_ring, out, held, turned = refs[count:]
    rows, length = out.shape
    inner = length // RADIX

    def group(g, carry):
        at = pl.ds(pl.multiple_of(g * 16, 16), 16)
        for half in range(inner // 128):
            sign, turn = 1, twist
            if ring is not None:
                tile = ring[half * RADIX : half * RADIX + RADIX]
                values = [(tile[n][0, 0, at, :], tile[n][0, 1, at, :]) for n in range(RADIX)]
                sign, turn = -1, twist_ring
            else:
                block = blocks[0]
                values = [(block[n, half, 0, at, :], block[n, half, 1, at, :]) for n in range(RADIX)]
            for k, value in enumerate(sixteen(values, sign)):
                real, imag = twisted(value, turn, k, half * 128, 1)
                store_split(held, k, g, half * 128, imag, real)
        return carry

    lax.fori_loop(0, rows // 16, group, 0)

    def wave(pair, carry):
        both = product(table, held, pair, inner)
        for odd in range(2):
            turned[pl.ds(2 * pair + odd, inner, RADIX), :] = both[:, odd * 128 : odd * 128 + 128]
        return carry

    lax.fori_loop(0, RADIX // 2, wave, 0)
    scale = 1.0 / (NX * NZ)

    def turn(b, carry):
        cols = pl.ds(pl.multiple_of(b * 256, 256), 256)
        out[:, cols] = turned[cols, :].T[:rows] * scale
        return carry

    lax.fori_loop(0, length // 256, turn, 0)


def whole_spec(array):
    zeros = (0,) * array.ndim
    return pl.BlockSpec(array.shape, lambda *_: zeros)


PARAMS = pltpu.CompilerParams(vmem_limit_bytes=67043328)
SCALARS = pl.BlockSpec(memory_space=pltpu.SMEM)


def is_light(distance, count):
    return min(distance, count - distance) * 3 <= count


def ringed(blocks):
    count = lax.axis_size("slab")
    moved = [blocks[0]]
    for n in range(1, count):
        pairs = [(source, (source + n) % count) for source in range(count)]
        moved.append(lax.ppermute(blocks[n], "slab", pairs))
    return moved


def after_light(arrived, then):
    count = len(arrived)
    light = [n for n in range(1, count) if is_light(n, count)]
    held = lax.optimization_barrier((tuple(arrived[n] for n in light), *then))
    arrived = list(arrived)
    for n, value in zip(light, held[0]):
        arrived[n] = value
    return (arrived, *held[1:])


def exchanged(value):
    return lax.all_to_all(value, "slab", split_axis=0, concat_axis=0, tiled=True)


def local(velocity, kernel, history, impedance, prestress, strength, fault_state):
    slabs = lax.axis_size("slab")
    rows_dev, length = prestress.shape
    inner = length // RADIX
    chunk_rows = rows_dev // CHUNKS
    halves = rows_dev // 128
    if slabs != RADIX or rows_dev != inner or chunk_rows != 128:
        return local_general(
            velocity, kernel, history, impedance, prestress, strength, fault_state
        )
    lags = history.shape[1]
    table_np, twist_np = constant_tables()
    table, twist = jnp.asarray(table_np), jnp.asarray(twist_np)
    is_first = lax.axis_index("side") == 0
    eta_first, eta_second = impedance[0], impedance[1]
    eta_total = eta_first + eta_second
    weight_first, weight_second = eta_second / eta_total, eta_first / eta_total
    scalars = jnp.stack(
        [
            jnp.where(is_first, weight_first, weight_second),
            jnp.where(is_first, weight_second, weight_first),
            eta_first * eta_second / eta_total,
            jnp.where(is_first, eta_first, eta_second),
            jnp.where(is_first, 1.0, -1.0).astype(f32),
        ]
    )

    def tiles(counts, rows=128):
        return [jax.ShapeDtypeStruct((slabs, count, 2, rows, 128), f32) for count in counts]

    def ring_tiles(count):
        return [jax.ShapeDtypeStruct((count, 2, 128, 128), f32)] * slabs

    def forward_shapes(chunk, ring):
        shapes = ring_tiles(1) + tiles([1])
        if chunk == 0:
            shapes = ring_tiles(halves) if ring else tiles([halves])
        return shapes, [whole_spec(shape) for shape in shapes]

    me = lax.axis_index("slab")
    place = jnp.reshape(me, (1,)).astype(jnp.int32)
    spread = pltpu.VMEM((2 * inner, 2 * 128), f32)
    held = pltpu.VMEM((RADIX // 2, 256, 4 * inner), bf16)
    rows_shape = jax.ShapeDtypeStruct((chunk_rows, length), f32)
    rows_spec = pl.BlockSpec((chunk_rows, length), lambda *_: (0, 0))

    def chunk_spec(chunk):
        return pl.BlockSpec((chunk_rows, length), lambda *_: (chunk, 0))

    def start(chunk):
        shapes, specs = forward_shapes(chunk, chunk == 0)
        return pl.pallas_call(
            start_kernel,
            out_shape=shapes,
            grid=(1,),
            in_specs=[
                SCALARS,
                pl.BlockSpec((1, chunk_rows, length), lambda *_: (0, chunk, 0)),
                whole_spec(table),
                whole_spec(twist),
            ],
            out_specs=specs,
            scratch_shapes=[held, spread],
            compiler_params=PARAMS,
        )(place, velocity, table, twist)

    def middle(chunk, own, other, state):
        shapes, specs = forward_shapes(chunk, False)
        *sent, state_new = pl.pallas_call(
            middle_kernel,
            out_shape=shapes + [rows_shape],
            grid=(1,),
            in_specs=[
                SCALARS,
                SCALARS,
                rows_spec,
                rows_spec,
                chunk_spec(chunk),
                chunk_spec(chunk),
                chunk_spec(chunk),
                whole_spec(table),
                whole_spec(twist),
            ],
            out_specs=specs + [rows_spec],
            scratch_shapes=[held, spread, pltpu.VMEM((chunk_rows, length), f32)],
            compiler_params=PARAMS,
        )(place, scalars, own, other, prestress, strength, state, table, twist)
        return sent, state_new

    def end(row, own, other, state, before):
        full = jax.ShapeDtypeStruct((rows_dev, length), f32)
        step = 16
        parts = own.shape[0] // step
        base = row // step
        ahead = row % chunk_rows // step
        moving = pl.BlockSpec((step, length), lambda g: (base + g, 0))
        near = pl.BlockSpec((step, length), lambda g: (g, 0))
        held_state = pl.BlockSpec((step, length), lambda g: (ahead + g, 0))
        moving_speed = pl.BlockSpec((1, step, length), lambda g: (0, base + g, 0))
        kept = [pl.BlockSpec(memory_space=pl.ANY)] * len(before)
        return pl.pallas_call(
            end_kernel,
            out_shape=(jax.ShapeDtypeStruct((1, rows_dev, length), f32), full, full),
            grid=(parts,),
            in_specs=[SCALARS, near, near, moving, moving, held_state] + kept,
            out_specs=(moving_speed, moving, moving),
            input_output_aliases={6 + n: n for n in range(len(before))},
            compiler_params=PARAMS,
        )(scalars, own, other, prestress, strength, state, *before)

    def past_sums():
        step = 32
        total = jax.ShapeDtypeStruct((2, rows_dev, length), f32)
        spec = pl.BlockSpec((2, step, length), lambda g: (0, g, 0))
        return pl.pallas_call(
            history_kernel,
            out_shape=(total, total),
            grid=(rows_dev // step,),
            in_specs=[
                pl.BlockSpec((1, lags + 1, step, length), lambda g: (0, 0, g, 0)),
                pl.BlockSpec((1, lags, 2, step, length), lambda g: (0, 0, 0, g, 0)),
            ],
            out_specs=(spec, spec),
            compiler_params=PARAMS,
        )(kernel, history)

    def spectral(half, ring, near, past_sum, past, pieces, before):
        def block(array):
            place = half if array.shape[1] == halves else 0
            shape = (slabs, 1, 2, array.shape[3], 128)
            return pl.BlockSpec(shape, lambda *_: (0, place, 0, 0, 0))

        lag_spec = [
            pl.BlockSpec((1, 1, 128, length), functools.partial(lambda lag, *_: (0, lag, half, 0), lag))
            for lag in range(2)
        ]
        sum_spec = pl.BlockSpec((2, 128, length), lambda *_: (0, half, 0))
        spec_spec = pl.BlockSpec((2, 128, length), lambda *_: (0, 0, 0))

        def arrived(tile):
            if len(tile) == 1:
                return [block(tile[0])]
            spot = half if tile[0].shape[0] == halves else 0
            return [pl.BlockSpec((1, 2, 128, 128), lambda *_: (spot, 0, 0, 0))] * slabs

        operands = [place, *ring, *near, kernel, past_sum, table, twist, twist_ring]
        in_specs = [SCALARS] + arrived(ring) + arrived(near) + [lag_spec[0], sum_spec]
        in_specs += [whole_spec(table), whole_spec(twist), whole_spec(twist_ring)]
        out_shape = []
        for row, count in pieces[1:]:
            out_shape += tiles([halves], count)
        out_specs = [block(shape) for shape in out_shape]
        shapes = ring_tiles(1)
        out_shape = shapes + out_shape
        out_specs = [whole_spec(shape) for shape in shapes] + out_specs
        if past is not None:
            operands += [kernel, past]
            in_specs += [lag_spec[1], spec_spec]
        else:
            out_shape.append(jax.ShapeDtypeStruct((2, 128, length), bf16))
            out_specs.append(spec_spec)
        aliases = {}
        if before is not None:
            aliases = {len(operands) + n: slabs + n for n in range(len(before))}
            operands += before
            in_specs += [pl.BlockSpec(memory_space=pl.ANY)] * len(before)
        return pl.pallas_call(
            functools.partial(
                spectral_kernel, (len(ring), len(near)), past is not None, half, pieces
            ),
            input_output_aliases=aliases,
            out_shape=out_shape,
            grid=(1,),
            in_specs=in_specs,
            out_specs=out_specs,
            scratch_shapes=[
                held,
                pltpu.VMEM((2, length, 128), f32),
                pltpu.VMEM((2, 128, length), f32),
                spread,
            ],
            compiler_params=PARAMS,
        )(*operands)

    def inverse(*blocks):
        rows = blocks[0].shape[-2]
        return pl.pallas_call(
            functools.partial(inverse_kernel, len(blocks)),
            out_shape=jax.ShapeDtypeStruct((rows, length), f32),
            grid=(1,),
            in_specs=[whole_spec(b) for b in (*blocks, table, twist, twist_ring)],
            out_specs=pl.BlockSpec((rows, length), lambda *_: (0, 0)),
            scratch_shapes=[held, pltpu.VMEM((length, 128), f32)],
            compiler_params=PARAMS,
        )(*blocks, table, twist, twist_ring)

    hold = lax.optimization_barrier
    states = [fault_state] * CHUNKS
    past = [None] * halves
    sums, waiting = None, None
    whole, cut = chunk_rows, LAST_CUT
    sent = [start(0), None]
    for step_index in range(STEPS):
        last = step_index == STEPS - 1
        pieces = [(0, whole), (whole, cut), (whole + cut, whole - cut)]
        if not last:
            pieces = [(0, whole), (whole, whole)]
        ring = ringed(sent[0]) if step_index == 0 else [exchanged(sent[0][0])]
        if step_index == 0:
            sent[1] = start(1)
            sent[1], shift = hold((tuple(sent[1]), me))
            turn = lax.broadcasted_iota(jnp.int32, (RADIX, inner), 0) * (
                lax.broadcasted_iota(jnp.int32, (RADIX, inner), 1) + inner * shift
            )
            turn = (turn % length).astype(f32) * (2.0 * math.pi / length)
            twist_ring = jnp.stack([jnp.cos(turn), jnp.sin(turn)])
        else:
            own = inverse(waiting)
            sent[1], states[1] = middle(1, own, swapped(own, "side", 0), states[1])
        near = ringed(sent[1][:slabs])
        if step_index == 0:
            sums = past_sums()
        near, far, sums = after_light(near, (sent[1][slabs], sums))
        far = exchanged(far)
        outs = spectral(0, ring, near, sums[step_index], past[0], pieces, None)
        if step_index == 0:
            past[0] = outs[-1]
        late = outs[slabs : slabs + len(pieces) - 1]
        back = ringed(outs[:slabs])
        far, late = hold((far, list(late)))
        outs = spectral(1, ring, [far], sums[step_index], past[1], pieces, late)
        if step_index == 0:
            past[1] = outs[-1]
        late = outs[slabs : slabs + len(pieces) - 1]
        more = ringed(outs[:slabs])
        more, late = after_light(more, (list(late),))
        waiting = exchanged(late[0])
        own = inverse(*back, *more)
        other = swapped(own, "side", 0)
        if not last:
            sent[0], states[0] = middle(0, own, other, states[0])
        if not last:
            waiting, sent[0], states[0] = hold((waiting, sent[0], states[0]))
            continue
        waiting, own, other, final = hold((waiting, own, other, late[1]))
        final = exchanged(final)
        own_near = inverse(waiting)
        other_near = swapped(own_near, "side", 0)
        results = end(0, own, other, states[0], ())
        final, own_near, results = hold((final, own_near, tuple(results)))
        own = inverse(final)
        other = swapped(own, "side", 0)
        results = end(whole, own_near, other_near, states[1], results)
        results = end(whole + cut, own, other, states[1], results)
    return tuple(results)


def solution(mesh):
    placed = (
        P("side", "slab", None),
        P("side", None, "slab", None),
        P("side", None, None, "slab", None),
        P(),
        P("slab", None),
        P("slab", None),
        P("slab", None),
    )
    return jax.shard_map(
        local,
        mesh=mesh,
        in_specs=placed,
        out_specs=(P("side", "slab", None), P("slab", None), P("slab", None)),
        check_vma=False,
    )
```

```python
import functools
import math

import jax
import jax.numpy as jnp
import numpy as np
from jax import lax
from jax.experimental import pallas as pl
from jax.experimental.pallas import tpu as pltpu
from jax.sharding import PartitionSpec as P


NX = 4096
NZ = 4096
NEWTON = 4
STEPS = 2


highest = lax.Precision.HIGHEST


def swapped(value, axis, distance):
    mask = 2**distance
    pairs = [(source, source ^ mask) for source in range(lax.axis_size(axis))]
    return lax.ppermute(value, axis, pairs)


def inverse_sinh(value):
    magnitude = jnp.abs(value)
    result = jnp.log1p(
        magnitude + magnitude * magnitude / (1.0 + jnp.sqrt(1.0 + magnitude * magnitude))
    )
    return jnp.where(value < 0.0, -result, result)


def angle_table(rows_count, cols_count, period, sign):
    first = lax.broadcasted_iota(jnp.int32, (rows_count, cols_count), 0)
    second = lax.broadcasted_iota(jnp.int32, (rows_count, cols_count), 1)
    phase = (first * second % period).astype(jnp.float32) * (2.0 * math.pi / period)
    return (jnp.cos(phase), sign * jnp.sin(phase))


def transform_last(real_part, imag_part, sign, real_only):
    length = real_part.shape[-1]
    inner = min(length, 256)
    outer = length // inner
    leading = real_part.shape[:-1]
    cos_outer, sin_outer = angle_table(outer, outer, outer, sign)
    cos_twist, sin_twist = angle_table(outer, inner, length, sign)
    cos_inner, sin_inner = angle_table(inner, inner, inner, sign)
    shaped_real = real_part.reshape(leading + (outer, inner))
    step_real = jnp.einsum("kn,...nq->...kq", cos_outer, shaped_real, precision=highest)
    step_imag = jnp.einsum("kn,...nq->...kq", sin_outer, shaped_real, precision=highest)
    if imag_part is not None:
        shaped_imag = imag_part.reshape(leading + (outer, inner))
        step_real = step_real - jnp.einsum(
            "kn,...nq->...kq", sin_outer, shaped_imag, precision=highest
        )
        step_imag = step_imag + jnp.einsum(
            "kn,...nq->...kq", cos_outer, shaped_imag, precision=highest
        )
    twist_real = step_real * cos_twist - step_imag * sin_twist
    twist_imag = step_real * sin_twist + step_imag * cos_twist
    out_real = jnp.matmul(twist_real, cos_inner, precision=highest) - jnp.matmul(
        twist_imag, sin_inner, precision=highest
    )
    result_real = jnp.swapaxes(out_real, -1, -2).reshape(leading + (length,))
    if real_only:
        return (result_real, None)
    out_imag = jnp.matmul(twist_real, sin_inner, precision=highest) + jnp.matmul(
        twist_imag, cos_inner, precision=highest
    )
    result_imag = jnp.swapaxes(out_imag, -1, -2).reshape(leading + (length,))
    return (result_real, result_imag)


def to_spectrum(rows_field):
    slab_count = lax.axis_size("slab")
    z_real, z_imag = transform_last(rows_field, None, -1.0, False)
    stacked = jnp.stack([z_real, z_imag])
    rows_dev = stacked.shape[1]
    length_z = stacked.shape[2]
    moved = jnp.transpose(stacked, (0, 2, 1)).reshape(
        2, slab_count, length_z // slab_count, rows_dev
    )
    block = lax.all_to_all(moved, "slab", split_axis=1, concat_axis=3, tiled=True)
    spec_real, spec_imag = transform_last(block[0, 0], block[1, 0], -1.0, False)
    return jnp.stack([spec_real, spec_imag]).astype(jnp.bfloat16)


def to_rows(spec_real, spec_imag):
    slab_count = lax.axis_size("slab")
    x_real, x_imag = transform_last(spec_real, spec_imag, 1.0, False)
    stacked = jnp.stack([x_real, x_imag], axis=1)
    batch = stacked.shape[0]
    kz_dev = stacked.shape[2]
    length_x = stacked.shape[3]
    moved = stacked.reshape(batch, 2, kz_dev, slab_count, length_x // slab_count)
    scale = 1.0 / (NX * NZ)
    turned = jnp.swapaxes(
        lax.all_to_all(moved, "slab", split_axis=3, concat_axis=2, tiled=True)[:, :, :, 0, :], 2, 3
    )
    field_real, _ = transform_last(turned[:, 0], turned[:, 1], 1.0, True)
    return field_real * scale


def local_general(velocity, kernel, history, impedance, prestress, strength, fault_state):
    side_index = lax.axis_index("side")
    is_first = side_index == 0
    eta_first = impedance[0]
    eta_second = impedance[1]
    eta_total = eta_first + eta_second
    weight_first = eta_second / eta_total
    weight_second = eta_first / eta_total
    eta_joint = eta_first * eta_second / eta_total
    own_eta = jnp.where(is_first, eta_first, eta_second)
    own_sign = jnp.where(is_first, 1.0, -1.0).astype(jnp.float32)
    lag_kernel = kernel[0]
    lag_history = history[0]
    kernel_now = lag_kernel[0].astype(jnp.float32)
    speed = velocity[0]
    state_now = fault_state
    rate = jnp.zeros_like(prestress)
    for _ in range(STEPS):
        spec_now = to_spectrum(speed)
        total = kernel_now * spec_now.astype(jnp.float32) + jnp.einsum(
            "lzx,lczx->czx", lag_kernel[1:], lag_history, preferred_element_type=jnp.float32
        )
        force_now = to_rows(total[0][None], total[1][None])[0]
        force_other = swapped(force_now, "side", 0)
        force_first = jnp.where(is_first, force_now, force_other)
        force_second = jnp.where(is_first, force_other, force_now)
        coupled = weight_first * force_first + weight_second * force_second
        locked = prestress + coupled
        friction_rate = locked / (eta_joint + strength)
        factor = 0.5 * jnp.exp(state_now)
        for _ in range(NEWTON):
            scaled = factor * friction_rate
            misfit = strength * inverse_sinh(scaled) + eta_joint * friction_rate - locked
            slope = strength * factor / jnp.sqrt(1.0 + scaled * scaled) + eta_joint
            friction_rate = friction_rate - 0.5 * misfit / slope
        stress = locked - eta_joint * friction_rate
        speed_new = own_sign * (prestress + force_now - stress) / own_eta
        state_new = state_now + 0.25 * (jnp.exp(-state_now) - jnp.abs(friction_rate))
        speed = speed_new
        rate = friction_rate
        state_now = state_new
        lag_history = jnp.concatenate([spec_now[None], lag_history[:-1]], axis=0)
    return (speed[None], rate, state_now)


RADIX = 16
CHUNKS = 2
LAST_CUT = 80
f32 = jnp.float32
bf16 = jnp.bfloat16


def constant_tables():
    inner = NX // RADIX
    grid = np.outer(np.arange(inner), np.arange(inner)) % inner
    phase = grid * (2.0 * np.pi / inner)
    cos, sin = np.cos(phase), np.sin(phase)
    full = np.concatenate(
        [np.concatenate([cos, sin], 1), np.concatenate([-sin, cos], 1)], 0
    ).astype(np.float32)
    high = full.astype(jnp.bfloat16)
    low = (full - high.astype(np.float32)).astype(jnp.bfloat16)
    table = np.concatenate([high, high, low], 1)
    turn = np.outer(np.arange(RADIX), np.arange(inner)) * (2.0 * np.pi / NX)
    twist = np.stack([np.cos(turn), np.sin(turn)]).astype(np.float32)
    return table, twist


def plus(a, b):
    return tuple(
        (p if q is None else q if p is None else p + q) for p, q in zip(a, b)
    )


def minus(a, b):
    return tuple(
        (p if q is None else -q if p is None else p - q) for p, q in zip(a, b)
    )


def times_i(a, sign):
    real, imag = a
    if sign > 0:
        return (None if imag is None else -imag, real)
    return (imag, None if real is None else -real)


def turned_by(a, cos, sin):
    real, imag = a
    if imag is None:
        return (real * cos, real * sin)
    if real is None:
        return (-(imag * sin), imag * cos)
    return (real * cos - imag * sin, real * sin + imag * cos)


def four(x, sign):
    a, b = plus(x[0], x[2]), minus(x[0], x[2])
    c, d = plus(x[1], x[3]), times_i(minus(x[1], x[3]), sign)
    return [plus(a, c), plus(b, d), minus(a, c), minus(b, d)]


def sixteen(x, sign):
    rows = [four([x[4 * m + n] for m in range(4)], sign) for n in range(4)]
    out = [None] * 16
    for k in range(4):
        terms = []
        for n in range(4):
            power = n * k
            term = rows[n][k]
            if power == 4:
                term = times_i(term, sign)
            elif power:
                angle = 2.0 * math.pi * power / 16
                term = turned_by(term, math.cos(angle), sign * math.sin(angle))
            terms.append(term)
        for m, value in enumerate(four(terms, sign)):
            out[k + 4 * m] = value
    return out


def store_split(held, k, group, lane, first, second):
    inner = NX // RADIX
    rows = pl.ds(pl.multiple_of(group * 16 + (k % 2) * 128, 16), 16)
    for place, value in ((0, first), (1, second)):
        high = value.astype(bf16)
        low = (value - high.astype(f32)).astype(bf16)
        held[k // 2, rows, pl.ds(place * inner + lane, 128)] = high
        held[k // 2, rows, pl.ds((2 + place) * inner + lane, 128)] = low


def twisted(value, twist, k, lane, sign):
    if k == 0:
        real, imag = value
        return (real, jnp.zeros_like(real) if imag is None else imag)
    cos = twist[0, k : k + 1, pl.ds(lane, 128)]
    sin = twist[1, k : k + 1, pl.ds(lane, 128)]
    return turned_by(value, cos, sin if sign > 0 else -sin)


def product(table, held, k, start):
    wide = table.shape[1] // 3
    rows = pl.ds(start, table.shape[0] - start)
    dims = (((1,), (1,)), ((), ()))
    return lax.dot_general(
        table[rows, : 2 * wide], held[k], dims, preferred_element_type=f32
    ) + lax.dot_general(
        table[rows, 2 * wide :], held[k, :, :wide], dims, preferred_element_type=f32
    )


def store_ring(place, spread, both, outs, pair, lead, first_part, row):
    inner = both.shape[0] // 2
    per = inner // RADIX
    spread[...] = both
    for n in range(RADIX):
        target = lax.rem(place[0] + n, RADIX)
        for part in range(2):
            base = (part if first_part == 0 else 1 - part) * inner
            rows = pl.ds(pl.multiple_of(base + target * per + row, 8), 8)
            for odd in range(2):
                outs[n][lead, part, pl.ds(2 * pair + odd, 8, RADIX), :] = spread[
                    rows, odd * 128 : odd * 128 + 128
                ]


def forward_rows(rows_ref, table, twist, place, outs, held, spread):
    rows, length = rows_ref.shape
    inner = length // RADIX

    def group(g, carry):
        at = pl.ds(pl.multiple_of(g * 16, 16), 16)
        for lane in range(0, inner, 128):
            values = [(rows_ref[at, pl.ds(n * inner + lane, 128)], None) for n in range(RADIX)]
            for k, value in enumerate(sixteen(values, -1)):
                store_split(held, k, g, lane, *twisted(value, twist, k, lane, -1))
        return carry

    lax.fori_loop(0, rows // 16, group, 0)

    def wave(pair, carry):
        both = product(table, held, pair, 0)
        if len(outs) >= RADIX:
            for half in range(outs[0].shape[0]):
                store_ring(place, spread, both, outs[:RADIX], pair, half, 0, half * 8)
            if len(outs) == RADIX:
                return carry
        slabs, halves = outs[-1].shape[0], 2
        per = inner // slabs // halves
        for slab in range(slabs):
            for half in range(halves - outs[-1].shape[1], halves):
                out, spot = outs[-1], half - halves + outs[-1].shape[1]
                for part in range(2):
                    first = part * inner + (slab * halves + half) * per
                    for odd in range(2):
                        out[slab, spot, part, pl.ds(2 * pair + odd, per, RADIX), :] = both[
                            first : first + per, odd * 128 : odd * 128 + 128
                        ]
        return carry

    lax.fori_loop(0, RADIX // 2, wave, 0)


def start_kernel(place, velocity, table, twist, *refs):
    forward_rows(velocity.at[0], table, twist, place, refs[:-2], *refs[-2:])


def friction(scalars, own, other, prestress, strength, state):
    weight_own, weight_other, joint, eta, sign = [scalars[n] for n in range(5)]
    locked = prestress + (weight_own * own + weight_other * other)
    rate = locked / (joint + strength)
    factor = 0.5 * jnp.exp(state)
    for _ in range(NEWTON):
        scaled = factor * rate
        wide = 1.0 + scaled * scaled
        narrow = lax.rsqrt(wide)
        bent = jnp.log(jnp.abs(scaled) + wide * narrow)
        bent = jnp.where(scaled < 0.0, -bent, bent)
        misfit = strength * bent + joint * rate - locked
        slope = strength * factor * narrow + joint
        rate = rate - 0.5 * misfit / slope
    stress = locked - joint * rate
    speed = (sign / eta) * (prestress + own - stress)
    state_new = state + 0.25 * (jnp.exp(-state) - jnp.abs(rate))
    return speed, rate, state_new


def middle_kernel(place, scalars, own, other, prestress, strength, state, table, twist, *refs):
    outs = refs[:-4]
    state_out, held, spread, speed_held = refs[-4:]

    def group(g, carry):
        at = pl.ds(pl.multiple_of(g * 8, 8), 8)
        for lane in range(0, own.shape[1], 1024):
            cols = pl.ds(lane, 1024)
            speed, _, state_new = friction(
                scalars,
                own[at, cols],
                other[at, cols],
                prestress[at, cols],
                strength[at, cols],
                state[at, cols],
            )
            speed_held[at, cols] = speed
            state_out[at, cols] = state_new
        return carry

    lax.fori_loop(0, own.shape[0] // 8, group, 0)
    forward_rows(speed_held, table, twist, place, outs, held, spread)


def end_kernel(scalars, own, other, prestress, strength, state, *refs):
    speed_out, rate_out, state_out = refs[-3:]

    def group(g, carry):
        at = pl.ds(pl.multiple_of(g * 8, 8), 8)
        for lane in range(0, own.shape[1], 1024):
            cols = pl.ds(lane, 1024)
            speed, rate, state_new = friction(
                scalars,
                own[at, cols],
                other[at, cols],
                prestress[at, cols],
                strength[at, cols],
                state[at, cols],
            )
            speed_out[0, at, cols] = speed
            rate_out[at, cols] = rate
            state_out[at, cols] = state_new
        return carry

    lax.fori_loop(0, own.shape[0] // 8, group, 0)


def history_kernel(kernel, history, now, later):
    def group(g, carry):
        cols = pl.ds(pl.multiple_of(g * 256, 256), 256)
        lags = [kernel[0, n, :, cols].astype(f32) for n in range(kernel.shape[1])]
        for part in range(2):
            total_now = total_later = 0.0
            for n in range(history.shape[1]):
                past = history[0, n, part, :, cols].astype(f32)
                total_now = total_now + lags[n + 1] * past
                if n + 2 < len(lags):
                    total_later = total_later + lags[n + 2] * past
            now[part, :, cols] = total_now
            later[part, :, cols] = total_later
        return carry

    lax.fori_loop(0, now.shape[2] // 256, group, 0)


def spectral_kernel(counts, has_past, half, pieces, *refs):
    count = 1 + sum(counts)
    place, arrived = refs[0], (refs[1 : 1 + counts[0]], refs[1 + counts[0] : count])
    kernel_now, past_sum, table, twist, twist_ring = refs[count : count + 5]
    rest = list(refs[count + 5 :])
    if has_past:
        kernel_past, spec_past = rest.pop(0), rest.pop(0)
        spec_out = None
    if half > 0:
        rest = rest[len(pieces) - 1 :]
    ring_out, rest = rest[:RADIX], rest[RADIX:]
    pieces = pieces[1:]
    outs, rest = rest[: len(pieces)], rest[len(pieces) :]
    if not has_past:
        spec_out = rest.pop(0)
    held, turned, total, spread = rest
    rows = 128
    inner = RADIX * 16
    length = total.shape[2]

    def group(g, carry):
        at = pl.ds(pl.multiple_of(g * 16, 16), 16)
        for chunk, tile in enumerate(arrived):
            if len(tile) == 1:
                values = [(tile[0][n, 0, 0, at, :], tile[0][n, 0, 1, at, :]) for n in range(RADIX)]
                sign, turn = -1, twist
            else:
                values = [(tile[n][0, 0, at, :], tile[n][0, 1, at, :]) for n in range(RADIX)]
                sign, turn = 1, twist_ring
            lane = chunk * 128
            for k, value in enumerate(sixteen(values, sign)):
                store_split(held, k, g, lane, *twisted(value, turn, k, lane, -1))
        return carry

    lax.fori_loop(0, rows // 16, group, 0)

    def wave(pair, carry):
        both = product(table, held, pair, 0)
        for odd in range(2):
            for part in range(2):
                turned[part, pl.ds(2 * pair + odd, inner, RADIX), :] = both[
                    part * inner : part * inner + inner, odd * 128 : odd * 128 + 128
                ]
        return carry

    lax.fori_loop(0, RADIX // 2, wave, 0)

    def convolve(b, carry):
        cols = pl.ds(pl.multiple_of(b * 256, 256), 256)
        weight = kernel_now[0, 0, :, cols].astype(f32)
        for part in range(2):
            spec = turned[part, cols, :].T.astype(bf16)
            value = weight * spec.astype(f32) + past_sum[part, :, cols]
            if has_past:
                value = value + kernel_past[0, 0, :, cols].astype(f32) * spec_past[
                    part, :, cols
                ].astype(f32)
            else:
                spec_out[part, :, cols] = spec
            total[part, :, cols] = value
        return carry

    lax.fori_loop(0, length // 256, convolve, 0)

    def group_back(g, carry):
        at = pl.ds(pl.multiple_of(g * 16, 16), 16)
        for lane in range(0, inner, 128):
            values = [
                (total[0, at, pl.ds(n * inner + lane, 128)], total[1, at, pl.ds(n * inner + lane, 128)])
                for n in range(RADIX)
            ]
            for k, value in enumerate(sixteen(values, 1)):
                real, imag = twisted(value, twist, k, lane, 1)
                store_split(held, k, g, lane, imag, real)
        return carry

    lax.fori_loop(0, rows // 16, group_back, 0)

    def wave_back(pair, carry):
        both = product(table, held, pair, 0)
        store_ring(place, spread, both, ring_out, pair, 0, 1, 0)
        slabs = outs[0].shape[0]
        per = inner // slabs
        for slab in range(slabs):
            for out, (row, count) in zip(outs, pieces):
                count = count // RADIX
                for part in range(2):
                    first = (1 - part) * inner + slab * per + row // RADIX
                    for odd in range(2):
                        out[slab, 0, part, pl.ds(2 * pair + odd, count, RADIX), :] = both[
                            first : first + count, odd * 128 : odd * 128 + 128
                        ]
        return carry

    lax.fori_loop(0, RADIX // 2, wave_back, 0)


def inverse_kernel(count, *refs):
    blocks = refs[:count]
    ring = blocks if count > 1 else None
    table, twist, twist_ring, out, held, turned = refs[count:]
    rows, length = out.shape
    inner = length // RADIX

    def group(g, carry):
        at = pl.ds(pl.multiple_of(g * 16, 16), 16)
        for half in range(inner // 128):
            sign, turn = 1, twist
            if ring is not None:
                tile = ring[half * RADIX : half * RADIX + RADIX]
                values = [(tile[n][0, 0, at, :], tile[n][0, 1, at, :]) for n in range(RADIX)]
                sign, turn = -1, twist_ring
            else:
                block = blocks[0]
                values = [(block[n, half, 0, at, :], block[n, half, 1, at, :]) for n in range(RADIX)]
            for k, value in enumerate(sixteen(values, sign)):
                real, imag = twisted(value, turn, k, half * 128, 1)
                store_split(held, k, g, half * 128, imag, real)
        return carry

    lax.fori_loop(0, rows // 16, group, 0)

    def wave(pair, carry):
        both = product(table, held, pair, inner)
        for odd in range(2):
            turned[pl.ds(2 * pair + odd, inner, RADIX), :] = both[:, odd * 128 : odd * 128 + 128]
        return carry

    lax.fori_loop(0, RADIX // 2, wave, 0)
    scale = 1.0 / (NX * NZ)

    def turn(b, carry):
        cols = pl.ds(pl.multiple_of(b * 256, 256), 256)
        out[:, cols] = turned[cols, :].T[:rows] * scale
        return carry

    lax.fori_loop(0, length // 256, turn, 0)


def whole_spec(array):
    zeros = (0,) * array.ndim
    return pl.BlockSpec(array.shape, lambda *_: zeros)


PARAMS = pltpu.CompilerParams(vmem_limit_bytes=67043328)
SCALARS = pl.BlockSpec(memory_space=pltpu.SMEM)


def is_light(distance, count):
    return min(distance, count - distance) * 3 <= count


def ringed(blocks):
    count = lax.axis_size("slab")
    moved = [blocks[0]]
    for n in range(1, count):
        pairs = [(source, (source + n) % count) for source in range(count)]
        moved.append(lax.ppermute(blocks[n], "slab", pairs))
    return moved


def after_first(arrived, then):
    count = len(arrived)
    first = [n for n in range(1, count) if not is_light(n, count)]
    held = lax.optimization_barrier((tuple(arrived[n] for n in first), *then))
    arrived = list(arrived)
    for n, value in zip(first, held[0]):
        arrived[n] = value
    return (arrived, *held[1:])


def tick_kernel(before, after):
    for n in range(before.shape[0]):
        after[n] = before[n]


def ticked(scalars):
    return pl.pallas_call(
        tick_kernel,
        out_shape=jax.ShapeDtypeStruct(scalars.shape, scalars.dtype),
        in_specs=[SCALARS],
        out_specs=SCALARS,
    )(scalars)


def exchanged(value):
    return lax.all_to_all(value, "slab", split_axis=0, concat_axis=0, tiled=True)


def local(velocity, kernel, history, impedance, prestress, strength, fault_state):
    slabs = lax.axis_size("slab")
    rows_dev, length = prestress.shape
    inner = length // RADIX
    chunk_rows = rows_dev // CHUNKS
    halves = rows_dev // 128
    if slabs != RADIX or rows_dev != inner or chunk_rows != 128:
        return local_general(
            velocity, kernel, history, impedance, prestress, strength, fault_state
        )
    lags = history.shape[1]
    table_np, twist_np = constant_tables()
    table, twist = jnp.asarray(table_np), jnp.asarray(twist_np)
    is_first = lax.axis_index("side") == 0
    eta_first, eta_second = impedance[0], impedance[1]
    eta_total = eta_first + eta_second
    weight_first, weight_second = eta_second / eta_total, eta_first / eta_total
    scalars = jnp.stack(
        [
            jnp.where(is_first, weight_first, weight_second),
            jnp.where(is_first, weight_second, weight_first),
            eta_first * eta_second / eta_total,
            jnp.where(is_first, eta_first, eta_second),
            jnp.where(is_first, 1.0, -1.0).astype(f32),
        ]
    )

    def tiles(counts, rows=128):
        return [jax.ShapeDtypeStruct((slabs, count, 2, rows, 128), f32) for count in counts]

    def ring_tiles(count):
        return [jax.ShapeDtypeStruct((count, 2, 128, 128), f32)] * slabs

    def forward_shapes(chunk, ring):
        shapes = ring_tiles(1) + tiles([1])
        if chunk == 0:
            shapes = ring_tiles(halves) if ring else tiles([halves])
        return shapes, [whole_spec(shape) for shape in shapes]

    me = lax.axis_index("slab")
    place = jnp.reshape(me, (1,)).astype(jnp.int32)
    spread = pltpu.VMEM((2 * inner, 2 * 128), f32)
    held = pltpu.VMEM((RADIX // 2, 256, 4 * inner), bf16)
    rows_shape = jax.ShapeDtypeStruct((chunk_rows, length), f32)
    rows_spec = pl.BlockSpec((chunk_rows, length), lambda *_: (0, 0))

    def chunk_spec(chunk):
        return pl.BlockSpec((chunk_rows, length), lambda *_: (chunk, 0))

    def start(chunk):
        shapes, specs = forward_shapes(chunk, chunk == 0)
        return pl.pallas_call(
            start_kernel,
            out_shape=shapes,
            grid=(1,),
            in_specs=[
                SCALARS,
                pl.BlockSpec((1, chunk_rows, length), lambda *_: (0, chunk, 0)),
                whole_spec(table),
                whole_spec(twist),
            ],
            out_specs=specs,
            scratch_shapes=[held, spread],
            compiler_params=PARAMS,
        )(place, velocity, table, twist)

    def middle(scalars, chunk, own, other, state):
        shapes, specs = forward_shapes(chunk, False)
        *sent, state_new = pl.pallas_call(
            middle_kernel,
            out_shape=shapes + [rows_shape],
            grid=(1,),
            in_specs=[
                SCALARS,
                SCALARS,
                rows_spec,
                rows_spec,
                chunk_spec(chunk),
                chunk_spec(chunk),
                chunk_spec(chunk),
                whole_spec(table),
                whole_spec(twist),
            ],
            out_specs=specs + [rows_spec],
            scratch_shapes=[held, spread, pltpu.VMEM((chunk_rows, length), f32)],
            compiler_params=PARAMS,
        )(place, scalars, own, other, prestress, strength, state, table, twist)
        return sent, state_new

    def end(scalars, row, own, other, state, before):
        full = jax.ShapeDtypeStruct((rows_dev, length), f32)
        step = 16
        parts = own.shape[0] // step
        base = row // step
        ahead = row % chunk_rows // step
        moving = pl.BlockSpec((step, length), lambda g: (base + g, 0))
        near = pl.BlockSpec((step, length), lambda g: (g, 0))
        held_state = pl.BlockSpec((step, length), lambda g: (ahead + g, 0))
        moving_speed = pl.BlockSpec((1, step, length), lambda g: (0, base + g, 0))
        kept = [pl.BlockSpec(memory_space=pl.ANY)] * len(before)
        return pl.pallas_call(
            end_kernel,
            out_shape=(jax.ShapeDtypeStruct((1, rows_dev, length), f32), full, full),
            grid=(parts,),
            in_specs=[SCALARS, near, near, moving, moving, held_state] + kept,
            out_specs=(moving_speed, moving, moving),
            input_output_aliases={6 + n: n for n in range(len(before))},
            compiler_params=PARAMS,
        )(scalars, own, other, prestress, strength, state, *before)

    def past_sums():
        step = 32
        total = jax.ShapeDtypeStruct((2, rows_dev, length), f32)
        spec = pl.BlockSpec((2, step, length), lambda g: (0, g, 0))
        return pl.pallas_call(
            history_kernel,
            out_shape=(total, total),
            grid=(rows_dev // step,),
            in_specs=[
                pl.BlockSpec((1, lags + 1, step, length), lambda g: (0, 0, g, 0)),
                pl.BlockSpec((1, lags, 2, step, length), lambda g: (0, 0, 0, g, 0)),
            ],
            out_specs=(spec, spec),
            compiler_params=PARAMS,
        )(kernel, history)

    def spectral(half, ring, near, past_sum, past, pieces, before):
        def block(array):
            place = half if array.shape[1] == halves else 0
            shape = (slabs, 1, 2, array.shape[3], 128)
            return pl.BlockSpec(shape, lambda *_: (0, place, 0, 0, 0))

        lag_spec = [
            pl.BlockSpec((1, 1, 128, length), functools.partial(lambda lag, *_: (0, lag, half, 0), lag))
            for lag in range(2)
        ]
        sum_spec = pl.BlockSpec((2, 128, length), lambda *_: (0, half, 0))
        spec_spec = pl.BlockSpec((2, 128, length), lambda *_: (0, 0, 0))

        def arrived(tile):
            if len(tile) == 1:
                return [block(tile[0])]
            spot = half if tile[0].shape[0] == halves else 0
            return [pl.BlockSpec((1, 2, 128, 128), lambda *_: (spot, 0, 0, 0))] * slabs

        operands = [place, *ring, *near, kernel, past_sum, table, twist, twist_ring]
        in_specs = [SCALARS] + arrived(ring) + arrived(near) + [lag_spec[0], sum_spec]
        in_specs += [whole_spec(table), whole_spec(twist), whole_spec(twist_ring)]
        out_shape = []
        for row, count in pieces[1:]:
            out_shape += tiles([halves], count)
        out_specs = [block(shape) for shape in out_shape]
        shapes = ring_tiles(1)
        out_shape = shapes + out_shape
        out_specs = [whole_spec(shape) for shape in shapes] + out_specs
        if past is not None:
            operands += [kernel, past]
            in_specs += [lag_spec[1], spec_spec]
        else:
            out_shape.append(jax.ShapeDtypeStruct((2, 128, length), bf16))
            out_specs.append(spec_spec)
        aliases = {}
        if before is not None:
            aliases = {len(operands) + n: slabs + n for n in range(len(before))}
            operands += before
            in_specs += [pl.BlockSpec(memory_space=pl.ANY)] * len(before)
        return pl.pallas_call(
            functools.partial(
                spectral_kernel, (len(ring), len(near)), past is not None, half, pieces
            ),
            input_output_aliases=aliases,
            out_shape=out_shape,
            grid=(1,),
            in_specs=in_specs,
            out_specs=out_specs,
            scratch_shapes=[
                held,
                pltpu.VMEM((2, length, 128), f32),
                pltpu.VMEM((2, 128, length), f32),
                spread,
            ],
            compiler_params=PARAMS,
        )(*operands)

    def inverse(*blocks):
        rows = blocks[0].shape[-2]
        return pl.pallas_call(
            functools.partial(inverse_kernel, len(blocks)),
            out_shape=jax.ShapeDtypeStruct((rows, length), f32),
            grid=(1,),
            in_specs=[whole_spec(b) for b in (*blocks, table, twist, twist_ring)],
            out_specs=pl.BlockSpec((rows, length), lambda *_: (0, 0)),
            scratch_shapes=[held, pltpu.VMEM((length, 128), f32)],
            compiler_params=PARAMS,
        )(*blocks, table, twist, twist_ring)

    hold = lax.optimization_barrier
    states = [fault_state] * CHUNKS
    past = [None] * halves
    sums, waiting = None, None
    whole, cut = chunk_rows, LAST_CUT
    sent = [start(0), None]
    for step_index in range(STEPS):
        last = step_index == STEPS - 1
        pieces = [(0, whole), (whole, cut), (whole + cut, whole - cut)]
        if not last:
            pieces = [(0, whole), (whole, whole)]
        ring = ringed(sent[0]) if step_index == 0 else [exchanged(sent[0][0])]
        if step_index == 0:
            sent[1] = start(1)
            sent[1], shift = hold((tuple(sent[1]), me))
            turn = lax.broadcasted_iota(jnp.int32, (RADIX, inner), 0) * (
                lax.broadcasted_iota(jnp.int32, (RADIX, inner), 1) + inner * shift
            )
            turn = (turn % length).astype(f32) * (2.0 * math.pi / length)
            twist_ring = jnp.stack([jnp.cos(turn), jnp.sin(turn)])
        else:
            own = inverse(waiting)
            sent[1], states[1] = middle(scalars, 1, own, swapped(own, "side", 0), states[1])
        near = ringed(sent[1][:slabs])
        if step_index == 0:
            sums = past_sums()
        else:
            scalars = ticked(scalars)
        near, far, sums = after_first(near, (sent[1][slabs], sums))
        far = exchanged(far)
        outs = spectral(0, ring, near, sums[step_index], past[0], pieces, None)
        if step_index == 0:
            past[0] = outs[-1]
        late = outs[slabs : slabs + len(pieces) - 1]
        back = ringed(outs[:slabs])
        far, late = hold((far, list(late)))
        outs = spectral(1, ring, [far], sums[step_index], past[1], pieces, late)
        if step_index == 0:
            past[1] = outs[-1]
        late = outs[slabs : slabs + len(pieces) - 1]
        more = ringed(outs[:slabs])
        scalars = ticked(scalars)
        more, late = after_first(more, (list(late),))
        waiting = exchanged(late[0])
        own = inverse(*back, *more)
        other = swapped(own, "side", 0)
        if not last:
            sent[0], states[0] = middle(scalars, 0, own, other, states[0])
        if not last:
            waiting, sent[0], states[0] = hold((waiting, sent[0], states[0]))
            continue
        waiting, own, other, final = hold((waiting, own, other, late[1]))
        final = exchanged(final)
        own_near = inverse(waiting)
        other_near = swapped(own_near, "side", 0)
        results = end(scalars, 0, own, other, states[0], ())
        final, own_near, results = hold((final, own_near, tuple(results)))
        own = inverse(final)
        other = swapped(own, "side", 0)
        results = end(scalars, whole, own_near, other_near, states[1], results)
        results = end(scalars, whole + cut, own, other, states[1], results)
    return tuple(results)


def solution(mesh):
    placed = (
        P("side", "slab", None),
        P("side", None, "slab", None),
        P("side", None, None, "slab", None),
        P(),
        P("slab", None),
        P("slab", None),
        P("slab", None),
    )
    return jax.shard_map(
        local,
        mesh=mesh,
        in_specs=placed,
        out_specs=(P("side", "slab", None), P("slab", None), P("slab", None)),
        check_vma=False,
    )
```

```python
import functools
import math

import jax
import jax.numpy as jnp
import numpy as np
from jax import lax
from jax.experimental import pallas as pl
from jax.experimental.pallas import tpu as pltpu
from jax.sharding import PartitionSpec as P


NX = 4096
NZ = 4096
NEWTON = 4
STEPS = 2


highest = lax.Precision.HIGHEST


def swapped(value, axis, distance):
    mask = 2**distance
    pairs = [(source, source ^ mask) for source in range(lax.axis_size(axis))]
    return lax.ppermute(value, axis, pairs)


def inverse_sinh(value):
    magnitude = jnp.abs(value)
    result = jnp.log1p(
        magnitude + magnitude * magnitude / (1.0 + jnp.sqrt(1.0 + magnitude * magnitude))
    )
    return jnp.where(value < 0.0, -result, result)


def angle_table(rows_count, cols_count, period, sign):
    first = lax.broadcasted_iota(jnp.int32, (rows_count, cols_count), 0)
    second = lax.broadcasted_iota(jnp.int32, (rows_count, cols_count), 1)
    phase = (first * second % period).astype(jnp.float32) * (2.0 * math.pi / period)
    return (jnp.cos(phase), sign * jnp.sin(phase))


def transform_last(real_part, imag_part, sign, real_only):
    length = real_part.shape[-1]
    inner = min(length, 256)
    outer = length // inner
    leading = real_part.shape[:-1]
    cos_outer, sin_outer = angle_table(outer, outer, outer, sign)
    cos_twist, sin_twist = angle_table(outer, inner, length, sign)
    cos_inner, sin_inner = angle_table(inner, inner, inner, sign)
    shaped_real = real_part.reshape(leading + (outer, inner))
    step_real = jnp.einsum("kn,...nq->...kq", cos_outer, shaped_real, precision=highest)
    step_imag = jnp.einsum("kn,...nq->...kq", sin_outer, shaped_real, precision=highest)
    if imag_part is not None:
        shaped_imag = imag_part.reshape(leading + (outer, inner))
        step_real = step_real - jnp.einsum(
            "kn,...nq->...kq", sin_outer, shaped_imag, precision=highest
        )
        step_imag = step_imag + jnp.einsum(
            "kn,...nq->...kq", cos_outer, shaped_imag, precision=highest
        )
    twist_real = step_real * cos_twist - step_imag * sin_twist
    twist_imag = step_real * sin_twist + step_imag * cos_twist
    out_real = jnp.matmul(twist_real, cos_inner, precision=highest) - jnp.matmul(
        twist_imag, sin_inner, precision=highest
    )
    result_real = jnp.swapaxes(out_real, -1, -2).reshape(leading + (length,))
    if real_only:
        return (result_real, None)
    out_imag = jnp.matmul(twist_real, sin_inner, precision=highest) + jnp.matmul(
        twist_imag, cos_inner, precision=highest
    )
    result_imag = jnp.swapaxes(out_imag, -1, -2).reshape(leading + (length,))
    return (result_real, result_imag)


def to_spectrum(rows_field):
    slab_count = lax.axis_size("slab")
    z_real, z_imag = transform_last(rows_field, None, -1.0, False)
    stacked = jnp.stack([z_real, z_imag])
    rows_dev = stacked.shape[1]
    length_z = stacked.shape[2]
    moved = jnp.transpose(stacked, (0, 2, 1)).reshape(
        2, slab_count, length_z // slab_count, rows_dev
    )
    block = lax.all_to_all(moved, "slab", split_axis=1, concat_axis=3, tiled=True)
    spec_real, spec_imag = transform_last(block[0, 0], block[1, 0], -1.0, False)
    return jnp.stack([spec_real, spec_imag]).astype(jnp.bfloat16)


def to_rows(spec_real, spec_imag):
    slab_count = lax.axis_size("slab")
    x_real, x_imag = transform_last(spec_real, spec_imag, 1.0, False)
    stacked = jnp.stack([x_real, x_imag], axis=1)
    batch = stacked.shape[0]
    kz_dev = stacked.shape[2]
    length_x = stacked.shape[3]
    moved = stacked.reshape(batch, 2, kz_dev, slab_count, length_x // slab_count)
    scale = 1.0 / (NX * NZ)
    turned = jnp.swapaxes(
        lax.all_to_all(moved, "slab", split_axis=3, concat_axis=2, tiled=True)[:, :, :, 0, :], 2, 3
    )
    field_real, _ = transform_last(turned[:, 0], turned[:, 1], 1.0, True)
    return field_real * scale


def local_general(velocity, kernel, history, impedance, prestress, strength, fault_state):
    side_index = lax.axis_index("side")
    is_first = side_index == 0
    eta_first = impedance[0]
    eta_second = impedance[1]
    eta_total = eta_first + eta_second
    weight_first = eta_second / eta_total
    weight_second = eta_first / eta_total
    eta_joint = eta_first * eta_second / eta_total
    own_eta = jnp.where(is_first, eta_first, eta_second)
    own_sign = jnp.where(is_first, 1.0, -1.0).astype(jnp.float32)
    lag_kernel = kernel[0]
    lag_history = history[0]
    kernel_now = lag_kernel[0].astype(jnp.float32)
    speed = velocity[0]
    state_now = fault_state
    rate = jnp.zeros_like(prestress)
    for _ in range(STEPS):
        spec_now = to_spectrum(speed)
        total = kernel_now * spec_now.astype(jnp.float32) + jnp.einsum(
            "lzx,lczx->czx", lag_kernel[1:], lag_history, preferred_element_type=jnp.float32
        )
        force_now = to_rows(total[0][None], total[1][None])[0]
        force_other = swapped(force_now, "side", 0)
        force_first = jnp.where(is_first, force_now, force_other)
        force_second = jnp.where(is_first, force_other, force_now)
        coupled = weight_first * force_first + weight_second * force_second
        locked = prestress + coupled
        friction_rate = locked / (eta_joint + strength)
        factor = 0.5 * jnp.exp(state_now)
        for _ in range(NEWTON):
            scaled = factor * friction_rate
            misfit = strength * inverse_sinh(scaled) + eta_joint * friction_rate - locked
            slope = strength * factor / jnp.sqrt(1.0 + scaled * scaled) + eta_joint
            friction_rate = friction_rate - 0.5 * misfit / slope
        stress = locked - eta_joint * friction_rate
        speed_new = own_sign * (prestress + force_now - stress) / own_eta
        state_new = state_now + 0.25 * (jnp.exp(-state_now) - jnp.abs(friction_rate))
        speed = speed_new
        rate = friction_rate
        state_now = state_new
        lag_history = jnp.concatenate([spec_now[None], lag_history[:-1]], axis=0)
    return (speed[None], rate, state_now)


RADIX = 16
CHUNKS = 2
LAST_CUT = 80
f32 = jnp.float32
bf16 = jnp.bfloat16


def constant_tables():
    inner = NX // RADIX
    grid = np.outer(np.arange(inner), np.arange(inner)) % inner
    phase = grid * (2.0 * np.pi / inner)
    cos, sin = np.cos(phase), np.sin(phase)
    full = np.concatenate(
        [np.concatenate([cos, sin], 1), np.concatenate([-sin, cos], 1)], 0
    ).astype(np.float32)
    high = full.astype(jnp.bfloat16)
    low = (full - high.astype(np.float32)).astype(jnp.bfloat16)
    table = np.concatenate([high, high, low], 1)
    turn = np.outer(np.arange(RADIX), np.arange(inner)) * (2.0 * np.pi / NX)
    twist = np.stack([np.cos(turn), np.sin(turn)]).astype(np.float32)
    return table, twist


def plus(a, b):
    return tuple(
        (p if q is None else q if p is None else p + q) for p, q in zip(a, b)
    )


def minus(a, b):
    return tuple(
        (p if q is None else -q if p is None else p - q) for p, q in zip(a, b)
    )


def times_i(a, sign):
    real, imag = a
    if sign > 0:
        return (None if imag is None else -imag, real)
    return (imag, None if real is None else -real)


def turned_by(a, cos, sin):
    real, imag = a
    if imag is None:
        return (real * cos, real * sin)
    if real is None:
        return (-(imag * sin), imag * cos)
    return (real * cos - imag * sin, real * sin + imag * cos)


def four(x, sign):
    a, b = plus(x[0], x[2]), minus(x[0], x[2])
    c, d = plus(x[1], x[3]), times_i(minus(x[1], x[3]), sign)
    return [plus(a, c), plus(b, d), minus(a, c), minus(b, d)]


def sixteen(x, sign):
    rows = [four([x[4 * m + n] for m in range(4)], sign) for n in range(4)]
    out = [None] * 16
    for k in range(4):
        terms = []
        for n in range(4):
            power = n * k
            term = rows[n][k]
            if power == 4:
                term = times_i(term, sign)
            elif power:
                angle = 2.0 * math.pi * power / 16
                term = turned_by(term, math.cos(angle), sign * math.sin(angle))
            terms.append(term)
        for m, value in enumerate(four(terms, sign)):
            out[k + 4 * m] = value
    return out


def store_split(held, k, group, lane, first, second):
    inner = NX // RADIX
    rows = pl.ds(pl.multiple_of(group * 16 + (k % 2) * 128, 16), 16)
    for place, value in ((0, first), (1, second)):
        high = value.astype(bf16)
        low = (value - high.astype(f32)).astype(bf16)
        held[k // 2, rows, pl.ds(place * inner + lane, 128)] = high
        held[k // 2, rows, pl.ds((2 + place) * inner + lane, 128)] = low


def twisted(value, twist, k, lane, sign):
    if k == 0:
        real, imag = value
        return (real, jnp.zeros_like(real) if imag is None else imag)
    cos = twist[0, k : k + 1, pl.ds(lane, 128)]
    sin = twist[1, k : k + 1, pl.ds(lane, 128)]
    return turned_by(value, cos, sin if sign > 0 else -sin)


def product(table, held, k, start):
    wide = table.shape[1] // 3
    rows = pl.ds(start, table.shape[0] - start)
    dims = (((1,), (1,)), ((), ()))
    return lax.dot_general(
        table[rows, : 2 * wide], held[k], dims, preferred_element_type=f32
    ) + lax.dot_general(
        table[rows, 2 * wide :], held[k, :, :wide], dims, preferred_element_type=f32
    )


def store_ring(place, spread, both, outs, pair, lead, first_part, row):
    inner = both.shape[0] // 2
    per = inner // RADIX
    spread[...] = both
    for n in range(RADIX):
        target = lax.rem(place[0] + n, RADIX)
        for part in range(2):
            base = (part if first_part == 0 else 1 - part) * inner
            rows = pl.ds(pl.multiple_of(base + target * per + row, 8), 8)
            for odd in range(2):
                outs[n][lead, part, pl.ds(2 * pair + odd, 8, RADIX), :] = spread[
                    rows, odd * 128 : odd * 128 + 128
                ]


def forward_rows(rows_ref, table, twist, place, outs, held, spread):
    rows, length = rows_ref.shape
    inner = length // RADIX

    def group(g, carry):
        at = pl.ds(pl.multiple_of(g * 16, 16), 16)
        for lane in range(0, inner, 128):
            values = [(rows_ref[at, pl.ds(n * inner + lane, 128)], None) for n in range(RADIX)]
            for k, value in enumerate(sixteen(values, -1)):
                store_split(held, k, g, lane, *twisted(value, twist, k, lane, -1))
        return carry

    lax.fori_loop(0, rows // 16, group, 0)

    def wave(pair, carry):
        both = product(table, held, pair, 0)
        if len(outs) >= RADIX:
            for half in range(outs[0].shape[0]):
                store_ring(place, spread, both, outs[:RADIX], pair, half, 0, half * 8)
            if len(outs) == RADIX:
                return carry
        slabs, halves = outs[-1].shape[0], 2
        per = inner // slabs // halves
        for slab in range(slabs):
            for half in range(halves - outs[-1].shape[1], halves):
                out, spot = outs[-1], half - halves + outs[-1].shape[1]
                for part in range(2):
                    first = part * inner + (slab * halves + half) * per
                    for odd in range(2):
                        out[slab, spot, part, pl.ds(2 * pair + odd, per, RADIX), :] = both[
                            first : first + per, odd * 128 : odd * 128 + 128
                        ]
        return carry

    lax.fori_loop(0, RADIX // 2, wave, 0)


def start_kernel(place, velocity, table, twist, *refs):
    forward_rows(velocity.at[0], table, twist, place, refs[:-2], *refs[-2:])


def friction(scalars, own, other, prestress, strength, state):
    weight_own, weight_other, joint, eta, sign = [scalars[n] for n in range(5)]
    locked = prestress + (weight_own * own + weight_other * other)
    rate = locked / (joint + strength)
    factor = 0.5 * jnp.exp(state)
    for _ in range(NEWTON):
        scaled = factor * rate
        wide = 1.0 + scaled * scaled
        narrow = lax.rsqrt(wide)
        bent = jnp.log(jnp.abs(scaled) + wide * narrow)
        bent = jnp.where(scaled < 0.0, -bent, bent)
        misfit = strength * bent + joint * rate - locked
        slope = strength * factor * narrow + joint
        rate = rate - 0.5 * misfit / slope
    stress = locked - joint * rate
    speed = (sign / eta) * (prestress + own - stress)
    state_new = state + 0.25 * (jnp.exp(-state) - jnp.abs(rate))
    return speed, rate, state_new


def middle_kernel(place, scalars, own, other, prestress, strength, state, table, twist, *refs):
    outs = refs[:-4]
    state_out, held, spread, speed_held = refs[-4:]

    def group(g, carry):
        at = pl.ds(pl.multiple_of(g * 8, 8), 8)
        for lane in range(0, own.shape[1], 1024):
            cols = pl.ds(lane, 1024)
            speed, _, state_new = friction(
                scalars,
                own[at, cols],
                other[at, cols],
                prestress[at, cols],
                strength[at, cols],
                state[at, cols],
            )
            speed_held[at, cols] = speed
            state_out[at, cols] = state_new
        return carry

    lax.fori_loop(0, own.shape[0] // 8, group, 0)
    forward_rows(speed_held, table, twist, place, outs, held, spread)


def end_kernel(scalars, own, other, prestress, strength, state, *refs):
    speed_out, rate_out, state_out = refs[-3:]

    def group(g, carry):
        at = pl.ds(pl.multiple_of(g * 8, 8), 8)
        for lane in range(0, own.shape[1], 1024):
            cols = pl.ds(lane, 1024)
            speed, rate, state_new = friction(
                scalars,
                own[at, cols],
                other[at, cols],
                prestress[at, cols],
                strength[at, cols],
                state[at, cols],
            )
            speed_out[0, at, cols] = speed
            rate_out[at, cols] = rate
            state_out[at, cols] = state_new
        return carry

    lax.fori_loop(0, own.shape[0] // 8, group, 0)


def history_kernel(kernel, history, now, later):
    def group(g, carry):
        cols = pl.ds(pl.multiple_of(g * 256, 256), 256)
        lags = [kernel[0, n, :, cols].astype(f32) for n in range(kernel.shape[1])]
        for part in range(2):
            total_now = total_later = 0.0
            for n in range(history.shape[1]):
                past = history[0, n, part, :, cols].astype(f32)
                total_now = total_now + lags[n + 1] * past
                if n + 2 < len(lags):
                    total_later = total_later + lags[n + 2] * past
            now[part, :, cols] = total_now
            later[part, :, cols] = total_later
        return carry

    lax.fori_loop(0, now.shape[2] // 256, group, 0)


def spectral_kernel(counts, has_past, half, pieces, *refs):
    count = 1 + sum(counts)
    place, arrived = refs[0], (refs[1 : 1 + counts[0]], refs[1 + counts[0] : count])
    kernel_now, past_sum, table, twist, twist_ring = refs[count : count + 5]
    rest = list(refs[count + 5 :])
    if has_past:
        kernel_past, spec_past = rest.pop(0), rest.pop(0)
        spec_out = None
    if half > 0:
        rest = rest[len(pieces) - 1 :]
    ring_out, rest = rest[:RADIX], rest[RADIX:]
    pieces = pieces[1:]
    outs, rest = rest[: len(pieces)], rest[len(pieces) :]
    if not has_past:
        spec_out = rest.pop(0)
    held, turned, total, spread = rest
    rows = 128
    inner = RADIX * 16
    length = total.shape[2]

    def group(g, carry):
        at = pl.ds(pl.multiple_of(g * 16, 16), 16)
        for chunk, tile in enumerate(arrived):
            if len(tile) == 1:
                values = [(tile[0][n, 0, 0, at, :], tile[0][n, 0, 1, at, :]) for n in range(RADIX)]
                sign, turn = -1, twist
            else:
                values = [(tile[n][0, 0, at, :], tile[n][0, 1, at, :]) for n in range(RADIX)]
                sign, turn = 1, twist_ring
            lane = chunk * 128
            for k, value in enumerate(sixteen(values, sign)):
                store_split(held, k, g, lane, *twisted(value, turn, k, lane, -1))
        return carry

    lax.fori_loop(0, rows // 16, group, 0)

    def wave(pair, carry):
        both = product(table, held, pair, 0)
        for odd in range(2):
            for part in range(2):
                turned[part, pl.ds(2 * pair + odd, inner, RADIX), :] = both[
                    part * inner : part * inner + inner, odd * 128 : odd * 128 + 128
                ]
        return carry

    lax.fori_loop(0, RADIX // 2, wave, 0)

    def convolve(b, carry):
        cols = pl.ds(pl.multiple_of(b * 256, 256), 256)
        weight = kernel_now[0, 0, :, cols].astype(f32)
        for part in range(2):
            spec = turned[part, cols, :].T.astype(bf16)
            value = weight * spec.astype(f32) + past_sum[part, :, cols]
            if has_past:
                value = value + kernel_past[0, 0, :, cols].astype(f32) * spec_past[
                    part, :, cols
                ].astype(f32)
            else:
                spec_out[part, :, cols] = spec
            total[part, :, cols] = value
        return carry

    lax.fori_loop(0, length // 256, convolve, 0)

    def group_back(g, carry):
        at = pl.ds(pl.multiple_of(g * 16, 16), 16)
        for lane in range(0, inner, 128):
            values = [
                (total[0, at, pl.ds(n * inner + lane, 128)], total[1, at, pl.ds(n * inner + lane, 128)])
                for n in range(RADIX)
            ]
            for k, value in enumerate(sixteen(values, 1)):
                real, imag = twisted(value, twist, k, lane, 1)
                store_split(held, k, g, lane, imag, real)
        return carry

    lax.fori_loop(0, rows // 16, group_back, 0)

    def wave_back(pair, carry):
        both = product(table, held, pair, 0)
        store_ring(place, spread, both, ring_out, pair, 0, 1, 0)
        slabs = outs[0].shape[0]
        per = inner // slabs
        for slab in range(slabs):
            for out, (row, count) in zip(outs, pieces):
                count = count // RADIX
                for part in range(2):
                    first = (1 - part) * inner + slab * per + row // RADIX
                    for odd in range(2):
                        out[slab, 0, part, pl.ds(2 * pair + odd, count, RADIX), :] = both[
                            first : first + count, odd * 128 : odd * 128 + 128
                        ]
        return carry

    lax.fori_loop(0, RADIX // 2, wave_back, 0)


def inverse_kernel(count, *refs):
    blocks = refs[:count]
    ring = blocks if count > 1 else None
    table, twist, twist_ring, out, held, turned = refs[count:]
    rows, length = out.shape
    inner = length // RADIX

    def group(g, carry):
        at = pl.ds(pl.multiple_of(g * 16, 16), 16)
        for half in range(inner // 128):
            sign, turn = 1, twist
            if ring is not None:
                tile = ring[half * RADIX : half * RADIX + RADIX]
                values = [(tile[n][0, 0, at, :], tile[n][0, 1, at, :]) for n in range(RADIX)]
                sign, turn = -1, twist_ring
            else:
                block = blocks[0]
                values = [(block[n, half, 0, at, :], block[n, half, 1, at, :]) for n in range(RADIX)]
            for k, value in enumerate(sixteen(values, sign)):
                real, imag = twisted(value, turn, k, half * 128, 1)
                store_split(held, k, g, half * 128, imag, real)
        return carry

    lax.fori_loop(0, rows // 16, group, 0)

    def wave(pair, carry):
        both = product(table, held, pair, inner)
        for odd in range(2):
            turned[pl.ds(2 * pair + odd, inner, RADIX), :] = both[:, odd * 128 : odd * 128 + 128]
        return carry

    lax.fori_loop(0, RADIX // 2, wave, 0)
    scale = 1.0 / (NX * NZ)

    def turn(b, carry):
        cols = pl.ds(pl.multiple_of(b * 256, 256), 256)
        out[:, cols] = turned[cols, :].T[:rows] * scale
        return carry

    lax.fori_loop(0, length // 256, turn, 0)


def whole_spec(array):
    zeros = (0,) * array.ndim
    return pl.BlockSpec(array.shape, lambda *_: zeros)


PARAMS = pltpu.CompilerParams(vmem_limit_bytes=67043328)
SCALARS = pl.BlockSpec(memory_space=pltpu.SMEM)


def is_light(distance, count):
    return min(distance, count - distance) * 3 <= count


def ringed(blocks, which=(False, True)):
    count = lax.axis_size("slab")
    moved = list(blocks)
    for n in range(1, count):
        if is_light(n, count) not in which:
            continue
        pairs = [(source, (source + n) % count) for source in range(count)]
        moved[n] = lax.ppermute(blocks[n], "slab", pairs)
    return moved


def after_first(arrived, then):
    count = len(arrived)
    first = [n for n in range(1, count) if not is_light(n, count)]
    held = lax.optimization_barrier((tuple(arrived[n] for n in first), *then))
    arrived = list(arrived)
    for n, value in zip(first, held[0]):
        arrived[n] = value
    return (arrived, *held[1:])


def tick_kernel(before, after):
    for n in range(before.shape[0]):
        after[n] = before[n]


def ticked(scalars):
    return pl.pallas_call(
        tick_kernel,
        out_shape=jax.ShapeDtypeStruct(scalars.shape, scalars.dtype),
        in_specs=[SCALARS],
        out_specs=SCALARS,
    )(scalars)


def exchanged(value):
    return lax.all_to_all(value, "slab", split_axis=0, concat_axis=0, tiled=True)


def local(velocity, kernel, history, impedance, prestress, strength, fault_state):
    slabs = lax.axis_size("slab")
    rows_dev, length = prestress.shape
    inner = length // RADIX
    chunk_rows = rows_dev // CHUNKS
    halves = rows_dev // 128
    if slabs != RADIX or rows_dev != inner or chunk_rows != 128:
        return local_general(
            velocity, kernel, history, impedance, prestress, strength, fault_state
        )
    lags = history.shape[1]
    table_np, twist_np = constant_tables()
    table, twist = jnp.asarray(table_np), jnp.asarray(twist_np)
    is_first = lax.axis_index("side") == 0
    eta_first, eta_second = impedance[0], impedance[1]
    eta_total = eta_first + eta_second
    weight_first, weight_second = eta_second / eta_total, eta_first / eta_total
    scalars = jnp.stack(
        [
            jnp.where(is_first, weight_first, weight_second),
            jnp.where(is_first, weight_second, weight_first),
            eta_first * eta_second / eta_total,
            jnp.where(is_first, eta_first, eta_second),
            jnp.where(is_first, 1.0, -1.0).astype(f32),
        ]
    )

    def tiles(counts, rows=128):
        return [jax.ShapeDtypeStruct((slabs, count, 2, rows, 128), f32) for count in counts]

    def ring_tiles(count):
        return [jax.ShapeDtypeStruct((count, 2, 128, 128), f32)] * slabs

    def forward_shapes(chunk, ring):
        shapes = ring_tiles(1) + tiles([1])
        if chunk == 0:
            shapes = ring_tiles(halves) if ring else tiles([halves])
        return shapes, [whole_spec(shape) for shape in shapes]

    me = lax.axis_index("slab")
    place = jnp.reshape(me, (1,)).astype(jnp.int32)
    spread = pltpu.VMEM((2 * inner, 2 * 128), f32)
    held = pltpu.VMEM((RADIX // 2, 256, 4 * inner), bf16)
    rows_shape = jax.ShapeDtypeStruct((chunk_rows, length), f32)
    rows_spec = pl.BlockSpec((chunk_rows, length), lambda *_: (0, 0))

    def chunk_spec(chunk):
        return pl.BlockSpec((chunk_rows, length), lambda *_: (chunk, 0))

    def start(chunk):
        shapes, specs = forward_shapes(chunk, chunk == 0)
        return pl.pallas_call(
            start_kernel,
            out_shape=shapes,
            grid=(1,),
            in_specs=[
                SCALARS,
                pl.BlockSpec((1, chunk_rows, length), lambda *_: (0, chunk, 0)),
                whole_spec(table),
                whole_spec(twist),
            ],
            out_specs=specs,
            scratch_shapes=[held, spread],
            compiler_params=PARAMS,
        )(place, velocity, table, twist)

    def middle(scalars, chunk, own, other, state):
        shapes, specs = forward_shapes(chunk, False)
        *sent, state_new = pl.pallas_call(
            middle_kernel,
            out_shape=shapes + [rows_shape],
            grid=(1,),
            in_specs=[
                SCALARS,
                SCALARS,
                rows_spec,
                rows_spec,
                chunk_spec(chunk),
                chunk_spec(chunk),
                chunk_spec(chunk),
                whole_spec(table),
                whole_spec(twist),
            ],
            out_specs=specs + [rows_spec],
            scratch_shapes=[held, spread, pltpu.VMEM((chunk_rows, length), f32)],
            compiler_params=PARAMS,
        )(place, scalars, own, other, prestress, strength, state, table, twist)
        return sent, state_new

    def end(scalars, row, own, other, state, before):
        full = jax.ShapeDtypeStruct((rows_dev, length), f32)
        step = 16
        parts = own.shape[0] // step
        base = row // step
        ahead = row % chunk_rows // step
        moving = pl.BlockSpec((step, length), lambda g: (base + g, 0))
        near = pl.BlockSpec((step, length), lambda g: (g, 0))
        held_state = pl.BlockSpec((step, length), lambda g: (ahead + g, 0))
        moving_speed = pl.BlockSpec((1, step, length), lambda g: (0, base + g, 0))
        kept = [pl.BlockSpec(memory_space=pl.ANY)] * len(before)
        return pl.pallas_call(
            end_kernel,
            out_shape=(jax.ShapeDtypeStruct((1, rows_dev, length), f32), full, full),
            grid=(parts,),
            in_specs=[SCALARS, near, near, moving, moving, held_state] + kept,
            out_specs=(moving_speed, moving, moving),
            input_output_aliases={6 + n: n for n in range(len(before))},
            compiler_params=PARAMS,
        )(scalars, own, other, prestress, strength, state, *before)

    def past_sums():
        step = 32
        total = jax.ShapeDtypeStruct((2, rows_dev, length), f32)
        spec = pl.BlockSpec((2, step, length), lambda g: (0, g, 0))
        return pl.pallas_call(
            history_kernel,
            out_shape=(total, total),
            grid=(rows_dev // step,),
            in_specs=[
                pl.BlockSpec((1, lags + 1, step, length), lambda g: (0, 0, g, 0)),
                pl.BlockSpec((1, lags, 2, step, length), lambda g: (0, 0, 0, g, 0)),
            ],
            out_specs=(spec, spec),
            compiler_params=PARAMS,
        )(kernel, history)

    def spectral(half, ring, near, past_sum, past, pieces, before):
        def block(array):
            place = half if array.shape[1] == halves else 0
            shape = (slabs, 1, 2, array.shape[3], 128)
            return pl.BlockSpec(shape, lambda *_: (0, place, 0, 0, 0))

        lag_spec = [
            pl.BlockSpec((1, 1, 128, length), functools.partial(lambda lag, *_: (0, lag, half, 0), lag))
            for lag in range(2)
        ]
        sum_spec = pl.BlockSpec((2, 128, length), lambda *_: (0, half, 0))
        spec_spec = pl.BlockSpec((2, 128, length), lambda *_: (0, 0, 0))

        def arrived(tile):
            if len(tile) == 1:
                return [block(tile[0])]
            spot = half if tile[0].shape[0] == halves else 0
            return [pl.BlockSpec((1, 2, 128, 128), lambda *_: (spot, 0, 0, 0))] * slabs

        operands = [place, *ring, *near, kernel, past_sum, table, twist, twist_ring]
        in_specs = [SCALARS] + arrived(ring) + arrived(near) + [lag_spec[0], sum_spec]
        in_specs += [whole_spec(table), whole_spec(twist), whole_spec(twist_ring)]
        out_shape = []
        for row, count in pieces[1:]:
            out_shape += tiles([halves], count)
        out_specs = [block(shape) for shape in out_shape]
        shapes = ring_tiles(1)
        out_shape = shapes + out_shape
        out_specs = [whole_spec(shape) for shape in shapes] + out_specs
        if past is not None:
            operands += [kernel, past]
            in_specs += [lag_spec[1], spec_spec]
        else:
            out_shape.append(jax.ShapeDtypeStruct((2, 128, length), bf16))
            out_specs.append(spec_spec)
        aliases = {}
        if before is not None:
            aliases = {len(operands) + n: slabs + n for n in range(len(before))}
            operands += before
            in_specs += [pl.BlockSpec(memory_space=pl.ANY)] * len(before)
        return pl.pallas_call(
            functools.partial(
                spectral_kernel, (len(ring), len(near)), past is not None, half, pieces
            ),
            input_output_aliases=aliases,
            out_shape=out_shape,
            grid=(1,),
            in_specs=in_specs,
            out_specs=out_specs,
            scratch_shapes=[
                held,
                pltpu.VMEM((2, length, 128), f32),
                pltpu.VMEM((2, 128, length), f32),
                spread,
            ],
            compiler_params=PARAMS,
        )(*operands)

    def inverse(*blocks):
        rows = blocks[0].shape[-2]
        return pl.pallas_call(
            functools.partial(inverse_kernel, len(blocks)),
            out_shape=jax.ShapeDtypeStruct((rows, length), f32),
            grid=(1,),
            in_specs=[whole_spec(b) for b in (*blocks, table, twist, twist_ring)],
            out_specs=pl.BlockSpec((rows, length), lambda *_: (0, 0)),
            scratch_shapes=[held, pltpu.VMEM((length, 128), f32)],
            compiler_params=PARAMS,
        )(*blocks, table, twist, twist_ring)

    hold = lax.optimization_barrier
    states = [fault_state] * CHUNKS
    past = [None] * halves
    sums, waiting = None, None
    whole, cut = chunk_rows, LAST_CUT
    sent = [start(0), None]
    for step_index in range(STEPS):
        last = step_index == STEPS - 1
        pieces = [(0, whole), (whole, cut), (whole + cut, whole - cut)]
        if not last:
            pieces = [(0, whole), (whole, whole)]
        ring = ringed(sent[0]) if step_index == 0 else [exchanged(sent[0][0])]
        if step_index == 0:
            sent[1] = start(1)
            sent[1], shift = hold((tuple(sent[1]), me))
            turn = lax.broadcasted_iota(jnp.int32, (RADIX, inner), 0) * (
                lax.broadcasted_iota(jnp.int32, (RADIX, inner), 1) + inner * shift
            )
            turn = (turn % length).astype(f32) * (2.0 * math.pi / length)
            twist_ring = jnp.stack([jnp.cos(turn), jnp.sin(turn)])
        else:
            own = inverse(waiting)
            sent[1], states[1] = middle(scalars, 1, own, swapped(own, "side", 0), states[1])
        near = ringed(sent[1][:slabs])
        if step_index == 0:
            sums = past_sums()
        scalars = ticked(scalars)
        near, far, sums = after_first(near, (sent[1][slabs], sums))
        far = exchanged(far)
        outs = spectral(0, ring, near, sums[step_index], past[0], pieces, None)
        if step_index == 0:
            past[0] = outs[-1]
        late = outs[slabs : slabs + len(pieces) - 1]
        back = ringed(outs[:slabs], (True,))
        long = [n for n in range(1, slabs) if not is_light(n, slabs)]
        far, late, rest = hold((far, list(late), [back[n] for n in long]))
        for n, value in zip(long, rest):
            back[n] = value
        back = ringed(back, (False,))
        outs = spectral(1, ring, [far], sums[step_index], past[1], pieces, late)
        if step_index == 0:
            past[1] = outs[-1]
        late = outs[slabs : slabs + len(pieces) - 1]
        more = ringed(outs[:slabs])
        scalars = ticked(scalars)
        more, late = after_first(more, (list(late),))
        waiting = exchanged(late[0])
        own = inverse(*back, *more)
        other = swapped(own, "side", 0)
        if last:
            scalars = ticked(scalars)
        else:
            sent[0], states[0] = middle(scalars, 0, own, other, states[0])
        if not last:
            waiting, sent[0], states[0] = hold((waiting, sent[0], states[0]))
            continue
        waiting, scalars, final = hold((waiting, scalars, late[1]))
        final = exchanged(final)
        own_near = inverse(waiting)
        other_near = swapped(own_near, "side", 0)
        results = end(scalars, 0, own, other, states[0], ())
        final, own_near, results = hold((final, own_near, tuple(results)))
        own = inverse(final)
        other = swapped(own, "side", 0)
        results = end(scalars, whole, own_near, other_near, states[1], results)
        results = end(scalars, whole + cut, own, other, states[1], results)
    return tuple(results)


def solution(mesh):
    placed = (
        P("side", "slab", None),
        P("side", None, "slab", None),
        P("side", None, None, "slab", None),
        P(),
        P("slab", None),
        P("slab", None),
        P("slab", None),
    )
    return jax.shard_map(
        local,
        mesh=mesh,
        in_specs=placed,
        out_specs=(P("side", "slab", None), P("slab", None), P("slab", None)),
        check_vma=False,
    )
```

```python
import functools
import math

import jax
import jax.numpy as jnp
import numpy as np
from jax import lax
from jax.experimental import pallas as pl
from jax.experimental.pallas import tpu as pltpu
from jax.sharding import PartitionSpec as P


NX = 4096
NZ = 4096
NEWTON = 4
STEPS = 2


highest = lax.Precision.HIGHEST


def swapped(value, axis, distance):
    mask = 2**distance
    pairs = [(source, source ^ mask) for source in range(lax.axis_size(axis))]
    return lax.ppermute(value, axis, pairs)


def inverse_sinh(value):
    magnitude = jnp.abs(value)
    result = jnp.log1p(
        magnitude + magnitude * magnitude / (1.0 + jnp.sqrt(1.0 + magnitude * magnitude))
    )
    return jnp.where(value < 0.0, -result, result)


def angle_table(rows_count, cols_count, period, sign):
    first = lax.broadcasted_iota(jnp.int32, (rows_count, cols_count), 0)
    second = lax.broadcasted_iota(jnp.int32, (rows_count, cols_count), 1)
    phase = (first * second % period).astype(jnp.float32) * (2.0 * math.pi / period)
    return (jnp.cos(phase), sign * jnp.sin(phase))


def transform_last(real_part, imag_part, sign, real_only):
    length = real_part.shape[-1]
    inner = min(length, 256)
    outer = length // inner
    leading = real_part.shape[:-1]
    cos_outer, sin_outer = angle_table(outer, outer, outer, sign)
    cos_twist, sin_twist = angle_table(outer, inner, length, sign)
    cos_inner, sin_inner = angle_table(inner, inner, inner, sign)
    shaped_real = real_part.reshape(leading + (outer, inner))
    step_real = jnp.einsum("kn,...nq->...kq", cos_outer, shaped_real, precision=highest)
    step_imag = jnp.einsum("kn,...nq->...kq", sin_outer, shaped_real, precision=highest)
    if imag_part is not None:
        shaped_imag = imag_part.reshape(leading + (outer, inner))
        step_real = step_real - jnp.einsum(
            "kn,...nq->...kq", sin_outer, shaped_imag, precision=highest
        )
        step_imag = step_imag + jnp.einsum(
            "kn,...nq->...kq", cos_outer, shaped_imag, precision=highest
        )
    twist_real = step_real * cos_twist - step_imag * sin_twist
    twist_imag = step_real * sin_twist + step_imag * cos_twist
    out_real = jnp.matmul(twist_real, cos_inner, precision=highest) - jnp.matmul(
        twist_imag, sin_inner, precision=highest
    )
    result_real = jnp.swapaxes(out_real, -1, -2).reshape(leading + (length,))
    if real_only:
        return (result_real, None)
    out_imag = jnp.matmul(twist_real, sin_inner, precision=highest) + jnp.matmul(
        twist_imag, cos_inner, precision=highest
    )
    result_imag = jnp.swapaxes(out_imag, -1, -2).reshape(leading + (length,))
    return (result_real, result_imag)


def to_spectrum(rows_field):
    slab_count = lax.axis_size("slab")
    z_real, z_imag = transform_last(rows_field, None, -1.0, False)
    stacked = jnp.stack([z_real, z_imag])
    rows_dev = stacked.shape[1]
    length_z = stacked.shape[2]
    moved = jnp.transpose(stacked, (0, 2, 1)).reshape(
        2, slab_count, length_z // slab_count, rows_dev
    )
    block = lax.all_to_all(moved, "slab", split_axis=1, concat_axis=3, tiled=True)
    spec_real, spec_imag = transform_last(block[0, 0], block[1, 0], -1.0, False)
    return jnp.stack([spec_real, spec_imag]).astype(jnp.bfloat16)


def to_rows(spec_real, spec_imag):
    slab_count = lax.axis_size("slab")
    x_real, x_imag = transform_last(spec_real, spec_imag, 1.0, False)
    stacked = jnp.stack([x_real, x_imag], axis=1)
    batch = stacked.shape[0]
    kz_dev = stacked.shape[2]
    length_x = stacked.shape[3]
    moved = stacked.reshape(batch, 2, kz_dev, slab_count, length_x // slab_count)
    scale = 1.0 / (NX * NZ)
    turned = jnp.swapaxes(
        lax.all_to_all(moved, "slab", split_axis=3, concat_axis=2, tiled=True)[:, :, :, 0, :], 2, 3
    )
    field_real, _ = transform_last(turned[:, 0], turned[:, 1], 1.0, True)
    return field_real * scale


def local_general(velocity, kernel, history, impedance, prestress, strength, fault_state):
    side_index = lax.axis_index("side")
    is_first = side_index == 0
    eta_first = impedance[0]
    eta_second = impedance[1]
    eta_total = eta_first + eta_second
    weight_first = eta_second / eta_total
    weight_second = eta_first / eta_total
    eta_joint = eta_first * eta_second / eta_total
    own_eta = jnp.where(is_first, eta_first, eta_second)
    own_sign = jnp.where(is_first, 1.0, -1.0).astype(jnp.float32)
    lag_kernel = kernel[0]
    lag_history = history[0]
    kernel_now = lag_kernel[0].astype(jnp.float32)
    speed = velocity[0]
    state_now = fault_state
    rate = jnp.zeros_like(prestress)
    for _ in range(STEPS):
        spec_now = to_spectrum(speed)
        total = kernel_now * spec_now.astype(jnp.float32) + jnp.einsum(
            "lzx,lczx->czx", lag_kernel[1:], lag_history, preferred_element_type=jnp.float32
        )
        force_now = to_rows(total[0][None], total[1][None])[0]
        force_other = swapped(force_now, "side", 0)
        force_first = jnp.where(is_first, force_now, force_other)
        force_second = jnp.where(is_first, force_other, force_now)
        coupled = weight_first * force_first + weight_second * force_second
        locked = prestress + coupled
        friction_rate = locked / (eta_joint + strength)
        factor = 0.5 * jnp.exp(state_now)
        for _ in range(NEWTON):
            scaled = factor * friction_rate
            misfit = strength * inverse_sinh(scaled) + eta_joint * friction_rate - locked
            slope = strength * factor / jnp.sqrt(1.0 + scaled * scaled) + eta_joint
            friction_rate = friction_rate - 0.5 * misfit / slope
        stress = locked - eta_joint * friction_rate
        speed_new = own_sign * (prestress + force_now - stress) / own_eta
        state_new = state_now + 0.25 * (jnp.exp(-state_now) - jnp.abs(friction_rate))
        speed = speed_new
        rate = friction_rate
        state_now = state_new
        lag_history = jnp.concatenate([spec_now[None], lag_history[:-1]], axis=0)
    return (speed[None], rate, state_now)


RADIX = 16
CHUNKS = 2
LAST_CUT = 80
f32 = jnp.float32
bf16 = jnp.bfloat16


def constant_tables():
    inner = NX // RADIX
    grid = np.outer(np.arange(inner), np.arange(inner)) % inner
    phase = grid * (2.0 * np.pi / inner)
    cos, sin = np.cos(phase), np.sin(phase)
    full = np.concatenate(
        [np.concatenate([cos, sin], 1), np.concatenate([-sin, cos], 1)], 0
    ).astype(np.float32)
    high = full.astype(jnp.bfloat16)
    low = (full - high.astype(np.float32)).astype(jnp.bfloat16)
    table = np.concatenate([high, high, low], 1)
    turn = np.outer(np.arange(RADIX), np.arange(inner)) * (2.0 * np.pi / NX)
    twist = np.stack([np.cos(turn), np.sin(turn)]).astype(np.float32)
    return table, twist


def plus(a, b):
    return tuple(
        (p if q is None else q if p is None else p + q) for p, q in zip(a, b)
    )


def minus(a, b):
    return tuple(
        (p if q is None else -q if p is None else p - q) for p, q in zip(a, b)
    )


def times_i(a, sign):
    real, imag = a
    if sign > 0:
        return (None if imag is None else -imag, real)
    return (imag, None if real is None else -real)


def turned_by(a, cos, sin):
    real, imag = a
    if imag is None:
        return (real * cos, real * sin)
    if real is None:
        return (-(imag * sin), imag * cos)
    return (real * cos - imag * sin, real * sin + imag * cos)


def four(x, sign):
    a, b = plus(x[0], x[2]), minus(x[0], x[2])
    c, d = plus(x[1], x[3]), times_i(minus(x[1], x[3]), sign)
    return [plus(a, c), plus(b, d), minus(a, c), minus(b, d)]


def sixteen(x, sign):
    rows = [four([x[4 * m + n] for m in range(4)], sign) for n in range(4)]
    out = [None] * 16
    for k in range(4):
        terms = []
        for n in range(4):
            power = n * k
            term = rows[n][k]
            if power == 4:
                term = times_i(term, sign)
            elif power:
                angle = 2.0 * math.pi * power / 16
                term = turned_by(term, math.cos(angle), sign * math.sin(angle))
            terms.append(term)
        for m, value in enumerate(four(terms, sign)):
            out[k + 4 * m] = value
    return out


def store_split(held, k, group, lane, first, second):
    inner = NX // RADIX
    rows = pl.ds(pl.multiple_of(group * 16 + (k % 2) * 128, 16), 16)
    for place, value in ((0, first), (1, second)):
        high = value.astype(bf16)
        low = (value - high.astype(f32)).astype(bf16)
        held[k // 2, rows, pl.ds(place * inner + lane, 128)] = high
        held[k // 2, rows, pl.ds((2 + place) * inner + lane, 128)] = low


def twisted(value, twist, k, lane, sign):
    if k == 0:
        real, imag = value
        return (real, jnp.zeros_like(real) if imag is None else imag)
    cos = twist[0, k : k + 1, pl.ds(lane, 128)]
    sin = twist[1, k : k + 1, pl.ds(lane, 128)]
    return turned_by(value, cos, sin if sign > 0 else -sin)


def product(table, held, k, start):
    wide = table.shape[1] // 3
    rows = pl.ds(start, table.shape[0] - start)
    dims = (((1,), (1,)), ((), ()))
    return lax.dot_general(
        table[rows, : 2 * wide], held[k], dims, preferred_element_type=f32
    ) + lax.dot_general(
        table[rows, 2 * wide :], held[k, :, :wide], dims, preferred_element_type=f32
    )


def store_ring(place, spread, both, outs, pair, lead, first_part, row):
    inner = both.shape[0] // 2
    per = inner // RADIX
    spread[...] = both
    for n in range(RADIX):
        target = lax.rem(place[0] + n, RADIX)
        for part in range(2):
            base = (part if first_part == 0 else 1 - part) * inner
            rows = pl.ds(pl.multiple_of(base + target * per + row, 8), 8)
            for odd in range(2):
                outs[n][lead, part, pl.ds(2 * pair + odd, 8, RADIX), :] = spread[
                    rows, odd * 128 : odd * 128 + 128
                ]


def forward_rows(rows_ref, table, twist, place, outs, held, spread):
    rows, length = rows_ref.shape
    inner = length // RADIX

    def group(g, carry):
        at = pl.ds(pl.multiple_of(g * 16, 16), 16)
        for lane in range(0, inner, 128):
            values = [(rows_ref[at, pl.ds(n * inner + lane, 128)], None) for n in range(RADIX)]
            for k, value in enumerate(sixteen(values, -1)):
                store_split(held, k, g, lane, *twisted(value, twist, k, lane, -1))
        return carry

    lax.fori_loop(0, rows // 16, group, 0)

    def wave(pair, carry):
        both = product(table, held, pair, 0)
        if len(outs) >= RADIX:
            for half in range(outs[0].shape[0]):
                store_ring(place, spread, both, outs[:RADIX], pair, half, 0, half * 8)
            if len(outs) == RADIX:
                return carry
        slabs, halves = outs[-1].shape[0], 2
        per = inner // slabs // halves
        for slab in range(slabs):
            for half in range(halves - outs[-1].shape[1], halves):
                out, spot = outs[-1], half - halves + outs[-1].shape[1]
                for part in range(2):
                    first = part * inner + (slab * halves + half) * per
                    for odd in range(2):
                        out[slab, spot, part, pl.ds(2 * pair + odd, per, RADIX), :] = both[
                            first : first + per, odd * 128 : odd * 128 + 128
                        ]
        return carry

    lax.fori_loop(0, RADIX // 2, wave, 0)


def start_kernel(place, velocity, table, twist, *refs):
    forward_rows(velocity.at[0], table, twist, place, refs[:-2], *refs[-2:])


def friction(scalars, own, other, prestress, strength, state):
    weight_own, weight_other, joint, eta, sign = [scalars[n] for n in range(5)]
    locked = prestress + (weight_own * own + weight_other * other)
    rate = locked / (joint + strength)
    factor = 0.5 * jnp.exp(state)
    for _ in range(NEWTON):
        scaled = factor * rate
        wide = 1.0 + scaled * scaled
        narrow = lax.rsqrt(wide)
        bent = jnp.log(jnp.abs(scaled) + wide * narrow)
        bent = jnp.where(scaled < 0.0, -bent, bent)
        misfit = strength * bent + joint * rate - locked
        slope = strength * factor * narrow + joint
        rate = rate - 0.5 * misfit / slope
    stress = locked - joint * rate
    speed = (sign / eta) * (prestress + own - stress)
    state_new = state + 0.25 * (jnp.exp(-state) - jnp.abs(rate))
    return speed, rate, state_new


def middle_kernel(place, scalars, own, other, prestress, strength, state, table, twist, *refs):
    outs = refs[:-4]
    state_out, held, spread, speed_held = refs[-4:]

    def group(g, carry):
        at = pl.ds(pl.multiple_of(g * 8, 8), 8)
        for lane in range(0, own.shape[1], 1024):
            cols = pl.ds(lane, 1024)
            speed, _, state_new = friction(
                scalars,
                own[at, cols],
                other[at, cols],
                prestress[at, cols],
                strength[at, cols],
                state[at, cols],
            )
            speed_held[at, cols] = speed
            state_out[at, cols] = state_new
        return carry

    lax.fori_loop(0, own.shape[0] // 8, group, 0)
    forward_rows(speed_held, table, twist, place, outs, held, spread)


def end_kernel(scalars, own, other, prestress, strength, state, *refs):
    speed_out, rate_out, state_out = refs[-3:]

    def group(g, carry):
        at = pl.ds(pl.multiple_of(g * 8, 8), 8)
        for lane in range(0, own.shape[1], 1024):
            cols = pl.ds(lane, 1024)
            speed, rate, state_new = friction(
                scalars,
                own[at, cols],
                other[at, cols],
                prestress[at, cols],
                strength[at, cols],
                state[at, cols],
            )
            speed_out[0, at, cols] = speed
            rate_out[at, cols] = rate
            state_out[at, cols] = state_new
        return carry

    lax.fori_loop(0, own.shape[0] // 8, group, 0)


def history_kernel(kernel, history, now, later):
    def group(g, carry):
        cols = pl.ds(pl.multiple_of(g * 256, 256), 256)
        lags = [kernel[0, n, :, cols].astype(f32) for n in range(kernel.shape[1])]
        for part in range(2):
            total_now = total_later = 0.0
            for n in range(history.shape[1]):
                past = history[0, n, part, :, cols].astype(f32)
                total_now = total_now + lags[n + 1] * past
                if n + 2 < len(lags):
                    total_later = total_later + lags[n + 2] * past
            now[part, :, cols] = total_now
            later[part, :, cols] = total_later
        return carry

    lax.fori_loop(0, now.shape[2] // 256, group, 0)


def spectral_kernel(counts, has_past, half, pieces, *refs):
    count = 1 + sum(counts)
    place, arrived = refs[0], (refs[1 : 1 + counts[0]], refs[1 + counts[0] : count])
    kernel_now, past_sum, table, twist, twist_ring = refs[count : count + 5]
    rest = list(refs[count + 5 :])
    if has_past:
        kernel_past, spec_past = rest.pop(0), rest.pop(0)
        spec_out = None
    if half > 0:
        rest = rest[len(pieces) - 1 :]
    ring_out, rest = rest[:RADIX], rest[RADIX:]
    pieces = pieces[1:]
    outs, rest = rest[: len(pieces)], rest[len(pieces) :]
    if not has_past:
        spec_out = rest.pop(0)
    held, turned, total, spread, sum_held, lag_held, spec_held, sems = rest
    rows = 128
    own_rows = pl.ds(half * rows, rows)
    copies = [
        pltpu.make_async_copy(past_sum.at[:, own_rows, :], sum_held, sems.at[0]),
        pltpu.make_async_copy(kernel_now.at[0, 0, own_rows, :], lag_held.at[0], sems.at[1]),
    ]
    if has_past:
        copies += [
            pltpu.make_async_copy(kernel_past.at[0, 1, own_rows, :], lag_held.at[1], sems.at[2]),
            pltpu.make_async_copy(spec_past, spec_held, sems.at[3]),
        ]
    for copy in copies:
        copy.start()
    inner = RADIX * 16
    length = total.shape[2]

    def group(g, carry):
        at = pl.ds(pl.multiple_of(g * 16, 16), 16)
        for chunk, tile in enumerate(arrived):
            if len(tile) == 1:
                values = [(tile[0][n, 0, 0, at, :], tile[0][n, 0, 1, at, :]) for n in range(RADIX)]
                sign, turn = -1, twist
            else:
                values = [(tile[n][0, 0, at, :], tile[n][0, 1, at, :]) for n in range(RADIX)]
                sign, turn = 1, twist_ring
            lane = chunk * 128
            for k, value in enumerate(sixteen(values, sign)):
                store_split(held, k, g, lane, *twisted(value, turn, k, lane, -1))
        return carry

    lax.fori_loop(0, rows // 16, group, 0)

    def wave(pair, carry):
        both = product(table, held, pair, 0)
        for odd in range(2):
            for part in range(2):
                turned[part, pl.ds(2 * pair + odd, inner, RADIX), :] = both[
                    part * inner : part * inner + inner, odd * 128 : odd * 128 + 128
                ]
        return carry

    lax.fori_loop(0, RADIX // 2, wave, 0)

    for copy in copies:
        copy.wait()

    def convolve(b, carry):
        cols = pl.ds(pl.multiple_of(b * 256, 256), 256)
        weight = lag_held[0, :, cols].astype(f32)
        for part in range(2):
            spec = turned[part, cols, :].T.astype(bf16)
            value = weight * spec.astype(f32) + sum_held[part, :, cols]
            if has_past:
                value = value + lag_held[1, :, cols].astype(f32) * spec_held[
                    part, :, cols
                ].astype(f32)
            else:
                spec_held[part, :, cols] = spec
            total[part, :, cols] = value
        return carry

    lax.fori_loop(0, length // 256, convolve, 0)
    if not has_past:
        leaving = pltpu.make_async_copy(spec_held, spec_out, sems.at[2])
        leaving.start()

    def group_back(g, carry):
        at = pl.ds(pl.multiple_of(g * 16, 16), 16)
        for lane in range(0, inner, 128):
            values = [
                (total[0, at, pl.ds(n * inner + lane, 128)], total[1, at, pl.ds(n * inner + lane, 128)])
                for n in range(RADIX)
            ]
            for k, value in enumerate(sixteen(values, 1)):
                real, imag = twisted(value, twist, k, lane, 1)
                store_split(held, k, g, lane, imag, real)
        return carry

    lax.fori_loop(0, rows // 16, group_back, 0)

    def wave_back(pair, carry):
        both = product(table, held, pair, 0)
        store_ring(place, spread, both, ring_out, pair, 0, 1, 0)
        slabs = outs[0].shape[0]
        per = inner // slabs
        for slab in range(slabs):
            for out, (row, count) in zip(outs, pieces):
                count = count // RADIX
                for part in range(2):
                    first = (1 - part) * inner + slab * per + row // RADIX
                    for odd in range(2):
                        out[slab, 0, part, pl.ds(2 * pair + odd, count, RADIX), :] = both[
                            first : first + count, odd * 128 : odd * 128 + 128
                        ]
        return carry

    lax.fori_loop(0, RADIX // 2, wave_back, 0)
    if not has_past:
        leaving.wait()


def inverse_kernel(count, *refs):
    blocks = refs[:count]
    ring = blocks if count > 1 else None
    table, twist, twist_ring, out, held, turned = refs[count:]
    rows, length = out.shape
    inner = length // RADIX

    def group(g, carry):
        at = pl.ds(pl.multiple_of(g * 16, 16), 16)
        for half in range(inner // 128):
            sign, turn = 1, twist
            if ring is not None:
                tile = ring[half * RADIX : half * RADIX + RADIX]
                values = [(tile[n][0, 0, at, :], tile[n][0, 1, at, :]) for n in range(RADIX)]
                sign, turn = -1, twist_ring
            else:
                block = blocks[0]
                values = [(block[n, half, 0, at, :], block[n, half, 1, at, :]) for n in range(RADIX)]
            for k, value in enumerate(sixteen(values, sign)):
                real, imag = twisted(value, turn, k, half * 128, 1)
                store_split(held, k, g, half * 128, imag, real)
        return carry

    lax.fori_loop(0, rows // 16, group, 0)

    def wave(pair, carry):
        both = product(table, held, pair, inner)
        for odd in range(2):
            turned[pl.ds(2 * pair + odd, inner, RADIX), :] = both[:, odd * 128 : odd * 128 + 128]
        return carry

    lax.fori_loop(0, RADIX // 2, wave, 0)
    scale = 1.0 / (NX * NZ)

    def turn(b, carry):
        cols = pl.ds(pl.multiple_of(b * 256, 256), 256)
        out[:, cols] = turned[cols, :].T[:rows] * scale
        return carry

    lax.fori_loop(0, length // 256, turn, 0)


def whole_spec(array):
    zeros = (0,) * array.ndim
    return pl.BlockSpec(array.shape, lambda *_: zeros)


PARAMS = pltpu.CompilerParams(vmem_limit_bytes=67043328)
SCALARS = pl.BlockSpec(memory_space=pltpu.SMEM)


def is_light(distance, count):
    return min(distance, count - distance) * 3 <= count


def ringed(blocks, which=(False, True)):
    count = lax.axis_size("slab")
    moved = list(blocks)
    for n in range(1, count):
        if is_light(n, count) not in which:
            continue
        pairs = [(source, (source + n) % count) for source in range(count)]
        moved[n] = lax.ppermute(blocks[n], "slab", pairs)
    return moved


def after_first(arrived, then):
    count = len(arrived)
    first = [n for n in range(1, count) if not is_light(n, count)]
    held = lax.optimization_barrier((tuple(arrived[n] for n in first), *then))
    arrived = list(arrived)
    for n, value in zip(first, held[0]):
        arrived[n] = value
    return (arrived, *held[1:])


def tick_kernel(before, after):
    for n in range(before.shape[0]):
        after[n] = before[n]


def ticked(scalars):
    return pl.pallas_call(
        tick_kernel,
        out_shape=jax.ShapeDtypeStruct(scalars.shape, scalars.dtype),
        in_specs=[SCALARS],
        out_specs=SCALARS,
    )(scalars)


def exchanged(value):
    return lax.all_to_all(value, "slab", split_axis=0, concat_axis=0, tiled=True)


def local(velocity, kernel, history, impedance, prestress, strength, fault_state):
    slabs = lax.axis_size("slab")
    rows_dev, length = prestress.shape
    inner = length // RADIX
    chunk_rows = rows_dev // CHUNKS
    halves = rows_dev // 128
    if slabs != RADIX or rows_dev != inner or chunk_rows != 128:
        return local_general(
            velocity, kernel, history, impedance, prestress, strength, fault_state
        )
    lags = history.shape[1]
    table_np, twist_np = constant_tables()
    table, twist = jnp.asarray(table_np), jnp.asarray(twist_np)
    is_first = lax.axis_index("side") == 0
    eta_first, eta_second = impedance[0], impedance[1]
    eta_total = eta_first + eta_second
    weight_first, weight_second = eta_second / eta_total, eta_first / eta_total
    scalars = jnp.stack(
        [
            jnp.where(is_first, weight_first, weight_second),
            jnp.where(is_first, weight_second, weight_first),
            eta_first * eta_second / eta_total,
            jnp.where(is_first, eta_first, eta_second),
            jnp.where(is_first, 1.0, -1.0).astype(f32),
        ]
    )

    def tiles(counts, rows=128):
        return [jax.ShapeDtypeStruct((slabs, count, 2, rows, 128), f32) for count in counts]

    def ring_tiles(count):
        return [jax.ShapeDtypeStruct((count, 2, 128, 128), f32)] * slabs

    def forward_shapes(chunk, ring):
        shapes = ring_tiles(1) + tiles([1])
        if chunk == 0:
            shapes = ring_tiles(halves) if ring else tiles([halves])
        return shapes, [whole_spec(shape) for shape in shapes]

    me = lax.axis_index("slab")
    place = jnp.reshape(me, (1,)).astype(jnp.int32)
    spread = pltpu.VMEM((2 * inner, 2 * 128), f32)
    held = pltpu.VMEM((RADIX // 2, 256, 4 * inner), bf16)
    rows_shape = jax.ShapeDtypeStruct((chunk_rows, length), f32)
    rows_spec = pl.BlockSpec((chunk_rows, length), lambda *_: (0, 0))

    def chunk_spec(chunk):
        return pl.BlockSpec((chunk_rows, length), lambda *_: (chunk, 0))

    def start(chunk):
        shapes, specs = forward_shapes(chunk, chunk == 0)
        return pl.pallas_call(
            start_kernel,
            out_shape=shapes,
            grid=(1,),
            in_specs=[
                SCALARS,
                pl.BlockSpec((1, chunk_rows, length), lambda *_: (0, chunk, 0)),
                whole_spec(table),
                whole_spec(twist),
            ],
            out_specs=specs,
            scratch_shapes=[held, spread],
            compiler_params=PARAMS,
        )(place, velocity, table, twist)

    def middle(scalars, chunk, own, other, state):
        shapes, specs = forward_shapes(chunk, False)
        *sent, state_new = pl.pallas_call(
            middle_kernel,
            out_shape=shapes + [rows_shape],
            grid=(1,),
            in_specs=[
                SCALARS,
                SCALARS,
                rows_spec,
                rows_spec,
                chunk_spec(chunk),
                chunk_spec(chunk),
                chunk_spec(chunk),
                whole_spec(table),
                whole_spec(twist),
            ],
            out_specs=specs + [rows_spec],
            scratch_shapes=[held, spread, pltpu.VMEM((chunk_rows, length), f32)],
            compiler_params=PARAMS,
        )(place, scalars, own, other, prestress, strength, state, table, twist)
        return sent, state_new

    def end(scalars, row, own, other, state, before):
        full = jax.ShapeDtypeStruct((rows_dev, length), f32)
        step = 16
        parts = own.shape[0] // step
        base = row // step
        ahead = row % chunk_rows // step
        moving = pl.BlockSpec((step, length), lambda g: (base + g, 0))
        near = pl.BlockSpec((step, length), lambda g: (g, 0))
        held_state = pl.BlockSpec((step, length), lambda g: (ahead + g, 0))
        moving_speed = pl.BlockSpec((1, step, length), lambda g: (0, base + g, 0))
        kept = [pl.BlockSpec(memory_space=pl.ANY)] * len(before)
        return pl.pallas_call(
            end_kernel,
            out_shape=(jax.ShapeDtypeStruct((1, rows_dev, length), f32), full, full),
            grid=(parts,),
            in_specs=[SCALARS, near, near, moving, moving, held_state] + kept,
            out_specs=(moving_speed, moving, moving),
            input_output_aliases={6 + n: n for n in range(len(before))},
            compiler_params=PARAMS,
        )(scalars, own, other, prestress, strength, state, *before)

    def past_sums():
        step = 32
        total = jax.ShapeDtypeStruct((2, rows_dev, length), f32)
        spec = pl.BlockSpec((2, step, length), lambda g: (0, g, 0))
        return pl.pallas_call(
            history_kernel,
            out_shape=(total, total),
            grid=(rows_dev // step,),
            in_specs=[
                pl.BlockSpec((1, lags + 1, step, length), lambda g: (0, 0, g, 0)),
                pl.BlockSpec((1, lags, 2, step, length), lambda g: (0, 0, 0, g, 0)),
            ],
            out_specs=(spec, spec),
            compiler_params=PARAMS,
        )(kernel, history)

    def spectral(half, ring, near, past_sum, past, pieces, before):
        def block(array):
            place = half if array.shape[1] == halves else 0
            shape = (slabs, 1, 2, array.shape[3], 128)
            return pl.BlockSpec(shape, lambda *_: (0, place, 0, 0, 0))

        anywhere = pl.BlockSpec(memory_space=pl.ANY)

        def arrived(tile):
            if len(tile) == 1:
                return [block(tile[0])]
            spot = half if tile[0].shape[0] == halves else 0
            return [pl.BlockSpec((1, 2, 128, 128), lambda *_: (spot, 0, 0, 0))] * slabs

        operands = [place, *ring, *near, kernel, past_sum, table, twist, twist_ring]
        in_specs = [SCALARS] + arrived(ring) + arrived(near) + [anywhere, anywhere]
        in_specs += [whole_spec(table), whole_spec(twist), whole_spec(twist_ring)]
        out_shape = []
        for row, count in pieces[1:]:
            out_shape += tiles([halves], count)
        out_specs = [block(shape) for shape in out_shape]
        shapes = ring_tiles(1)
        out_shape = shapes + out_shape
        out_specs = [whole_spec(shape) for shape in shapes] + out_specs
        if past is not None:
            operands += [kernel, past]
            in_specs += [anywhere, anywhere]
        else:
            out_shape.append(jax.ShapeDtypeStruct((2, 128, length), bf16))
            out_specs.append(anywhere)
        aliases = {}
        if before is not None:
            aliases = {len(operands) + n: slabs + n for n in range(len(before))}
            operands += before
            in_specs += [pl.BlockSpec(memory_space=pl.ANY)] * len(before)
        return pl.pallas_call(
            functools.partial(
                spectral_kernel, (len(ring), len(near)), past is not None, half, pieces
            ),
            input_output_aliases=aliases,
            out_shape=out_shape,
            grid=(1,),
            in_specs=in_specs,
            out_specs=out_specs,
            scratch_shapes=[
                held,
                pltpu.VMEM((2, length, 128), f32),
                pltpu.VMEM((2, 128, length), f32),
                spread,
                pltpu.VMEM((2, 128, length), f32),
                pltpu.VMEM((2, 128, length), bf16),
                pltpu.VMEM((2, 128, length), bf16),
                pltpu.SemaphoreType.DMA((4,)),
            ],
            compiler_params=PARAMS,
        )(*operands)

    def inverse(*blocks):
        rows = blocks[0].shape[-2]
        return pl.pallas_call(
            functools.partial(inverse_kernel, len(blocks)),
            out_shape=jax.ShapeDtypeStruct((rows, length), f32),
            grid=(1,),
            in_specs=[whole_spec(b) for b in (*blocks, table, twist, twist_ring)],
            out_specs=pl.BlockSpec((rows, length), lambda *_: (0, 0)),
            scratch_shapes=[held, pltpu.VMEM((length, 128), f32)],
            compiler_params=PARAMS,
        )(*blocks, table, twist, twist_ring)

    hold = lax.optimization_barrier
    states = [fault_state] * CHUNKS
    past = [None] * halves
    sums, waiting = None, None
    whole, cut = chunk_rows, LAST_CUT
    sent = [start(0), None]
    for step_index in range(STEPS):
        last = step_index == STEPS - 1
        pieces = [(0, whole), (whole, cut), (whole + cut, whole - cut)]
        if not last:
            pieces = [(0, whole), (whole, whole)]
        ring = ringed(sent[0]) if step_index == 0 else [exchanged(sent[0][0])]
        if step_index == 0:
            sent[1] = start(1)
            sent[1], shift = hold((tuple(sent[1]), me))
            turn = lax.broadcasted_iota(jnp.int32, (RADIX, inner), 0) * (
                lax.broadcasted_iota(jnp.int32, (RADIX, inner), 1) + inner * shift
            )
            turn = (turn % length).astype(f32) * (2.0 * math.pi / length)
            twist_ring = jnp.stack([jnp.cos(turn), jnp.sin(turn)])
        else:
            own = inverse(waiting)
            sent[1], states[1] = middle(scalars, 1, own, swapped(own, "side", 0), states[1])
        near = ringed(sent[1][:slabs])
        if step_index == 0:
            sums = past_sums()
        scalars = ticked(scalars)
        near, far, sums = after_first(near, (sent[1][slabs], sums))
        far = exchanged(far)
        outs = spectral(0, ring, near, sums[step_index], past[0], pieces, None)
        if step_index == 0:
            past[0] = outs[-1]
        late = outs[slabs : slabs + len(pieces) - 1]
        back = ringed(outs[:slabs], (True,))
        long = [n for n in range(1, slabs) if not is_light(n, slabs)]
        far, late, rest = hold((far, list(late), [back[n] for n in long]))
        for n, value in zip(long, rest):
            back[n] = value
        back = ringed(back, (False,))
        outs = spectral(1, ring, [far], sums[step_index], past[1], pieces, late)
        if step_index == 0:
            past[1] = outs[-1]
        late = outs[slabs : slabs + len(pieces) - 1]
        more = ringed(outs[:slabs])
        scalars = ticked(scalars)
        more, late = after_first(more, (list(late),))
        waiting = exchanged(late[0])
        own = inverse(*back, *more)
        other = swapped(own, "side", 0)
        if last:
            scalars = ticked(scalars)
        else:
            sent[0], states[0] = middle(scalars, 0, own, other, states[0])
        if not last:
            waiting, sent[0], states[0] = hold((waiting, sent[0], states[0]))
            continue
        waiting, scalars, final = hold((waiting, scalars, late[1]))
        final = exchanged(final)
        own_near = inverse(waiting)
        other_near = swapped(own_near, "side", 0)
        results = end(scalars, 0, own, other, states[0], ())
        final, own_near, results = hold((final, own_near, tuple(results)))
        own = inverse(final)
        other = swapped(own, "side", 0)
        results = end(scalars, whole, own_near, other_near, states[1], results)
        results = end(scalars, whole + cut, own, other, states[1], results)
    return tuple(results)


def solution(mesh):
    placed = (
        P("side", "slab", None),
        P("side", None, "slab", None),
        P("side", None, None, "slab", None),
        P(),
        P("slab", None),
        P("slab", None),
        P("slab", None),
    )
    return jax.shard_map(
        local,
        mesh=mesh,
        in_specs=placed,
        out_specs=(P("side", "slab", None), P("slab", None), P("slab", None)),
        check_vma=False,
    )
```
